32 devices in a mesh: seq: 2 (over x), ctx: 8 (over z, y), fsdp: 2 (over core).
Axes of the slice: x: 2, y: 2, z: 4, core: 2. Of those that a mesh axis runs over, the one named last changes fastest.
Arguments:
- hidden: bfloat16 [4, 1280, 768], P(('seq', 'fsdp'), 'ctx'), may hold values from -6 to 6
- segment_ids: int32 [4, 1280], P(('seq', 'fsdp')), may hold values from 0 to 15, never falling along the last dimension, each value on 1 to 960 neighbouring positions
- out_grad: bfloat16 [4, 1280, 768], P(('seq', 'fsdp'), 'ctx'), may hold values from -6 to 6
- w_qkv: bfloat16 [768, 2304], P('fsdp'), may hold values from -0.21875 to 0.21875
- bias_query: bfloat16 [768], P('fsdp'), may hold values from -3 to 3
- bias_value: bfloat16 [768], P('fsdp'), may hold values from -3 to 3
- w_out: bfloat16 [768, 768], P('fsdp'), may hold values from -0.625 to 0.625
- bias_out: bfloat16 [768], P('fsdp'), may hold values from -2 to 2
- gain_one: bfloat16 [768], P('fsdp'), may hold values from 0.25 to 1.75
- shift_one: bfloat16 [768], P('fsdp'), may hold values from -2 to 2
- w_up: bfloat16 [768, 3072], P('fsdp'), may hold values from -0.21875 to 0.21875
- bias_up: bfloat16 [3072], P('fsdp'), may hold values from -3 to 3
- w_down: bfloat16 [3072, 768], P('fsdp'), may hold values from -0.109375 to 0.109375
- bias_down: bfloat16 [768], P('fsdp'), may hold values from -2 to 2
- gain_two: bfloat16 [768], P('fsdp'), may hold values from 0.25 to 1.75
- shift_two: bfloat16 [768], P('fsdp'), may hold values from -2 to 2
Outputs:
- output: bfloat16 [4, 1280, 768], P(('seq', 'fsdp'), 'ctx')
- grad_hidden: float32 [4, 1280, 768], P(('seq', 'fsdp'), 'ctx')
- grad_w_qkv: float32 [768, 2304], P(('ctx', 'fsdp'))
- grad_bias_query: float32 [768], P(('ctx', 'fsdp'))
- grad_bias_value: float32 [768], P(('ctx', 'fsdp'))
- grad_w_out: float32 [768, 768], P(('ctx', 'fsdp'))
- grad_bias_out: float32 [768], P(('ctx', 'fsdp'))
- grad_gain_one: float32 [768], P(('ctx', 'fsdp'))
- grad_shift_one: float32 [768], P(('ctx', 'fsdp'))
- grad_w_up: float32 [768, 3072], P(('ctx', 'fsdp'))
- grad_bias_up: float32 [3072], P(('ctx', 'fsdp'))
- grad_w_down: float32 [3072, 768], P(('ctx', 'fsdp'))
- grad_bias_down: float32 [768], P(('ctx', 'fsdp'))
- grad_gain_two: float32 [768], P(('ctx', 'fsdp'))
- grad_shift_two: float32 [768], P(('ctx', 'fsdp'))
The draws below stay inside these ranges and needn't reach their ends.
Inputs may be any that keep to these rules, and one draw needn't show every extreme that they name: `segment_ids`: each row numbers its 16 documents 0 to 15 in order, never falling, each document a run of consecutive tokens; the longest has exactly 960 tokens.
All inputs are finite; a program needn't handle non-finite values.
Results may differ from the reference program's by a relative error of at most 0.015.
Values may be sent and summed in bfloat16 or wider, within the bound.
A program may use at most 256 MiB of HBM per device.

```python
import math
import jax
import jax.numpy as jnp
import numpy as np
from jax import lax

D = 768
HEADS = 12
HEAD = 64
FF = 3072
TOK_DEV = 160
SEQ_LEN = 1280
SEQS = 4
DOCS = 16
LONGEST = 960


def spiked(values, key, source, target, shards_of, factor):
    def block_of(axis_at):
        return (jnp.arange(values.shape[axis_at]) // (values.shape[axis_at] // shards_of)).reshape((-1,) + (1,) * (values.ndim - 1 - axis_at))

    first = jax.random.permutation(key, shards_of)[block_of(target)]
    other_side = (block_of(target) + shards_of // 2) % shards_of
    return jnp.where((block_of(source) == first) | (block_of(source) == other_side), factor * values, values)


def shard_levels(rng, extent, shards, least, largest):
    loudness = 1.0
    for axis_at, parts in shards:
        heights = jax.random.uniform(jax.random.fold_in(jax.random.fold_in(rng, 6), axis_at), (parts,), jnp.float32, least / len(shards), largest / len(shards))
        loudness = loudness * jnp.repeat(jnp.exp(heights), extent[axis_at] // parts).reshape((-1,) + (1,) * (len(extent) - 1 - axis_at))
    return loudness


def profile(count, total, bound, slope):
    portions = [(1 << 20) // math.isqrt(rank ** slope) + 1 for rank in range(2, count + 1)]
    surplus, given = total - bound - (count - 1), [1] * (count - 1)
    while surplus > 0:
        candidates = [i for i in range(count - 1) if given[i] < bound]
        whole, left = sum([portions[i] for i in candidates]), surplus
        for i in candidates:
            extra = min(bound - given[i], max(1, left * portions[i] // whole), surplus)
            given[i] = given[i] + extra
            surplus = surplus - extra
    return np.array([bound] + given)


def ragged(stream_key, amount, total, most, skew):
    if amount == 2:
        one = jax.random.randint(stream_key, (), max(1, total - most), min(most, total - 1) + 1)
        return jnp.stack([one, total - one])
    tallies = jnp.asarray(profile(amount, total, most, skew), jnp.int32)
    couples = (amount - 1) // 2
    donor, receiver = tallies[1:1 + 2 * couples:2], tallies[2:2 + 2 * couples:2]
    slack = jnp.minimum(donor - 1, most - receiver)
    passed = jax.random.randint(jax.random.fold_in(stream_key, 1), (couples,), 0, 1 << 20) % (slack + 1)
    tallies = tallies.at[1:1 + 2 * couples:2].set(donor - passed).at[2:2 + 2 * couples:2].set(receiver + passed)
    return tallies[jax.random.permutation(jax.random.fold_in(stream_key, 2), amount)]


def normal_values(stream_key, shape, width, bound, shards=(), held_as=jnp.bfloat16):
    result = width * jax.random.normal(stream_key, shape, jnp.float32)
    if shards:
        result = result * shard_levels(stream_key, shape, shards, -0.22, 0.18)
    return jnp.clip(result, -bound, bound).astype(held_as)


def gaussian_with(stream_key, extent, scale, limit, cuts, heavy, held_as=jnp.bfloat16):
    result = scale * jax.random.normal(stream_key, extent, jnp.float32)
    if cuts:
        result = result * shard_levels(stream_key, extent, cuts, -0.22, 0.18)
    return jnp.clip(spiked(result, jax.random.fold_in(stream_key, 3), *heavy), -limit, limit).astype(held_as)


def setup_inputs(seed: int = 0) -> dict:
    streams_of = jax.random.split(jax.random.key(seed), 17)
    hidden = normal_values(streams_of[0], (SEQS, SEQ_LEN, D), 1.0, 6.0, ((0, 4), (1, 8)))
    segment_ids = jax.vmap(lambda own: jnp.searchsorted(jnp.cumsum(ragged(own, DOCS, SEQ_LEN, LONGEST, 2)), jnp.arange(SEQ_LEN), side="right"))(jax.random.split(streams_of[1], SEQS)).reshape((SEQS, SEQ_LEN)).astype(jnp.int32)
    out_grad = gaussian_with(streams_of[2], (SEQS, SEQ_LEN, D), 1.0, 6.0, ((0, 4), (1, 8)), (1, 2, 8, 2.0))
    w_qkv = normal_values(streams_of[3], (D, 3 * D), D ** -0.5, 0.21875, ((0, 2),))
    bias_query = normal_values(streams_of[4], (D,), 0.5, 3.0, ((0, 2),))
    bias_value = normal_values(streams_of[5], (D,), 0.5, 3.0, ((0, 2),))
    w_out = normal_values(streams_of[6], (D, D), (D // 8) ** -0.5, 0.625, ((0, 2),))
    bias_out = normal_values(streams_of[7], (D,), 0.3, 2.0, ((0, 2),))
    gain_one = jnp.clip(1.0 + 0.15 * jax.random.normal(streams_of[8], (D,), jnp.float32), 0.25, 1.75).astype(jnp.bfloat16)
    shift_one = normal_values(streams_of[9], (D,), 0.3, 2.0, ((0, 2),))
    w_up = normal_values(streams_of[10], (D, FF), D ** -0.5, 0.21875, ((0, 2),))
    bias_up = normal_values(streams_of[11], (FF,), 0.5, 3.0, ((0, 2),))
    w_down = normal_values(streams_of[12], (FF, D), FF ** -0.5, 0.109375, ((0, 2),))
    bias_down = normal_values(streams_of[13], (D,), 0.3, 2.0, ((0, 2),))
    gain_two = jnp.clip(1.0 + 0.15 * jax.random.normal(streams_of[14], (D,), jnp.float32), 0.25, 1.75).astype(jnp.bfloat16)
    shift_two = normal_values(streams_of[15], (D,), 0.3, 2.0, ((0, 2),))
    return {"hidden": hidden, "segment_ids": segment_ids, "out_grad": out_grad, "w_qkv": w_qkv, "bias_query": bias_query, "bias_value": bias_value, "w_out": w_out, "bias_out": bias_out, "gain_one": gain_one, "shift_one": shift_one, "w_up": w_up, "bias_up": bias_up, "w_down": w_down, "bias_down": bias_down, "gain_two": gain_two, "shift_two": shift_two}


@jax.custom_vjp
def low(v):
    return lax.optimization_barrier(v.astype(jnp.bfloat16)).astype(jnp.float32)

@jax.custom_vjp
def low_back(v):
    return v

def low_keep(v):
    return (low(v), None)

def low_pass(kept, grad):
    return (grad,)

def back_keep(v):
    return (v, None)

def back_low(kept, grad):
    return (low(grad),)
low.defvjp(low_keep, low_pass)
low_back.defvjp(back_keep, back_low)
EPSILON = 1e-12
NEGATIVE = -1e+30
LOG_TWO = 0.6931471805599453
LOG2_E = 1.4426950408889634
HIGHEST = lax.Precision.HIGHEST

def layer_norm(rows_in, gain_vec, shift_vec):
    row_mean = lax.optimization_barrier(jnp.mean(rows_in, axis=-1, keepdims=True))
    centered = rows_in - row_mean
    variance = lax.optimization_barrier(jnp.mean(centered * centered, axis=-1, keepdims=True))
    return centered * lax.rsqrt(variance + EPSILON) * gain_vec + shift_vec

def encoder_layer(tokens, doc_ids, params):
    w_qkv, bias_query, bias_value, w_out, bias_out, gain_one, shift_one, w_up, bias_up, w_down, bias_down, gain_two, shift_two = params
    mixed_rows = jnp.dot(tokens, w_qkv, precision=HIGHEST)
    query_rows = low(low_back(mixed_rows[:, :D] + bias_query))
    key_rows = low(low_back(mixed_rows[:, D:2 * D]))
    value_rows = low(low_back(mixed_rows[:, 2 * D:] + bias_value))
    key_heads = key_rows.reshape(SEQ_LEN, HEADS, HEAD)
    value_heads = value_rows.reshape(SEQ_LEN, HEADS, HEAD)
    block_rows = 2 * TOK_DEV
    query_blocks = query_rows.reshape(SEQ_LEN // block_rows, block_rows, HEADS, HEAD)
    id_blocks = doc_ids.reshape(SEQ_LEN // block_rows, block_rows)

    def attend(inputs):
        query_block, block_ids = inputs
        raw_scores = jnp.einsum('qhd,khd->hqk', query_block, key_heads, precision=HIGHEST) * 0.125
        scores = low_back(raw_scores)
        allowed = (block_ids[:, None] == doc_ids[None, :])[None]
        scores = jnp.where(allowed, scores, NEGATIVE)
        row_high = lax.optimization_barrier(jnp.max(scores, axis=-1, keepdims=True))
        shift = LOG_TWO * jnp.ceil(row_high * LOG2_E)
        unnorm = jnp.where(allowed, jnp.exp(scores - shift), 0.0)
        totals = lax.optimization_barrier(jnp.sum(unnorm, axis=-1))
        product = low_back(jnp.einsum('hqk,khd->qhd', low(unnorm), value_heads, precision=HIGHEST))
        return product / jnp.transpose(totals)[:, :, None]
    attended = lax.map(jax.checkpoint(attend), (query_blocks, id_blocks)).reshape(SEQ_LEN, D)
    attended = low(low_back(attended))
    branch = low_back(jnp.dot(attended, w_out, precision=HIGHEST) + bias_out)
    normed_one = layer_norm(tokens + branch, gain_one, shift_one)
    up_rows = low_back(jnp.dot(low(normed_one), w_up, precision=HIGHEST) + bias_up)
    active = low(jax.nn.gelu(up_rows, approximate=False))
    ffn_out = low_back(jnp.dot(active, w_down, precision=HIGHEST) + bias_down)
    return layer_norm(normed_one + ffn_out, gain_two, shift_two)

def reference(hidden, segment_ids, out_grad, w_qkv, bias_query, bias_value, w_out, bias_out, gain_one, shift_one, w_up, bias_up, w_down, bias_down, gain_two, shift_two):
    params = jax.tree.map(lambda member: member.astype(jnp.float32), (w_qkv, bias_query, bias_value, w_out, bias_out, gain_one, shift_one, w_up, bias_up, w_down, bias_down, gain_two, shift_two))

    def forward(tokens_all, params_all):

        def one_sequence(carried, inputs):
            tokens, doc_ids = inputs
            return (carried, encoder_layer(tokens, doc_ids, params_all))
        return lax.scan(one_sequence, jnp.float32(0.0), (tokens_all, segment_ids))[1]
    output, pullback = jax.vjp(forward, hidden.astype(jnp.float32), params)
    grad_hidden, grads = pullback(out_grad.astype(jnp.float32))
    return (output.astype(jnp.bfloat16), grad_hidden, grads[0], grads[1], grads[2], grads[3], grads[4], grads[5], grads[6], grads[7], grads[8], grads[9], grads[10], grads[11], grads[12])
```

```python
import functools

import jax
import jax.numpy as jnp
from jax import lax
from jax.experimental import pallas as pl
from jax.experimental.pallas import tpu as pltpu
from jax.sharding import PartitionSpec as P

HEAD = 64


EPSILON = 1e-12
NEGATIVE = -1e30
LOG_TWO = 0.6931471805599453
LOG2_E = 1.4426950408889634


def norm_forward(rows_in, gain_vec, shift_vec):
    row_mean = jnp.mean(rows_in, axis=-1, keepdims=True)
    centered = rows_in - row_mean
    variance = jnp.mean(centered * centered, axis=-1, keepdims=True)
    scaled = lax.rsqrt(variance + EPSILON)
    normed = centered * scaled
    return (normed * gain_vec + shift_vec, normed, scaled)


def norm_backward(grad_rows, normed, scaled, gain_vec):
    grad_normed = grad_rows * gain_vec
    inner_part = (
        grad_normed
        - jnp.mean(grad_normed, axis=-1, keepdims=True)
        - normed * jnp.mean(grad_normed * normed, axis=-1, keepdims=True)
    )
    return (inner_part * scaled, jnp.sum(grad_rows * normed, axis=0), jnp.sum(grad_rows, axis=0))


def head_scores(query_heads, key_heads):
    return (
        jnp.einsum("qhd,khd->hqk", query_heads, key_heads, preferred_element_type=jnp.float32)
        * 0.125
    )


def column_sums(rows_b):
    return jnp.sum(rows_b.astype(jnp.float32), axis=0)


def sweep(steps_total, advance, start_carry):

    def advance_one(running, block_index):
        running = advance(running, block_index)
        return (running, None)

    return lax.scan(advance_one, start_carry, jnp.arange(steps_total))[0]


def local_grads(scores, allowed, shift_rows, ratio_rows, grad_heads, value_heads):
    unnorm = jnp.where(allowed, jnp.exp(scores - shift_rows[..., None]), 0.0)
    grad_weights = jnp.einsum(
        "qhd,khd->hqk", grad_heads, value_heads, preferred_element_type=jnp.float32
    )
    grad_scores = (unnorm * (grad_weights - ratio_rows[..., None])).astype(jnp.bfloat16)
    return (unnorm.astype(jnp.bfloat16), grad_scores)


def on_device(
    hidden,
    segment_ids,
    out_grad,
    w_qkv,
    bias_query,
    bias_value,
    w_out,
    bias_out,
    gain_one,
    shift_one,
    w_up,
    bias_up,
    w_down,
    bias_down,
    gain_two,
    shift_two,
):
    (
        w_qkv,
        bias_query,
        bias_value,
        w_out,
        bias_out,
        gain_one,
        shift_one,
        w_up,
        bias_up,
        w_down,
        bias_down,
        gain_two,
        shift_two,
    ) = (
        lax.all_gather(w_qkv, "fsdp", axis=0, tiled=True),
        lax.all_gather(bias_query, "fsdp", axis=0, tiled=True),
        lax.all_gather(bias_value, "fsdp", axis=0, tiled=True),
        lax.all_gather(w_out, "fsdp", axis=0, tiled=True),
        lax.all_gather(bias_out, "fsdp", axis=0, tiled=True),
        lax.all_gather(gain_one, "fsdp", axis=0, tiled=True),
        lax.all_gather(shift_one, "fsdp", axis=0, tiled=True),
        lax.all_gather(w_up, "fsdp", axis=0, tiled=True),
        lax.all_gather(bias_up, "fsdp", axis=0, tiled=True),
        lax.all_gather(w_down, "fsdp", axis=0, tiled=True),
        lax.all_gather(bias_down, "fsdp", axis=0, tiled=True),
        lax.all_gather(gain_two, "fsdp", axis=0, tiled=True),
        lax.all_gather(shift_two, "fsdp", axis=0, tiled=True),
    )
    f32 = jnp.float32
    bf16 = jnp.bfloat16
    tokens = hidden[0]
    tok_rows = tokens.shape[0]
    model_width = tokens.shape[1]
    head_count = model_width // HEAD
    seq_rows = tok_rows * lax.axis_size("ctx")
    key_span = 4 * tok_rows
    block_total = seq_rows // key_span
    doc_ids = segment_ids[0]
    own_ids = lax.dynamic_slice_in_dim(doc_ids, lax.axis_index("ctx") * tok_rows, tok_rows)
    mixed_rows = jnp.dot(tokens, w_qkv, preferred_element_type=f32)
    query_rows = (mixed_rows[:, :model_width] + bias_query.astype(f32)).astype(bf16)
    key_value = jnp.concatenate(
        [
            mixed_rows[:, model_width : 2 * model_width],
            mixed_rows[:, 2 * model_width :] + bias_value.astype(f32),
        ],
        axis=1,
    ).astype(bf16)
    all_kv = lax.all_gather(key_value, "ctx", axis=0, tiled=True)
    query_heads = query_rows.reshape(tok_rows, head_count, HEAD)

    def key_block(block_index):
        kv_piece = lax.dynamic_slice_in_dim(all_kv, block_index * key_span, key_span, 0)
        key_ids = lax.dynamic_slice_in_dim(doc_ids, block_index * key_span, key_span)
        return (
            kv_piece[:, :model_width].reshape(key_span, head_count, HEAD),
            kv_piece[:, model_width:].reshape(key_span, head_count, HEAD),
            key_ids,
        )

    def forward_step(running, block_index):
        level_run, total_run, sum_run = running
        key_heads, value_heads, key_ids = key_block(block_index)
        allowed = (own_ids[:, None] == key_ids[None, :])[None]
        scores = jnp.where(allowed, head_scores(query_heads, key_heads), NEGATIVE)
        level_new = jnp.maximum(level_run, jnp.ceil(jnp.max(scores, axis=-1) * LOG2_E))
        rescale = jnp.exp(LOG_TWO * (level_run - level_new))
        unnorm = jnp.where(allowed, jnp.exp(scores - (LOG_TWO * level_new)[..., None]), 0.0)
        total_new = total_run * rescale + jnp.sum(unnorm, axis=-1)
        sum_new = sum_run * jnp.transpose(rescale)[:, :, None] + jnp.einsum(
            "hqk,khd->qhd", unnorm.astype(bf16), value_heads, preferred_element_type=f32
        )
        return (level_new, total_new, sum_new)

    start_state = (
        jnp.full((head_count, tok_rows), NEGATIVE, f32),
        jnp.zeros((head_count, tok_rows), f32),
        jnp.zeros((tok_rows, head_count, HEAD), f32),
    )
    level_end, row_total, raw_sum = sweep(block_total, forward_step, start_state)
    row_shift = LOG_TWO * level_end
    att_sum = raw_sum / jnp.transpose(row_total)[:, :, None]
    attended = att_sum.reshape(tok_rows, model_width).astype(bf16)
    branch = jnp.dot(attended, w_out, preferred_element_type=f32) + bias_out.astype(f32)
    normed_one, norm_one, scale_one = norm_forward(
        tokens.astype(f32) + branch, gain_one.astype(f32), shift_one.astype(f32)
    )
    normed_b = normed_one.astype(bf16)
    up_rows = jnp.dot(normed_b, w_up, preferred_element_type=f32) + bias_up.astype(f32)
    active, gelu_back = jax.vjp(lambda pre_act: jax.nn.gelu(pre_act, approximate=False), up_rows)
    active_b = active.astype(bf16)
    second = (
        normed_one + jnp.dot(active_b, w_down, preferred_element_type=f32) + bias_down.astype(f32)
    )
    result, norm_two, scale_two = norm_forward(second, gain_two.astype(f32), shift_two.astype(f32))
    grad_second, grad_gain_two, grad_shift_two = norm_backward(
        out_grad[0].astype(f32), norm_two, scale_two, gain_two.astype(f32)
    )
    grad_ffn = grad_second.astype(bf16)
    grad_bias_down = column_sums(grad_ffn)
    grad_w_down = jnp.dot(active_b.T, grad_ffn, preferred_element_type=f32)
    grad_active = jnp.dot(grad_ffn, w_down.T, preferred_element_type=f32)
    grad_up = gelu_back(grad_active)[0].astype(bf16)
    grad_bias_up = column_sums(grad_up)
    grad_w_up = jnp.dot(normed_b.T, grad_up, preferred_element_type=f32)
    grad_normed = grad_second + jnp.dot(grad_up, w_up.T, preferred_element_type=f32)
    grad_first, grad_gain_one, grad_shift_one = norm_backward(
        grad_normed, norm_one, scale_one, gain_one.astype(f32)
    )
    grad_branch = grad_first.astype(bf16)
    grad_bias_out = column_sums(grad_branch)
    grad_w_out = jnp.dot(attended.T, grad_branch, preferred_element_type=f32)
    grad_attended = jnp.dot(grad_branch, w_out.T, preferred_element_type=f32).astype(bf16)
    grad_att_f32 = grad_attended.reshape(tok_rows, head_count, HEAD).astype(f32)
    delta = jnp.einsum("qhd,qhd->hq", grad_att_f32, att_sum)
    delta_ratio = delta / row_total
    grad_scaled = (grad_att_f32 / jnp.transpose(row_total)[:, :, None]).astype(bf16)
    zero_query = jnp.zeros((tok_rows, head_count, HEAD), f32)

    def full_step(running, block_index):
        grad_query, grad_kv = running
        key_heads, value_heads, key_ids = key_block(block_index)
        allowed = (own_ids[:, None] == key_ids[None, :])[None]
        unnorm_b, grad_scores = local_grads(
            head_scores(query_heads, key_heads),
            allowed,
            row_shift,
            delta_ratio,
            grad_scaled,
            value_heads,
        )
        grad_query = (
            grad_query
            + jnp.einsum("hqk,khd->qhd", grad_scores, key_heads, preferred_element_type=f32) * 0.125
        )
        grad_keys = (
            jnp.einsum("hqk,qhd->khd", grad_scores, query_heads, preferred_element_type=f32) * 0.125
        )
        grad_values = jnp.einsum("hqk,qhd->khd", unnorm_b, grad_scaled, preferred_element_type=f32)
        both_grads = jnp.concatenate(
            [grad_keys.reshape(key_span, model_width), grad_values.reshape(key_span, model_width)],
            axis=1,
        )
        grad_kv = lax.dynamic_update_slice_in_dim(grad_kv, both_grads, block_index * key_span, 0)
        return (grad_query, grad_kv)

    start_full = (zero_query, jnp.zeros((seq_rows, 2 * model_width), f32))
    grad_query, grad_kv = sweep(block_total, full_step, start_full)
    own_kv = lax.psum_scatter(grad_kv, "ctx", scatter_dimension=0, tiled=True)
    grad_query_b = grad_query.reshape(tok_rows, model_width).astype(bf16)
    grad_kv_b = own_kv.astype(bf16)
    grad_mixed = jnp.concatenate([grad_query_b, grad_kv_b], axis=1)
    grad_tokens = grad_first + jnp.dot(grad_mixed, w_qkv.T, preferred_element_type=f32)
    grad_w_qkv = jnp.dot(tokens.T, grad_mixed, preferred_element_type=f32)
    grad_bias_query = column_sums(grad_query_b)
    grad_bias_value = column_sums(grad_kv_b[:, model_width:])
    shares = (
        lax.psum_scatter(grad_w_qkv, ("ctx", "fsdp"), scatter_dimension=0, tiled=True),
        lax.psum_scatter(grad_bias_query, ("ctx", "fsdp"), scatter_dimension=0, tiled=True),
        lax.psum_scatter(grad_bias_value, ("ctx", "fsdp"), scatter_dimension=0, tiled=True),
        lax.psum_scatter(grad_w_out, ("ctx", "fsdp"), scatter_dimension=0, tiled=True),
        lax.psum_scatter(grad_bias_out, ("ctx", "fsdp"), scatter_dimension=0, tiled=True),
        lax.psum_scatter(grad_gain_one, ("ctx", "fsdp"), scatter_dimension=0, tiled=True),
        lax.psum_scatter(grad_shift_one, ("ctx", "fsdp"), scatter_dimension=0, tiled=True),
        lax.psum_scatter(grad_w_up, ("ctx", "fsdp"), scatter_dimension=0, tiled=True),
        lax.psum_scatter(grad_bias_up, ("ctx", "fsdp"), scatter_dimension=0, tiled=True),
        lax.psum_scatter(grad_w_down, ("ctx", "fsdp"), scatter_dimension=0, tiled=True),
        lax.psum_scatter(grad_bias_down, ("ctx", "fsdp"), scatter_dimension=0, tiled=True),
        lax.psum_scatter(grad_gain_two, ("ctx", "fsdp"), scatter_dimension=0, tiled=True),
        lax.psum_scatter(grad_shift_two, ("ctx", "fsdp"), scatter_dimension=0, tiled=True),
    )
    summed = (
        lax.psum(shares[0].astype(jnp.bfloat16), "seq").astype(jnp.float32),
        lax.psum(shares[1].astype(jnp.bfloat16), "seq").astype(jnp.float32),
        lax.psum(shares[2].astype(jnp.bfloat16), "seq").astype(jnp.float32),
        lax.psum(shares[3].astype(jnp.bfloat16), "seq").astype(jnp.float32),
        lax.psum(shares[4].astype(jnp.bfloat16), "seq").astype(jnp.float32),
        lax.psum(shares[5].astype(jnp.bfloat16), "seq").astype(jnp.float32),
        lax.psum(shares[6].astype(jnp.bfloat16), "seq").astype(jnp.float32),
        lax.psum(shares[7].astype(jnp.bfloat16), "seq").astype(jnp.float32),
        lax.psum(shares[8].astype(jnp.bfloat16), "seq").astype(jnp.float32),
        lax.psum(shares[9].astype(jnp.bfloat16), "seq").astype(jnp.float32),
        lax.psum(shares[10].astype(jnp.bfloat16), "seq").astype(jnp.float32),
        lax.psum(shares[11].astype(jnp.bfloat16), "seq").astype(jnp.float32),
        lax.psum(shares[12].astype(jnp.bfloat16), "seq").astype(jnp.float32),
    )
    return (
        result.astype(bf16)[None],
        grad_tokens[None],
        summed[0],
        summed[1],
        summed[2],
        summed[3],
        summed[4],
        summed[5],
        summed[6],
        summed[7],
        summed[8],
        summed[9],
        summed[10],
        summed[11],
        summed[12],
    )


MESH_ID = pl.DeviceIdType.MESH
LINE = 4


def remote(src, dst, send, recv, target):
    return pltpu.make_async_remote_copy(
        src_ref=src,
        dst_ref=dst,
        send_sem=send,
        recv_sem=recv,
        device_id=target,
        device_id_type=MESH_ID,
    )


def weight_grad_kernel(dims, *refs):
    count = len(dims)
    a_refs, b_refs, vec_ref = refs[:count], refs[count : 2 * count], refs[2 * count]
    outs = refs[2 * count + 1 : 3 * count + 1]
    vec_out = refs[3 * count + 1]
    rest = refs[3 * count + 2 :]
    units = count + 1
    parts, from_core = rest[:units], rest[units : 2 * units]
    from_pair, from_low = rest[2 * units : 3 * units], rest[3 * units : 4 * units]
    from_high = rest[4 * units : 5 * units]
    vec_seq = rest[5 * units]
    sems = rest[5 * units + 1 :]
    core_out, core_in, pair_out, pair_in, low_out, low_in, high_out, high_in, seq_out, seq_in = sems
    place = lax.axis_index("ctx")
    core = lax.axis_index("fsdp")
    group = lax.axis_index("seq")
    line = place // 2
    side = place % 2
    to_core = {"fsdp": 1 - core}
    to_pair = {"ctx": place + 1 - 2 * side}
    to_seq = {"seq": 1 - group}
    to_up = {"ctx": lax.rem(place + 2, 2 * LINE)}
    to_down = {"ctx": lax.rem(place + 2 * LINE - 2, 2 * LINE)}
    has_low, has_high = line > 0, line < LINE - 1

    barrier = pltpu.get_barrier_semaphore()
    for target in (to_core, to_pair, to_seq):
        pl.semaphore_signal(barrier, inc=1, device_id=target, device_id_type=MESH_ID)

    @pl.when(has_high)
    def _():
        pl.semaphore_signal(barrier, inc=1, device_id=to_up, device_id_type=MESH_ID)

    @pl.when(has_low)
    def _():
        pl.semaphore_signal(barrier, inc=1, device_id=to_down, device_id_type=MESH_ID)

    pl.semaphore_wait(barrier, 3 + has_high.astype(jnp.int32) + has_low.astype(jnp.int32))

    def core_copy(u):
        return remote(parts[u].at[1 - core], from_core[u], core_out.at[u], core_in.at[u], to_core)

    def pair_copy(u, k):
        return remote(
            parts[u].at[core, k, 1 - side],
            from_pair[u].at[k],
            pair_out.at[u, k],
            pair_in.at[u, k],
            to_pair,
        )

    def up_copy(u, k):
        return remote(
            parts[u].at[core, k, side],
            from_low[u].at[k - 1],
            low_out.at[u, k - 1],
            low_in.at[u, k - 1],
            to_up,
        )

    def down_copy(u, k):
        return remote(
            parts[u].at[core, k, side],
            from_high[u].at[k],
            high_out.at[u, k],
            high_in.at[u, k],
            to_down,
        )

    def seq_copy(u):
        if u == count:
            return remote(parts[u].at[core, line, side], vec_seq, seq_out.at[u], seq_in.at[u], to_seq)
        rows, columns, wide = dims[u]
        if wide:
            where = outs[u].at[:, pl.ds(pl.multiple_of(group * columns, 128), columns)]
        else:
            where = outs[u].at[pl.ds(pl.multiple_of(group * rows, 16), rows)]
        return remote(parts[u].at[core, line, side], where, seq_out.at[u], seq_in.at[u], to_seq)

    def multiply(u):
        if u == count:
            parts[u][...] = vec_ref[...]
        else:
            rows, columns, _ = dims[u]
            step = 384
            for first in range(0, columns, step):
                product = lax.dot_general(
                    a_refs[u][...],
                    b_refs[u][:, first : first + step],
                    (((0,), (0,)), ((), ())),
                    preferred_element_type=jnp.float32,
                ).astype(jnp.bfloat16)
                for j in range(4 * LINE):
                    parts[u][j % 2, j // 4, (j // 2) % 2, :, first : first + step] = product[
                        j * rows : (j + 1) * rows
                    ]
        core_copy(u).start()

    def add_core(u):
        core_copy(u).wait_recv()
        for k in (3, 0, 2, 1):
            parts[u][core, k, 1 - side] += from_core[u][k, 1 - side]
            pair_copy(u, k).start()
        for k in range(LINE):
            parts[u][core, k, side] += from_core[u][k, side]

    def add_pair(u):
        for k in (3, 0, 2, 1):
            pair_copy(u, k).wait_recv()
            parts[u][core, k, side] += from_pair[u][k]

        @pl.when(line == 0)
        def _():
            for k in range(LINE - 1, 0, -1):
                up_copy(u, k).start()

        @pl.when(line == LINE - 1)
        def _():
            for k in range(LINE - 1):
                down_copy(u, k).start()

    def pass_up(u, k):
        up_copy(u, k).wait_recv()
        parts[u][core, k, side] += from_low[u][k - 1]
        up_copy(u, k).start()

    def pass_down(u, k):
        down_copy(u, k).wait_recv()
        parts[u][core, k, side] += from_high[u][k]
        down_copy(u, k).start()

    def first_hop(u):
        @pl.when(line == 1)
        def _():
            pass_up(u, 3)
            pass_up(u, 2)

        @pl.when(line == 2)
        def _():
            pass_down(u, 0)
            pass_down(u, 1)

    def second_hop(u):
        @pl.when(line == 2)
        def _():
            pass_up(u, 3)

        @pl.when(line == 1)
        def _():
            pass_down(u, 0)

    def finish(u):
        for k in range(LINE):

            @pl.when(line == k)
            def _(k=k):
                if k > 0:
                    up_copy(u, k).wait_recv()
                    parts[u][core, k, side] += from_low[u][k - 1]
                if k < LINE - 1:
                    down_copy(u, k).wait_recv()
                    parts[u][core, k, side] += from_high[u][k]

        seq_copy(u).start()
        if u < count:
            rows, columns, wide = dims[u]
            if wide:
                start = pl.multiple_of(group * columns, 128)
                outs[u][:, pl.ds(start, columns)] = parts[u][core, line, side]
            else:
                start = pl.multiple_of(group * rows, 16)
                outs[u][pl.ds(start, rows)] = parts[u][core, line, side]

    multiply(0)
    for u in range(units):
        if u + 1 < units:
            multiply(u + 1)
        add_core(u)
    for s in range(units + 3):
        if s < units:
            add_pair(s)
        if 0 <= s - 1 < units:
            first_hop(s - 1)
        if 0 <= s - 2 < units:
            second_hop(s - 2)
        if 0 <= s - 3 < units:
            finish(s - 3)
    for u in range(units):
        seq_copy(u).wait_recv()
    vec_out[...] = parts[count][core, line, side] + vec_seq[...]
    for u in range(units):
        core_copy(u).wait_send()
        seq_copy(u).wait_send()
        for k in range(LINE):
            pair_copy(u, k).wait_send()
        for k in range(1, LINE):

            @pl.when(line < k)
            def _(k=k):
                up_copy(u, k).wait_send()

        for k in range(LINE - 1):

            @pl.when(line > k)
            def _(k=k):
                down_copy(u, k).wait_send()


def weight_grads(a_list, b_list, vec):
    widths = [(a.shape[1], b.shape[1]) for a, b in zip(a_list, b_list)]
    dims, shapes = [], []
    for a_width, b_width in widths:
        rows = a_width // (4 * LINE)
        wide = a_width == a_list[0].shape[1]
        dims.append((rows, b_width, wide))
        shapes.append((rows, 2 * b_width) if wide else (2 * rows, b_width))
    blocks = [((rows, columns), jnp.bfloat16) for rows, columns, _ in dims]
    blocks.append(((8, 128), jnp.float32))
    units = len(blocks)
    scratch = []
    for lead in ((2, LINE, 2), (LINE, 2), (LINE,), (LINE - 1,), (LINE - 1,)):
        scratch += [pltpu.VMEM(lead + block, kind) for block, kind in blocks]
    scratch.append(pltpu.VMEM((8, 128), jnp.float32))
    for lead in ((), (LINE,), (LINE - 1,), (LINE - 1,), ()):
        scratch += [pltpu.SemaphoreType.DMA((units,) + lead)] * 2
    return pl.pallas_call(
        functools.partial(weight_grad_kernel, dims),
        out_shape=[jax.ShapeDtypeStruct(shape, jnp.bfloat16) for shape in shapes]
        + [jax.ShapeDtypeStruct((8, 128), jnp.float32)],
        in_specs=[pl.BlockSpec(memory_space=pltpu.VMEM)] * (2 * len(dims) + 1),
        out_specs=[pl.BlockSpec(memory_space=pltpu.VMEM)] * (len(dims) + 1),
        scratch_shapes=scratch,
        compiler_params=pltpu.CompilerParams(
            collective_id=0, has_side_effects=True, vmem_limit_bytes=60 << 20
        ),
        name="weight_grads",
    )(*a_list, *b_list, vec)


def block_device(
    hidden,
    segment_ids,
    out_grad,
    w_qkv,
    bias_query,
    bias_value,
    w_out,
    bias_out,
    gain_one,
    shift_one,
    w_up,
    bias_up,
    w_down,
    bias_down,
    gain_two,
    shift_two,
):
    (
        w_qkv,
        bias_query,
        bias_value,
        w_out,
        bias_out,
        gain_one,
        shift_one,
        w_up,
        bias_up,
        w_down,
        bias_down,
        gain_two,
        shift_two,
    ) = (
        lax.all_gather(w_qkv, "fsdp", axis=0, tiled=True),
        lax.all_gather(bias_query, "fsdp", axis=0, tiled=True),
        lax.all_gather(bias_value, "fsdp", axis=0, tiled=True),
        lax.all_gather(w_out, "fsdp", axis=0, tiled=True),
        lax.all_gather(bias_out, "fsdp", axis=0, tiled=True),
        lax.all_gather(gain_one, "fsdp", axis=0, tiled=True),
        lax.all_gather(shift_one, "fsdp", axis=0, tiled=True),
        lax.all_gather(w_up, "fsdp", axis=0, tiled=True),
        lax.all_gather(bias_up, "fsdp", axis=0, tiled=True),
        lax.all_gather(w_down, "fsdp", axis=0, tiled=True),
        lax.all_gather(bias_down, "fsdp", axis=0, tiled=True),
        lax.all_gather(gain_two, "fsdp", axis=0, tiled=True),
        lax.all_gather(shift_two, "fsdp", axis=0, tiled=True),
    )
    f32 = jnp.float32
    bf16 = jnp.bfloat16
    tokens = hidden[0]
    tok_rows = tokens.shape[0]
    model_width = tokens.shape[1]
    head_count = model_width // HEAD
    seq_rows = tok_rows * lax.axis_size("ctx")
    key_span = 4 * tok_rows
    block_total = seq_rows // key_span
    doc_ids = segment_ids[0]
    own_ids = lax.dynamic_slice_in_dim(doc_ids, lax.axis_index("ctx") * tok_rows, tok_rows)
    mixed_rows = jnp.dot(tokens, w_qkv, preferred_element_type=f32)
    query_rows = (mixed_rows[:, :model_width] + bias_query.astype(f32)).astype(bf16)
    key_value = jnp.concatenate(
        [
            mixed_rows[:, model_width : 2 * model_width],
            mixed_rows[:, 2 * model_width :] + bias_value.astype(f32),
        ],
        axis=1,
    ).astype(bf16)
    all_kv = lax.all_gather(key_value, "ctx", axis=0, tiled=True)
    query_heads = query_rows.reshape(tok_rows, head_count, HEAD)

    def key_block(block_index):
        kv_piece = lax.dynamic_slice_in_dim(all_kv, block_index * key_span, key_span, 0)
        key_ids = lax.dynamic_slice_in_dim(doc_ids, block_index * key_span, key_span)
        return (
            kv_piece[:, :model_width].reshape(key_span, head_count, HEAD),
            kv_piece[:, model_width:].reshape(key_span, head_count, HEAD),
            key_ids,
        )

    def forward_step(running, block_index):
        level_run, total_run, sum_run = running
        key_heads, value_heads, key_ids = key_block(block_index)
        allowed = (own_ids[:, None] == key_ids[None, :])[None]
        scores = jnp.where(allowed, head_scores(query_heads, key_heads), NEGATIVE)
        level_new = jnp.maximum(level_run, jnp.ceil(jnp.max(scores, axis=-1) * LOG2_E))
        rescale = jnp.exp(LOG_TWO * (level_run - level_new))
        unnorm = jnp.where(allowed, jnp.exp(scores - (LOG_TWO * level_new)[..., None]), 0.0)
        total_new = total_run * rescale + jnp.sum(unnorm, axis=-1)
        sum_new = sum_run * jnp.transpose(rescale)[:, :, None] + jnp.einsum(
            "hqk,khd->qhd", unnorm.astype(bf16), value_heads, preferred_element_type=f32
        )
        return (level_new, total_new, sum_new)

    start_state = (
        jnp.full((head_count, tok_rows), NEGATIVE, f32),
        jnp.zeros((head_count, tok_rows), f32),
        jnp.zeros((tok_rows, head_count, HEAD), f32),
    )
    level_end, row_total, raw_sum = sweep(block_total, forward_step, start_state)
    row_shift = LOG_TWO * level_end
    att_sum = raw_sum / jnp.transpose(row_total)[:, :, None]
    attended = att_sum.reshape(tok_rows, model_width).astype(bf16)
    branch = jnp.dot(attended, w_out, preferred_element_type=f32) + bias_out.astype(f32)
    normed_one, norm_one, scale_one = norm_forward(
        tokens.astype(f32) + branch, gain_one.astype(f32), shift_one.astype(f32)
    )
    normed_b = normed_one.astype(bf16)
    up_rows = jnp.dot(normed_b, w_up, preferred_element_type=f32) + bias_up.astype(f32)
    active, gelu_back = jax.vjp(lambda pre_act: jax.nn.gelu(pre_act, approximate=False), up_rows)
    active_b = active.astype(bf16)
    second = (
        normed_one + jnp.dot(active_b, w_down, preferred_element_type=f32) + bias_down.astype(f32)
    )
    result, norm_two, scale_two = norm_forward(second, gain_two.astype(f32), shift_two.astype(f32))
    grad_second, grad_gain_two, grad_shift_two = norm_backward(
        out_grad[0].astype(f32), norm_two, scale_two, gain_two.astype(f32)
    )
    grad_ffn = grad_second.astype(bf16)
    grad_bias_down = column_sums(grad_ffn)
    grad_active = jnp.dot(grad_ffn, w_down.T, preferred_element_type=f32)
    grad_up = gelu_back(grad_active)[0].astype(bf16)
    grad_bias_up = column_sums(grad_up)
    grad_normed = grad_second + jnp.dot(grad_up, w_up.T, preferred_element_type=f32)
    grad_first, grad_gain_one, grad_shift_one = norm_backward(
        grad_normed, norm_one, scale_one, gain_one.astype(f32)
    )
    grad_branch = grad_first.astype(bf16)
    grad_bias_out = column_sums(grad_branch)
    grad_attended = jnp.dot(grad_branch, w_out.T, preferred_element_type=f32).astype(bf16)
    grad_att_f32 = grad_attended.reshape(tok_rows, head_count, HEAD).astype(f32)
    delta = jnp.einsum("qhd,qhd->hq", grad_att_f32, att_sum)
    delta_ratio = delta / row_total
    grad_scaled = (grad_att_f32 / jnp.transpose(row_total)[:, :, None]).astype(bf16)
    zero_query = jnp.zeros((tok_rows, head_count, HEAD), f32)

    def full_step(running, block_index):
        grad_query, grad_kv = running
        key_heads, value_heads, key_ids = key_block(block_index)
        allowed = (own_ids[:, None] == key_ids[None, :])[None]
        unnorm_b, grad_scores = local_grads(
            head_scores(query_heads, key_heads),
            allowed,
            row_shift,
            delta_ratio,
            grad_scaled,
            value_heads,
        )
        grad_query = (
            grad_query
            + jnp.einsum("hqk,khd->qhd", grad_scores, key_heads, preferred_element_type=f32) * 0.125
        )
        grad_keys = (
            jnp.einsum("hqk,qhd->khd", grad_scores, query_heads, preferred_element_type=f32) * 0.125
        )
        grad_values = jnp.einsum("hqk,qhd->khd", unnorm_b, grad_scaled, preferred_element_type=f32)
        both_grads = jnp.concatenate(
            [grad_keys.reshape(key_span, model_width), grad_values.reshape(key_span, model_width)],
            axis=1,
        )
        grad_kv = lax.dynamic_update_slice_in_dim(grad_kv, both_grads, block_index * key_span, 0)
        return (grad_query, grad_kv)

    start_full = (zero_query, jnp.zeros((seq_rows, 2 * model_width), f32))
    grad_query, grad_kv = sweep(block_total, full_step, start_full)
    own_kv = lax.psum_scatter(grad_kv, "ctx", scatter_dimension=0, tiled=True)
    grad_query_b = grad_query.reshape(tok_rows, model_width).astype(bf16)
    grad_kv_b = own_kv.astype(bf16)
    grad_mixed = jnp.concatenate([grad_query_b, grad_kv_b], axis=1)
    grad_tokens = grad_first + jnp.dot(grad_mixed, w_qkv.T, preferred_element_type=f32)
    grad_bias_query = column_sums(grad_query_b)
    grad_bias_value = column_sums(grad_kv_b[:, model_width:])
    group = lax.axis_index("seq")
    pick = active_b.reshape(tok_rows, 16, 2, active_b.shape[1] // 32)

    def halves(values):
        width = values.shape[1] // 2
        own = lax.dynamic_slice_in_dim(values, group * width, width, 1)
        return own, lax.dynamic_slice_in_dim(values, (1 - group) * width, width, 1)

    def with_partner(own, sent):
        return jnp.concatenate([own, lax.ppermute(sent, "seq", [(0, 1), (1, 0)])], axis=0)

    def blocks_of(which):
        return lax.dynamic_index_in_dim(pick, which, 2, False).reshape(tok_rows, -1)

    a_list = [
        with_partner(normed_b, normed_b),
        with_partner(blocks_of(group), blocks_of(1 - group)),
        with_partner(tokens, tokens),
        with_partner(attended, attended),
    ]
    b_list = [
        with_partner(*halves(grad_up)),
        with_partner(grad_ffn, grad_ffn),
        with_partner(*halves(grad_mixed)),
        with_partner(*halves(grad_branch)),
    ]
    vectors = [
        grad_bias_query,
        grad_bias_value,
        grad_bias_out,
        grad_gain_one,
        grad_shift_one,
        grad_bias_up,
        grad_bias_down,
        grad_gain_two,
        grad_shift_two,
    ]
    packed = jnp.concatenate([v.reshape(16, -1) for v in vectors], axis=1)
    packed = jnp.pad(packed, ((0, 0), (0, 1024 - packed.shape[1])))
    packed = jnp.transpose(packed.reshape(LINE, 2, 2, 8, 128), (2, 0, 1, 3, 4))
    up_own, down_own, qkv_own, out_own, vec_own = weight_grads(a_list, b_list, packed)
    flat = vec_own.reshape(-1)
    summed, at = [], 0
    for v in vectors:
        summed.append(lax.slice_in_dim(flat, at, at + v.shape[0] // 16))
        at += v.shape[0] // 16
    return (
        result.astype(bf16)[None],
        grad_tokens[None],
        qkv_own.astype(f32),
        summed[0],
        summed[1],
        out_own.astype(f32),
        summed[2],
        summed[3],
        summed[4],
        up_own.astype(f32),
        summed[5],
        down_own.astype(f32),
        summed[6],
        summed[7],
        summed[8],
    )


def solution(mesh):
    small = (mesh.shape["seq"], mesh.shape["ctx"], mesh.shape["fsdp"]) == (2, 8, 2)
    return jax.shard_map(
        block_device if small else on_device,
        mesh=mesh,
        in_specs=(
            P(("seq", "fsdp"), "ctx", None),
            P(("seq", "fsdp"), None),
            P(("seq", "fsdp"), "ctx", None),
            P("fsdp", None),
            P("fsdp"),
            P("fsdp"),
            P("fsdp", None),
            P("fsdp"),
            P("fsdp"),
            P("fsdp"),
            P("fsdp", None),
            P("fsdp"),
            P("fsdp", None),
            P("fsdp"),
            P("fsdp"),
            P("fsdp"),
        ),
        out_specs=(
            P(("seq", "fsdp"), "ctx", None),
            P(("seq", "fsdp"), "ctx", None),
            P(("ctx", "fsdp"), None),
            P(("ctx", "fsdp")),
            P(("ctx", "fsdp")),
            P(("ctx", "fsdp"), None),
            P(("ctx", "fsdp")),
            P(("ctx", "fsdp")),
            P(("ctx", "fsdp")),
            P(("ctx", "fsdp"), None),
            P(("ctx", "fsdp")),
            P(("ctx", "fsdp"), None),
            P(("ctx", "fsdp")),
            P(("ctx", "fsdp")),
            P(("ctx", "fsdp")),
        ),
        check_vma=False,
    )
```

```python
import functools

import jax
import jax.numpy as jnp
from jax import lax
from jax.experimental import pallas as pl
from jax.experimental.pallas import tpu as pltpu
from jax.sharding import PartitionSpec as P

HEAD = 64


EPSILON = 1e-12
NEGATIVE = -1e30
LOG_TWO = 0.6931471805599453
LOG2_E = 1.4426950408889634


def norm_forward(rows_in, gain_vec, shift_vec):
    row_mean = jnp.mean(rows_in, axis=-1, keepdims=True)
    centered = rows_in - row_mean
    variance = jnp.mean(centered * centered, axis=-1, keepdims=True)
    scaled = lax.rsqrt(variance + EPSILON)
    normed = centered * scaled
    return (normed * gain_vec + shift_vec, normed, scaled)


def norm_backward(grad_rows, normed, scaled, gain_vec):
    grad_normed = grad_rows * gain_vec
    inner_part = (
        grad_normed
        - jnp.mean(grad_normed, axis=-1, keepdims=True)
        - normed * jnp.mean(grad_normed * normed, axis=-1, keepdims=True)
    )
    return (inner_part * scaled, jnp.sum(grad_rows * normed, axis=0), jnp.sum(grad_rows, axis=0))


def head_scores(query_heads, key_heads):
    return (
        jnp.einsum("qhd,khd->hqk", query_heads, key_heads, preferred_element_type=jnp.float32)
        * 0.125
    )


def column_sums(rows_b):
    return jnp.sum(rows_b.astype(jnp.float32), axis=0)


def sweep(steps_total, advance, start_carry):

    def advance_one(running, block_index):
        running = advance(running, block_index)
        return (running, None)

    return lax.scan(advance_one, start_carry, jnp.arange(steps_total))[0]


def local_grads(scores, allowed, shift_rows, ratio_rows, grad_heads, value_heads):
    unnorm = jnp.where(allowed, jnp.exp(scores - shift_rows[..., None]), 0.0)
    grad_weights = jnp.einsum(
        "qhd,khd->hqk", grad_heads, value_heads, preferred_element_type=jnp.float32
    )
    grad_scores = (unnorm * (grad_weights - ratio_rows[..., None])).astype(jnp.bfloat16)
    return (unnorm.astype(jnp.bfloat16), grad_scores)


def on_device(
    hidden,
    segment_ids,
    out_grad,
    w_qkv,
    bias_query,
    bias_value,
    w_out,
    bias_out,
    gain_one,
    shift_one,
    w_up,
    bias_up,
    w_down,
    bias_down,
    gain_two,
    shift_two,
):
    (
        w_qkv,
        bias_query,
        bias_value,
        w_out,
        bias_out,
        gain_one,
        shift_one,
        w_up,
        bias_up,
        w_down,
        bias_down,
        gain_two,
        shift_two,
    ) = (
        lax.all_gather(w_qkv, "fsdp", axis=0, tiled=True),
        lax.all_gather(bias_query, "fsdp", axis=0, tiled=True),
        lax.all_gather(bias_value, "fsdp", axis=0, tiled=True),
        lax.all_gather(w_out, "fsdp", axis=0, tiled=True),
        lax.all_gather(bias_out, "fsdp", axis=0, tiled=True),
        lax.all_gather(gain_one, "fsdp", axis=0, tiled=True),
        lax.all_gather(shift_one, "fsdp", axis=0, tiled=True),
        lax.all_gather(w_up, "fsdp", axis=0, tiled=True),
        lax.all_gather(bias_up, "fsdp", axis=0, tiled=True),
        lax.all_gather(w_down, "fsdp", axis=0, tiled=True),
        lax.all_gather(bias_down, "fsdp", axis=0, tiled=True),
        lax.all_gather(gain_two, "fsdp", axis=0, tiled=True),
        lax.all_gather(shift_two, "fsdp", axis=0, tiled=True),
    )
    f32 = jnp.float32
    bf16 = jnp.bfloat16
    tokens = hidden[0]
    tok_rows = tokens.shape[0]
    model_width = tokens.shape[1]
    head_count = model_width // HEAD
    seq_rows = tok_rows * lax.axis_size("ctx")
    key_span = 4 * tok_rows
    block_total = seq_rows // key_span
    doc_ids = segment_ids[0]
    own_ids = lax.dynamic_slice_in_dim(doc_ids, lax.axis_index("ctx") * tok_rows, tok_rows)
    mixed_rows = jnp.dot(tokens, w_qkv, preferred_element_type=f32)
    query_rows = (mixed_rows[:, :model_width] + bias_query.astype(f32)).astype(bf16)
    key_value = jnp.concatenate(
        [
            mixed_rows[:, model_width : 2 * model_width],
            mixed_rows[:, 2 * model_width :] + bias_value.astype(f32),
        ],
        axis=1,
    ).astype(bf16)
    all_kv = lax.all_gather(key_value, "ctx", axis=0, tiled=True)
    query_heads = query_rows.reshape(tok_rows, head_count, HEAD)

    def key_block(block_index):
        kv_piece = lax.dynamic_slice_in_dim(all_kv, block_index * key_span, key_span, 0)
        key_ids = lax.dynamic_slice_in_dim(doc_ids, block_index * key_span, key_span)
        return (
            kv_piece[:, :model_width].reshape(key_span, head_count, HEAD),
            kv_piece[:, model_width:].reshape(key_span, head_count, HEAD),
            key_ids,
        )

    def forward_step(running, block_index):
        level_run, total_run, sum_run = running
        key_heads, value_heads, key_ids = key_block(block_index)
        allowed = (own_ids[:, None] == key_ids[None, :])[None]
        scores = jnp.where(allowed, head_scores(query_heads, key_heads), NEGATIVE)
        level_new = jnp.maximum(level_run, jnp.ceil(jnp.max(scores, axis=-1) * LOG2_E))
        rescale = jnp.exp(LOG_TWO * (level_run - level_new))
        unnorm = jnp.where(allowed, jnp.exp(scores - (LOG_TWO * level_new)[..., None]), 0.0)
        total_new = total_run * rescale + jnp.sum(unnorm, axis=-1)
        sum_new = sum_run * jnp.transpose(rescale)[:, :, None] + jnp.einsum(
            "hqk,khd->qhd", unnorm.astype(bf16), value_heads, preferred_element_type=f32
        )
        return (level_new, total_new, sum_new)

    start_state = (
        jnp.full((head_count, tok_rows), NEGATIVE, f32),
        jnp.zeros((head_count, tok_rows), f32),
        jnp.zeros((tok_rows, head_count, HEAD), f32),
    )
    level_end, row_total, raw_sum = sweep(block_total, forward_step, start_state)
    row_shift = LOG_TWO * level_end
    att_sum = raw_sum / jnp.transpose(row_total)[:, :, None]
    attended = att_sum.reshape(tok_rows, model_width).astype(bf16)
    branch = jnp.dot(attended, w_out, preferred_element_type=f32) + bias_out.astype(f32)
    normed_one, norm_one, scale_one = norm_forward(
        tokens.astype(f32) + branch, gain_one.astype(f32), shift_one.astype(f32)
    )
    normed_b = normed_one.astype(bf16)
    up_rows = jnp.dot(normed_b, w_up, preferred_element_type=f32) + bias_up.astype(f32)
    active, gelu_back = jax.vjp(lambda pre_act: jax.nn.gelu(pre_act, approximate=False), up_rows)
    active_b = active.astype(bf16)
    second = (
        normed_one + jnp.dot(active_b, w_down, preferred_element_type=f32) + bias_down.astype(f32)
    )
    result, norm_two, scale_two = norm_forward(second, gain_two.astype(f32), shift_two.astype(f32))
    grad_second, grad_gain_two, grad_shift_two = norm_backward(
        out_grad[0].astype(f32), norm_two, scale_two, gain_two.astype(f32)
    )
    grad_ffn = grad_second.astype(bf16)
    grad_bias_down = column_sums(grad_ffn)
    grad_w_down = jnp.dot(active_b.T, grad_ffn, preferred_element_type=f32)
    grad_active = jnp.dot(grad_ffn, w_down.T, preferred_element_type=f32)
    grad_up = gelu_back(grad_active)[0].astype(bf16)
    grad_bias_up = column_sums(grad_up)
    grad_w_up = jnp.dot(normed_b.T, grad_up, preferred_element_type=f32)
    grad_normed = grad_second + jnp.dot(grad_up, w_up.T, preferred_element_type=f32)
    grad_first, grad_gain_one, grad_shift_one = norm_backward(
        grad_normed, norm_one, scale_one, gain_one.astype(f32)
    )
    grad_branch = grad_first.astype(bf16)
    grad_bias_out = column_sums(grad_branch)
    grad_w_out = jnp.dot(attended.T, grad_branch, preferred_element_type=f32)
    grad_attended = jnp.dot(grad_branch, w_out.T, preferred_element_type=f32).astype(bf16)
    grad_att_f32 = grad_attended.reshape(tok_rows, head_count, HEAD).astype(f32)
    delta = jnp.einsum("qhd,qhd->hq", grad_att_f32, att_sum)
    delta_ratio = delta / row_total
    grad_scaled = (grad_att_f32 / jnp.transpose(row_total)[:, :, None]).astype(bf16)
    zero_query = jnp.zeros((tok_rows, head_count, HEAD), f32)

    def full_step(running, block_index):
        grad_query, grad_kv = running
        key_heads, value_heads, key_ids = key_block(block_index)
        allowed = (own_ids[:, None] == key_ids[None, :])[None]
        unnorm_b, grad_scores = local_grads(
            head_scores(query_heads, key_heads),
            allowed,
            row_shift,
            delta_ratio,
            grad_scaled,
            value_heads,
        )
        grad_query = (
            grad_query
            + jnp.einsum("hqk,khd->qhd", grad_scores, key_heads, preferred_element_type=f32) * 0.125
        )
        grad_keys = (
            jnp.einsum("hqk,qhd->khd", grad_scores, query_heads, preferred_element_type=f32) * 0.125
        )
        grad_values = jnp.einsum("hqk,qhd->khd", unnorm_b, grad_scaled, preferred_element_type=f32)
        both_grads = jnp.concatenate(
            [grad_keys.reshape(key_span, model_width), grad_values.reshape(key_span, model_width)],
            axis=1,
        )
        grad_kv = lax.dynamic_update_slice_in_dim(grad_kv, both_grads, block_index * key_span, 0)
        return (grad_query, grad_kv)

    start_full = (zero_query, jnp.zeros((seq_rows, 2 * model_width), f32))
    grad_query, grad_kv = sweep(block_total, full_step, start_full)
    own_kv = lax.psum_scatter(grad_kv, "ctx", scatter_dimension=0, tiled=True)
    grad_query_b = grad_query.reshape(tok_rows, model_width).astype(bf16)
    grad_kv_b = own_kv.astype(bf16)
    grad_mixed = jnp.concatenate([grad_query_b, grad_kv_b], axis=1)
    grad_tokens = grad_first + jnp.dot(grad_mixed, w_qkv.T, preferred_element_type=f32)
    grad_w_qkv = jnp.dot(tokens.T, grad_mixed, preferred_element_type=f32)
    grad_bias_query = column_sums(grad_query_b)
    grad_bias_value = column_sums(grad_kv_b[:, model_width:])
    shares = (
        lax.psum_scatter(grad_w_qkv, ("ctx", "fsdp"), scatter_dimension=0, tiled=True),
        lax.psum_scatter(grad_bias_query, ("ctx", "fsdp"), scatter_dimension=0, tiled=True),
        lax.psum_scatter(grad_bias_value, ("ctx", "fsdp"), scatter_dimension=0, tiled=True),
        lax.psum_scatter(grad_w_out, ("ctx", "fsdp"), scatter_dimension=0, tiled=True),
        lax.psum_scatter(grad_bias_out, ("ctx", "fsdp"), scatter_dimension=0, tiled=True),
        lax.psum_scatter(grad_gain_one, ("ctx", "fsdp"), scatter_dimension=0, tiled=True),
        lax.psum_scatter(grad_shift_one, ("ctx", "fsdp"), scatter_dimension=0, tiled=True),
        lax.psum_scatter(grad_w_up, ("ctx", "fsdp"), scatter_dimension=0, tiled=True),
        lax.psum_scatter(grad_bias_up, ("ctx", "fsdp"), scatter_dimension=0, tiled=True),
        lax.psum_scatter(grad_w_down, ("ctx", "fsdp"), scatter_dimension=0, tiled=True),
        lax.psum_scatter(grad_bias_down, ("ctx", "fsdp"), scatter_dimension=0, tiled=True),
        lax.psum_scatter(grad_gain_two, ("ctx", "fsdp"), scatter_dimension=0, tiled=True),
        lax.psum_scatter(grad_shift_two, ("ctx", "fsdp"), scatter_dimension=0, tiled=True),
    )
    summed = (
        lax.psum(shares[0].astype(jnp.bfloat16), "seq").astype(jnp.float32),
        lax.psum(shares[1].astype(jnp.bfloat16), "seq").astype(jnp.float32),
        lax.psum(shares[2].astype(jnp.bfloat16), "seq").astype(jnp.float32),
        lax.psum(shares[3].astype(jnp.bfloat16), "seq").astype(jnp.float32),
        lax.psum(shares[4].astype(jnp.bfloat16), "seq").astype(jnp.float32),
        lax.psum(shares[5].astype(jnp.bfloat16), "seq").astype(jnp.float32),
        lax.psum(shares[6].astype(jnp.bfloat16), "seq").astype(jnp.float32),
        lax.psum(shares[7].astype(jnp.bfloat16), "seq").astype(jnp.float32),
        lax.psum(shares[8].astype(jnp.bfloat16), "seq").astype(jnp.float32),
        lax.psum(shares[9].astype(jnp.bfloat16), "seq").astype(jnp.float32),
        lax.psum(shares[10].astype(jnp.bfloat16), "seq").astype(jnp.float32),
        lax.psum(shares[11].astype(jnp.bfloat16), "seq").astype(jnp.float32),
        lax.psum(shares[12].astype(jnp.bfloat16), "seq").astype(jnp.float32),
    )
    return (
        result.astype(bf16)[None],
        grad_tokens[None],
        summed[0],
        summed[1],
        summed[2],
        summed[3],
        summed[4],
        summed[5],
        summed[6],
        summed[7],
        summed[8],
        summed[9],
        summed[10],
        summed[11],
        summed[12],
    )


MESH_ID = pl.DeviceIdType.MESH
LINE = 4


def remote(src, dst, send, recv, target):
    return pltpu.make_async_remote_copy(
        src_ref=src,
        dst_ref=dst,
        send_sem=send,
        recv_sem=recv,
        device_id=target,
        device_id_type=MESH_ID,
    )


def weight_grad_kernel(dims, *refs):
    count = len(dims)
    operands, vec_ref = refs[: 4 * count], refs[4 * count]
    outs = refs[4 * count + 1 : 5 * count + 1]
    vec_out = refs[5 * count + 1]
    rest = refs[5 * count + 2 :]
    units = count + 1
    parts, from_core = rest[:units], rest[units : 2 * units]
    from_pair, from_low = rest[2 * units : 3 * units], rest[3 * units : 4 * units]
    from_high = rest[4 * units : 5 * units]
    vec_seq = rest[5 * units]
    sems = rest[5 * units + 1 :]
    core_out, core_in, pair_out, pair_in, low_out, low_in, high_out, high_in, seq_out, seq_in = sems
    place = lax.axis_index("ctx")
    core = lax.axis_index("fsdp")
    group = lax.axis_index("seq")
    line = place // 2
    side = place % 2
    to_core = {"fsdp": 1 - core}
    to_pair = {"ctx": place + 1 - 2 * side}
    to_seq = {"seq": 1 - group}
    to_up = {"ctx": lax.rem(place + 2, 2 * LINE)}
    to_down = {"ctx": lax.rem(place + 2 * LINE - 2, 2 * LINE)}
    has_low, has_high = line > 0, line < LINE - 1

    barrier = pltpu.get_barrier_semaphore()
    for target in (to_core, to_pair, to_seq):
        pl.semaphore_signal(barrier, inc=1, device_id=target, device_id_type=MESH_ID)

    @pl.when(has_high)
    def _():
        pl.semaphore_signal(barrier, inc=1, device_id=to_up, device_id_type=MESH_ID)

    @pl.when(has_low)
    def _():
        pl.semaphore_signal(barrier, inc=1, device_id=to_down, device_id_type=MESH_ID)

    pl.semaphore_wait(barrier, 3 + has_high.astype(jnp.int32) + has_low.astype(jnp.int32))

    def core_copy(u):
        return remote(parts[u].at[1 - core], from_core[u], core_out.at[u], core_in.at[u], to_core)

    def pair_copy(u, k):
        return remote(
            parts[u].at[core, k, 1 - side],
            from_pair[u].at[k],
            pair_out.at[u, k],
            pair_in.at[u, k],
            to_pair,
        )

    def up_copy(u, k):
        return remote(
            parts[u].at[core, k, side],
            from_low[u].at[k - 1],
            low_out.at[u, k - 1],
            low_in.at[u, k - 1],
            to_up,
        )

    def down_copy(u, k):
        return remote(
            parts[u].at[core, k, side],
            from_high[u].at[k],
            high_out.at[u, k],
            high_in.at[u, k],
            to_down,
        )

    def seq_copy(u):
        if u == count:
            return remote(parts[u].at[core, line, side], vec_seq, seq_out.at[u], seq_in.at[u], to_seq)
        rows, columns, wide = dims[u]
        if wide:
            where = outs[u].at[:, pl.ds(pl.multiple_of(group * columns, 128), columns)]
        else:
            where = outs[u].at[pl.ds(pl.multiple_of(group * rows, 16), rows)]
        return remote(parts[u].at[core, line, side], where, seq_out.at[u], seq_in.at[u], to_seq)

    def multiply(u):
        if u == count:
            parts[u][...] = vec_ref[...]
        else:
            rows, columns, _ = dims[u]
            step = 384
            for first in range(0, columns, step):
                a_own, a_pair, b_own, b_pair = operands[4 * u : 4 * u + 4]
                span = slice(first, first + step)
                own_b = b_own[group, :, span] if len(b_own.shape) == 3 else b_own[:, span]
                own_a = a_own[group] if len(a_own.shape) == 3 else a_own[...]
                product = (dot_tn(own_a, own_b) + dot_tn(a_pair[...], b_pair[:, span])).astype(BF16)
                for j in range(4 * LINE):
                    parts[u][j % 2, j // 4, (j // 2) % 2, :, first : first + step] = product[
                        j * rows : (j + 1) * rows
                    ]
        core_copy(u).start()

    def add_core(u):
        core_copy(u).wait_recv()
        for k in (3, 0, 2, 1):
            parts[u][core, k, 1 - side] += from_core[u][k, 1 - side]
            pair_copy(u, k).start()
        for k in range(LINE):
            parts[u][core, k, side] += from_core[u][k, side]

    def add_pair(u):
        for k in (3, 0, 2, 1):
            pair_copy(u, k).wait_recv()
            parts[u][core, k, side] += from_pair[u][k]

        @pl.when(line == 0)
        def _():
            for k in range(LINE - 1, 0, -1):
                up_copy(u, k).start()

        @pl.when(line == LINE - 1)
        def _():
            for k in range(LINE - 1):
                down_copy(u, k).start()

    def pass_up(u, k):
        up_copy(u, k).wait_recv()
        parts[u][core, k, side] += from_low[u][k - 1]
        up_copy(u, k).start()

    def pass_down(u, k):
        down_copy(u, k).wait_recv()
        parts[u][core, k, side] += from_high[u][k]
        down_copy(u, k).start()

    def first_hop(u):
        @pl.when(line == 1)
        def _():
            pass_up(u, 3)
            pass_up(u, 2)

        @pl.when(line == 2)
        def _():
            pass_down(u, 0)
            pass_down(u, 1)

    def second_hop(u):
        @pl.when(line == 2)
        def _():
            pass_up(u, 3)

        @pl.when(line == 1)
        def _():
            pass_down(u, 0)

    def finish(u):
        for k in range(LINE):

            @pl.when(line == k)
            def _(k=k):
                if k > 0:
                    up_copy(u, k).wait_recv()
                    parts[u][core, k, side] += from_low[u][k - 1]
                if k < LINE - 1:
                    down_copy(u, k).wait_recv()
                    parts[u][core, k, side] += from_high[u][k]

        seq_copy(u).start()
        if u < count:
            rows, columns, wide = dims[u]
            if wide:
                start = pl.multiple_of(group * columns, 128)
                outs[u][:, pl.ds(start, columns)] = parts[u][core, line, side]
            else:
                start = pl.multiple_of(group * rows, 16)
                outs[u][pl.ds(start, rows)] = parts[u][core, line, side]

    multiply(0)
    for u in range(units):
        if u + 1 < units:
            multiply(u + 1)
        add_core(u)
    for s in range(units + 3):
        if s < units:
            add_pair(s)
        if 0 <= s - 1 < units:
            first_hop(s - 1)
        if 0 <= s - 2 < units:
            second_hop(s - 2)
        if 0 <= s - 3 < units:
            finish(s - 3)
    for u in range(units):
        seq_copy(u).wait_recv()
    vec_out[...] = parts[count][core, line, side] + vec_seq[...]
    for u in range(units):
        core_copy(u).wait_send()
        seq_copy(u).wait_send()
        for k in range(LINE):
            pair_copy(u, k).wait_send()
        for k in range(1, LINE):

            @pl.when(line < k)
            def _(k=k):
                up_copy(u, k).wait_send()

        for k in range(LINE - 1):

            @pl.when(line > k)
            def _(k=k):
                down_copy(u, k).wait_send()


def weight_grads(operands, vec):
    widths = [(group[1].shape[1], group[3].shape[1]) for group in operands]
    dims, shapes = [], []
    for a_width, b_width in widths:
        rows = a_width // (4 * LINE)
        wide = a_width == widths[0][0]
        dims.append((rows, b_width, wide))
        shapes.append((rows, 2 * b_width) if wide else (2 * rows, b_width))
    blocks = [((rows, columns), jnp.bfloat16) for rows, columns, _ in dims]
    blocks.append(((8, 128), jnp.float32))
    units = len(blocks)
    scratch = []
    for lead in ((2, LINE, 2), (LINE, 2), (LINE,), (LINE - 1,), (LINE - 1,)):
        scratch += [pltpu.VMEM(lead + block, kind) for block, kind in blocks]
    scratch.append(pltpu.VMEM((8, 128), jnp.float32))
    for lead in ((), (LINE,), (LINE - 1,), (LINE - 1,), ()):
        scratch += [pltpu.SemaphoreType.DMA((units,) + lead)] * 2
    return pl.pallas_call(
        functools.partial(weight_grad_kernel, dims),
        out_shape=[jax.ShapeDtypeStruct(shape, jnp.bfloat16) for shape in shapes]
        + [jax.ShapeDtypeStruct((8, 128), jnp.float32)],
        in_specs=[pl.BlockSpec(memory_space=pltpu.VMEM)] * (4 * len(dims) + 1),
        out_specs=[pl.BlockSpec(memory_space=pltpu.VMEM)] * (len(dims) + 1),
        scratch_shapes=scratch,
        compiler_params=pltpu.CompilerParams(
            collective_id=0, has_side_effects=True, vmem_limit_bytes=60 << 20
        ),
        name="weight_grads",
    )(*[a for group in operands for a in group], vec)


HEADS_OWN = 3
F32 = jnp.float32
BF16 = jnp.bfloat16
ANY = pl.BlockSpec(memory_space=pl.ANY)
INNER = pl.BlockSpec(memory_space=pltpu.VMEM)


def dot_nt(a, b):
    return lax.dot_general(a, b, (((1,), (1,)), ((), ())), preferred_element_type=F32)


def dot_tn(a, b):
    return lax.dot_general(a, b, (((0,), (0,)), ((), ())), preferred_element_type=F32)


def dot_nn(a, b):
    return lax.dot_general(a, b, (((1,), (0,)), ((), ())), preferred_element_type=F32)


def greet(targets):
    barrier = pltpu.get_barrier_semaphore()
    for target in targets:
        pl.semaphore_signal(barrier, inc=1, device_id=target, device_id_type=MESH_ID)
    pl.semaphore_wait(barrier, len(targets))


def attend_kernel(
    tok,
    ids_row,
    ids_col,
    vec,
    w_qkv,
    w_out,
    w_up,
    w_down,
    attended,
    tok_pair,
    vec_all,
    w_full,
    out_other,
    up_other,
    down_other,
    q_heads,
    k_heads,
    v_heads,
    att_full,
    totals,
    probs_out,
    w_all,
    mixed,
    sent,
    mine,
    other,
    att_sent,
    att_land,
    probs,
    local_sem,
    probs_sem,
    core_out,
    core_in,
    line_out,
    line_in,
    pair_out,
    pair_in,
    back_out,
    back_in,
    seq_out,
    seq_in,
):
    place = lax.axis_index("ctx")
    core = lax.axis_index("fsdp")
    group = lax.axis_index("seq")
    line, side = place // 2, place % 2
    to_core = {"fsdp": 1 - core}
    to_pair = {"ctx": place + 1 - 2 * side}
    to_seq = {"seq": 1 - group}
    rows = tok.shape[0]
    width = tok.shape[1]
    half = width // 2
    third = HEADS_OWN * HEAD

    def ahead(k):
        return lax.rem(line + k, LINE)

    def behind(k):
        return lax.rem(line + LINE - k, LINE)

    def to_line(k):
        return {"ctx": 2 * ahead(k) + side}

    def block(which):
        return pl.ds(pl.multiple_of(which * rows, 32), rows)

    own_rows = pl.ds(pl.multiple_of(core * half, 128), half)
    other_rows = pl.ds(pl.multiple_of((1 - core) * half, 128), half)

    own_load = pltpu.make_async_copy(w_qkv, w_all.at[own_rows], local_sem.at[0])
    own_load.start()
    greet([to_core, to_pair, to_seq] + [to_line(k) for k in range(1, LINE)])
    core_copies = [
        remote(w_qkv, w_all.at[own_rows], core_out.at[0], core_in.at[0], to_core),
        remote(vec, vec_all.at[:, own_rows], core_out.at[1], core_in.at[1], to_core),
        remote(w_out, out_other, core_out.at[2], core_in.at[2], to_core),
        remote(w_up, up_other, core_out.at[3], core_in.at[3], to_core),
        remote(w_down, down_other, core_out.at[4], core_in.at[4], to_core),
    ]
    seq_copy = remote(tok, tok_pair, seq_out.at[0], seq_in.at[0], to_seq)
    core_copies[0].start()
    core_copies[1].start()
    seq_copy.start()
    vec_all[:, own_rows] = vec[...]
    own_load.wait()
    step = width // 2
    for first in range(0, 3 * width, step):
        mixed[:, first : first + step] = dot_nn(
            tok[:, own_rows], w_all[own_rows, first : first + step]
        )
    core_copies[0].wait_recv()
    core_copies[1].wait_recv()
    for copy in core_copies[2:]:
        copy.start()
    bias = vec_all[...]
    for part in (1, 2, 0):
        for first in range(part * width, (part + 1) * width, step):
            total = mixed[:, first : first + step] + dot_nn(
                tok[:, other_rows], w_all[other_rows, first : first + step]
            )
            within = first - part * width
            if part == 0:
                total += bias[0:1, within : within + step]
            if part == 2:
                total += bias[1:2, within : within + step]
            total = total.astype(BF16)
            slot = (2, 0, 1)[part] * third
            for j in range(2):
                sent[within // third + j, :, slot : slot + third] = total[
                    :, j * third : (j + 1) * third
                ]

    def line_copy(k):
        return remote(
            sent.at[ahead(k)], mine.at[block(line)], line_out.at[k - 1], line_in.at[k - 1], to_line(k)
        )

    def line_landed(k):
        return remote(
            sent.at[ahead(k)],
            mine.at[block(behind(k))],
            line_out.at[k - 1],
            line_in.at[k - 1],
            to_line(k),
        )

    def pair_copy(k):
        where = block(behind(k))
        return remote(
            mine.at[where, 0 : 2 * third],
            other.at[where],
            pair_out.at[k],
            pair_in.at[k],
            to_pair,
        )

    for k in (3, 2, 1):
        line_copy(k).start()
    full_store = pltpu.make_async_copy(w_all, w_full, local_sem.at[1])
    full_store.start()
    mine[block(line)] = sent[line]
    pair_copy(0).start()
    for k in (1, 2, 3):
        line_landed(k).wait_recv()
        pair_copy(k).start()
    seq_rows = 2 * LINE * rows
    mid = LINE * rows
    for h in range(HEADS_OWN):
        q_heads[h] = mine[:, 2 * third + h * HEAD : 2 * third + (h + 1) * HEAD]
        k_heads[h, 0:mid] = mine[:, h * HEAD : (h + 1) * HEAD]
        v_heads[h, 0:mid] = mine[:, third + h * HEAD : third + (h + 1) * HEAD]
    for k in range(LINE):
        pair_copy(k).wait_recv()
    for h in range(HEADS_OWN):
        k_heads[h, mid:seq_rows] = other[:, h * HEAD : (h + 1) * HEAD]
        v_heads[h, mid:seq_rows] = other[:, third + h * HEAD : third + (h + 1) * HEAD]

    def back_copy(k):
        return remote(
            att_sent.at[ahead(k)],
            att_land.at[line],
            back_out.at[k - 1],
            back_in.at[k - 1],
            to_line(k),
        )

    def back_landed(k):
        return remote(
            att_sent.at[ahead(k)],
            att_land.at[behind(k)],
            back_out.at[k - 1],
            back_in.at[k - 1],
            to_line(k),
        )

    def probs_copy(k):
        where = block(ahead(k))
        return pltpu.make_async_copy(
            probs.at[:, where], probs_out.at[:, where], probs_sem.at[k - 1]
        )

    def attend(k, carry):
        which = ahead(k)
        where = block(which)
        allowed = ids_col[where] == ids_row[...]
        for h in range(HEADS_OWN):
            scores = dot_nt(q_heads[h, where], k_heads[h]) * 0.125
            scores = jnp.where(allowed, scores, NEGATIVE)
            level = jnp.ceil(jnp.max(scores, axis=-1, keepdims=True) * LOG2_E)
            unnorm = jnp.exp(scores - LOG_TWO * level)
            row_total = jnp.sum(unnorm, axis=-1, keepdims=True)
            unnorm_b = unnorm.astype(BF16)
            probs[h, where] = unnorm_b
            value = dot_nn(unnorm_b, v_heads[h]) / row_total
            att_full[where, h * HEAD : (h + 1) * HEAD] = value
            totals[where, h : h + 1] = row_total
            att_sent[which, :, h * HEAD : (h + 1) * HEAD] = value.astype(BF16)
        probs_copy(k).start()

        @pl.when(k < LINE)
        def _():
            back_copy(k).start()

        return carry

    lax.fori_loop(1, LINE + 1, attend, 0)
    att_land[line] = att_sent[line]
    for k in (1, 2, 3):
        back_landed(k).wait_recv()
    for d in range(LINE):
        attended[:, d * third : (d + 1) * third] = att_land[d]
    for k in (1, 2, 3):
        line_copy(k).wait_send()
        back_copy(k).wait_send()
    for k in range(LINE):
        pair_copy(k).wait_send()
        probs_copy(k + 1).wait()
    for copy in core_copies[2:]:
        copy.wait_recv()
    for copy in core_copies:
        copy.wait_send()
    seq_copy.wait()
    full_store.wait()


def attend_forward(tok, ids_row, ids_col, vec, w_qkv, w_out, w_up, w_down):
    rows, width = tok.shape
    third = HEADS_OWN * HEAD
    mid, seq_rows = LINE * rows, 2 * LINE * rows
    shape = jax.ShapeDtypeStruct
    outs = [
        (shape((rows, width), BF16), INNER),
        (shape((rows, width), BF16), INNER),
        (shape((16, width), F32), INNER),
        (shape((width, 3 * width), BF16), ANY),
        (shape(w_out.shape, BF16), ANY),
        (shape(w_up.shape, BF16), ANY),
        (shape(w_down.shape, BF16), ANY),
        (shape((HEADS_OWN, mid, HEAD), BF16), INNER),
        (shape((HEADS_OWN, seq_rows, HEAD), BF16), INNER),
        (shape((HEADS_OWN, seq_rows, HEAD), BF16), INNER),
        (shape((mid, third), F32), INNER),
        (shape((mid, 128), F32), INNER),
        (shape((HEADS_OWN, mid, seq_rows), BF16), ANY),
    ]
    dma = pltpu.SemaphoreType.DMA
    return pl.pallas_call(
        attend_kernel,
        out_shape=[o[0] for o in outs],
        in_specs=[INNER] * 4 + [ANY] * 4,
        out_specs=[o[1] for o in outs],
        scratch_shapes=[
            pltpu.VMEM((width, 3 * width), BF16),
            pltpu.VMEM((rows, 3 * width), F32),
            pltpu.VMEM((LINE, rows, 3 * third), BF16),
            pltpu.VMEM((mid, 3 * third), BF16),
            pltpu.VMEM((mid, 2 * third), BF16),
            pltpu.VMEM((LINE, rows, third), BF16),
            pltpu.VMEM((LINE, rows, third), BF16),
            pltpu.VMEM((HEADS_OWN, mid, seq_rows), BF16),
            dma((2,)),
            dma((LINE,)),
            dma((5,)),
            dma((5,)),
            dma((3,)),
            dma((3,)),
            dma((LINE,)),
            dma((LINE,)),
            dma((3,)),
            dma((3,)),
            dma((1,)),
            dma((1,)),
        ],
        compiler_params=pltpu.CompilerParams(
            collective_id=1, has_side_effects=True, vmem_limit_bytes=50 << 20
        ),
        name="attend_forward",
    )(tok, ids_row, ids_col, vec, w_qkv, w_out, w_up, w_down)


def token_kernel(
    attended,
    tok,
    grad_out,
    vec,
    w_out,
    out_other,
    w_up,
    up_other,
    w_down,
    down_other,
    result,
    normed_o,
    act_halves,
    up_halves,
    ffn_o,
    first_o,
    branch_halves,
    att_grads,
    vec_grads,
    out_all,
    up_all,
    down_all,
    active,
    slope,
    sem,
):
    core = lax.axis_index("fsdp")
    rows, width = tok.shape
    hidden_units = up_all.shape[1]
    third = HEADS_OWN * HEAD

    def place_of(which, size):
        return pl.ds(pl.multiple_of(which * size, 128), size)

    loads = []
    for i, (own, far, full) in enumerate(
        ((w_out, out_other, out_all), (w_up, up_other, up_all), (w_down, down_other, down_all))
    ):
        size = own.shape[0]
        loads.append(
            (
                pltpu.make_async_copy(own, full.at[place_of(core, size)], sem.at[2 * i]),
                pltpu.make_async_copy(far, full.at[place_of(1 - core, size)], sem.at[2 * i + 1]),
            )
        )
    for pair in loads:
        for load in pair:
            load.start()

    def arrived(i):
        for load in loads[i]:
            load.wait()

    bias_out, gain_one, shift_one = vec[2:3], vec[3:4], vec[4:5]
    bias_down, gain_two, shift_two = vec[5:6], vec[6:7], vec[7:8]
    arrived(0)
    branch = dot_nn(attended[...], out_all[...]) + bias_out
    normed_one, norm_one, scale_one = norm_forward(tok[...].astype(F32) + branch, gain_one, shift_one)
    normed_b = normed_one.astype(BF16)
    normed_o[...] = normed_b
    arrived(1)
    step = width
    half = width // 2
    for c in range(hidden_units // step):
        at, row = (c // 2) * half, 8 + 2 * (c % 2)
        bias = jnp.concatenate([vec[row : row + 1, at : at + half], vec[row + 1 : row + 2, at : at + half]], axis=1)
        up = dot_nn(normed_b, up_all[:, c * step : (c + 1) * step]) + bias
        cdf = 0.5 * (1.0 + lax.erf(up * 0.7071067811865476))
        active[:, c * step : (c + 1) * step] = (up * cdf).astype(BF16)
        slope[:, c * step : (c + 1) * step] = cdf + up * (
            0.3989422804014327 * jnp.exp(-0.5 * up * up)
        )
    arrived(2)
    second = normed_one + bias_down
    second += dot_nn(active[...], down_all[...])
    final, norm_two, scale_two = norm_forward(second, gain_two, shift_two)
    result[...] = final.astype(BF16)
    grad_second, gain_grad, shift_grad = norm_backward(
        grad_out[...].astype(F32), norm_two, scale_two, gain_two
    )
    grad_ffn = grad_second.astype(BF16)
    ffn_o[...] = grad_ffn
    vec_grads[...] = jnp.zeros(vec_grads.shape, F32)
    vec_grads[3:4] = jnp.sum(grad_ffn.astype(F32), axis=0, keepdims=True)
    vec_grads[4:5] = gain_grad[None]
    vec_grads[5:6] = shift_grad[None]
    grad_normed = grad_second
    piece = hidden_units // (8 * LINE)
    for c in range(hidden_units // step):
        span = slice(c * step, (c + 1) * step)
        grad_up = (dot_nt(grad_ffn, down_all[span]) * slope[:, span]).astype(BF16)
        vec_grads[8 + c : 9 + c] = jnp.sum(grad_up.astype(F32), axis=0, keepdims=True)
        grad_normed += dot_nt(grad_up, up_all[:, span])
        up_halves[c // 2, :, (c % 2) * step : (c % 2 + 1) * step] = grad_up
    for j in range(4 * LINE):
        for g in range(2):
            at = (2 * j + g) * piece
            act_halves[g, :, j * piece : (j + 1) * piece] = active[:, at : at + piece]
    grad_first, gain_grad, shift_grad = norm_backward(grad_normed, norm_one, scale_one, gain_one)
    first_o[...] = grad_first
    vec_grads[1:2] = gain_grad[None]
    vec_grads[2:3] = shift_grad[None]
    grad_branch = grad_first.astype(BF16)
    vec_grads[0:1] = jnp.sum(grad_branch.astype(F32), axis=0, keepdims=True)
    for g in range(2):
        branch_halves[g] = grad_branch[:, g * half : (g + 1) * half]
    grad_att = dot_nt(grad_branch, out_all[...]).astype(BF16)
    for d in range(LINE):
        att_grads[d] = grad_att[:, d * third : (d + 1) * third]


def token_local(attended, tok, grad_out, vec, w_out, out_other, w_up, up_other, w_down, down_other):
    rows, width = tok.shape
    units = w_up.shape[1]
    shape = jax.ShapeDtypeStruct
    return pl.pallas_call(
        token_kernel,
        out_shape=[
            shape((rows, width), BF16),
            shape((rows, width), BF16),
            shape((2, rows, units // 2), BF16),
            shape((2, rows, units // 2), BF16),
            shape((rows, width), BF16),
            shape((rows, width), F32),
            shape((2, rows, width // 2), BF16),
            shape((LINE, rows, HEADS_OWN * HEAD), BF16),
            shape((16, width), F32),
        ],
        in_specs=[INNER] * 4 + [ANY] * 6,
        out_specs=[INNER] * 9,
        scratch_shapes=[
            pltpu.VMEM((width, width), BF16),
            pltpu.VMEM((width, units), BF16),
            pltpu.VMEM((units, width), BF16),
            pltpu.VMEM((rows, units), BF16),
            pltpu.VMEM((rows, units), F32),
            pltpu.SemaphoreType.DMA((6,)),
        ],
        compiler_params=pltpu.CompilerParams(vmem_limit_bytes=50 << 20),
        name="token_local",
    )(attended, tok, grad_out, vec, w_out, out_other, w_up, up_other, w_down, down_other)


def attend_grad_kernel(
    att_grads,
    q_heads,
    k_heads,
    v_heads,
    att_full,
    totals,
    grad_first,
    probs_in,
    w_full,
    normed_b,
    act_halves,
    up_halves,
    grad_ffn,
    attended,
    branch_halves,
    grad_hidden,
    mixed_halves,
    vec_grads,
    normed_pair,
    act_pair,
    up_pair,
    ffn_pair,
    att_pair,
    branch_pair,
    mixed_pair,
    w_all,
    probs,
    grad_land,
    scaled,
    score_grads,
    query_grads,
    kv_own,
    kv_sent,
    kv_pair,
    kv_sum,
    kv_land,
    query_land,
    mixed,
    local_sem,
    line_out,
    line_in,
    pair_out,
    pair_in,
    back_out,
    back_in,
    seq_out,
    seq_in,
):
    place = lax.axis_index("ctx")
    group = lax.axis_index("seq")
    line, side = place // 2, place % 2
    to_pair = {"ctx": place + 1 - 2 * side}
    to_seq = {"seq": 1 - group}
    rows, width = grad_hidden.shape
    third = HEADS_OWN * HEAD
    mid = LINE * rows

    def ahead(k):
        return lax.rem(line + k, LINE)

    def behind(k):
        return lax.rem(line + LINE - k, LINE)

    def to_line(k):
        return {"ctx": 2 * ahead(k) + side}

    def block(which):
        return pl.ds(pl.multiple_of(which * rows, 32), rows)

    probs_load = pltpu.make_async_copy(probs_in, probs, local_sem.at[0])
    w_load = pltpu.make_async_copy(w_full, w_all, local_sem.at[1])
    probs_load.start()
    greet([to_pair, to_seq] + [to_line(k) for k in range(1, LINE)])

    def line_copy(k):
        return remote(
            att_grads.at[ahead(k)],
            grad_land.at[block(line)],
            line_out.at[k - 1],
            line_in.at[k - 1],
            to_line(k),
        )

    def line_landed(k):
        return remote(
            att_grads.at[ahead(k)],
            grad_land.at[block(behind(k))],
            line_out.at[k - 1],
            line_in.at[k - 1],
            to_line(k),
        )

    for k in (3, 2, 1):
        line_copy(k).start()
    seq_copies = []
    for i, (src, dst) in enumerate(
        (
            (normed_b, normed_pair),
            (up_halves.at[1 - group], up_pair),
            (act_halves.at[1 - group], act_pair),
            (grad_ffn, ffn_pair),
            (attended, att_pair),
            (branch_halves.at[1 - group], branch_pair),
            (mixed_halves.at[1 - group], mixed_pair),
        )
    ):
        seq_copies.append(remote(src, dst, seq_out.at[i], seq_in.at[i], to_seq))
    for copy in seq_copies[:-1]:
        copy.start()
    w_load.start()
    grad_land[block(line)] = att_grads[line]
    for k in (1, 2, 3):
        line_landed(k).wait_recv()
    probs_load.wait()

    def pair_copy(h):
        return remote(kv_sent.at[h], kv_pair.at[h], pair_out.at[h], pair_in.at[h], to_pair)

    for h in range(HEADS_OWN):
        lanes = slice(h * HEAD, (h + 1) * HEAD)

        def row_grads(i, carry, h=h, lanes=lanes):
            where = block(i)
            incoming = grad_land[where, lanes].astype(F32)
            row_total = totals[where, h : h + 1]
            delta = jnp.sum(incoming * att_full[where, lanes], axis=-1, keepdims=True)
            grad_scaled = (incoming / row_total).astype(BF16)
            scaled[where] = grad_scaled
            weights = dot_nt(grad_scaled, v_heads[h])
            ds = (probs[h, where].astype(F32) * (weights - delta / row_total)).astype(BF16)
            score_grads[where] = ds
            query_grads[where, lanes] = (dot_nn(ds, k_heads[h]) * 0.125).astype(BF16)
            return carry

        lax.fori_loop(0, LINE, row_grads, 0)
        both = jnp.concatenate(
            [dot_tn(q_heads[h], score_grads[...]) * 0.125, dot_tn(scaled[...], probs[h])], axis=0
        )
        both = jnp.transpose(both)
        kv_sent[h] = both[mid:].astype(BF16)
        pair_copy(h).start()
        kv_own[h] = both[:mid]

    def query_back(k):
        return remote(
            query_grads.at[block(ahead(k))],
            query_land.at[line],
            back_out.at[HEADS_OWN, k - 1],
            back_in.at[HEADS_OWN, k - 1],
            to_line(k),
        )

    def query_landed(k):
        return remote(
            query_grads.at[block(ahead(k))],
            query_land.at[behind(k)],
            back_out.at[HEADS_OWN, k - 1],
            back_in.at[HEADS_OWN, k - 1],
            to_line(k),
        )

    def kv_back(h, k):
        return remote(
            kv_sum.at[h, block(ahead(k))],
            kv_land.at[h, line],
            back_out.at[h, k - 1],
            back_in.at[h, k - 1],
            to_line(k),
        )

    def kv_landed(h, k):
        return remote(
            kv_sum.at[h, block(ahead(k))],
            kv_land.at[h, behind(k)],
            back_out.at[h, k - 1],
            back_in.at[h, k - 1],
            to_line(k),
        )

    for k in (3, 2, 1):
        query_back(k).start()
    query_land[line] = query_grads[block(line)]
    for h in range(HEADS_OWN):
        pair_copy(h).wait_recv()
        kv_sum[h] = (kv_own[h] + kv_pair[h].astype(F32)).astype(BF16)
        for k in (3, 2, 1):
            kv_back(h, k).start()
        kv_land[h, line] = kv_sum[h, block(line)]
    for k in (1, 2, 3):
        query_landed(k).wait_recv()
    for d in range(LINE):
        mixed[:, d * third : (d + 1) * third] = query_land[d]
    for h in range(HEADS_OWN):
        for k in (1, 2, 3):
            kv_landed(h, k).wait_recv()
        for d in range(LINE):
            at = width + d * third + h * HEAD
            mixed[:, at : at + HEAD] = kv_land[h, d, :, 0:HEAD]
            mixed[:, width + at : width + at + HEAD] = kv_land[h, d, :, HEAD:]
    middle = 3 * width // 2
    for g in range(2):
        mixed_halves[g] = mixed[:, g * middle : (g + 1) * middle]
    seq_copies[-1].start()
    w_load.wait()
    grad_hidden[...] = grad_first[...] + dot_nt(mixed[...], w_all[...])
    vec_grads[...] = jnp.zeros(vec_grads.shape, F32)
    vec_grads[0:1] = jnp.sum(mixed[:, :width].astype(F32), axis=0, keepdims=True)
    vec_grads[1:2] = jnp.sum(mixed[:, 2 * width :].astype(F32), axis=0, keepdims=True)
    for k in (1, 2, 3):
        line_copy(k).wait_send()
        query_back(k).wait_send()
        for h in range(HEADS_OWN):
            kv_back(h, k).wait_send()
    for h in range(HEADS_OWN):
        pair_copy(h).wait_send()
    for copy in seq_copies:
        copy.wait()


def attend_backward(*args):
    rows, width = args[6].shape
    units = args[10].shape[2]
    third = HEADS_OWN * HEAD
    mid, seq_rows = LINE * rows, 2 * LINE * rows
    shape = jax.ShapeDtypeStruct
    outs = [
        (shape((rows, width), F32), INNER),
        (shape((2, rows, 3 * width // 2), BF16), INNER),
        (shape((8, width), F32), INNER),
        (shape((rows, width), BF16), ANY),
        (shape((rows, units), BF16), ANY),
        (shape((rows, units), BF16), ANY),
        (shape((rows, width), BF16), ANY),
        (shape((rows, width), BF16), ANY),
        (shape((rows, width // 2), BF16), ANY),
        (shape((rows, 3 * width // 2), BF16), ANY),
    ]
    dma = pltpu.SemaphoreType.DMA
    return pl.pallas_call(
        attend_grad_kernel,
        out_shape=[o[0] for o in outs],
        in_specs=[INNER] * 7 + [ANY] * 8,
        out_specs=[o[1] for o in outs],
        scratch_shapes=[
            pltpu.VMEM((width, 3 * width), BF16),
            pltpu.VMEM((HEADS_OWN, mid, seq_rows), BF16),
            pltpu.VMEM((mid, third), BF16),
            pltpu.VMEM((mid, HEAD), BF16),
            pltpu.VMEM((mid, seq_rows), BF16),
            pltpu.VMEM((mid, third), BF16),
            pltpu.VMEM((HEADS_OWN, mid, 128), F32),
            pltpu.VMEM((HEADS_OWN, mid, 128), BF16),
            pltpu.VMEM((HEADS_OWN, mid, 128), BF16),
            pltpu.VMEM((HEADS_OWN, mid, 128), BF16),
            pltpu.VMEM((HEADS_OWN, LINE, rows, 128), BF16),
            pltpu.VMEM((LINE, rows, third), BF16),
            pltpu.VMEM((rows, 3 * width), BF16),
            dma((2,)),
            dma((3,)),
            dma((3,)),
            dma((3,)),
            dma((3,)),
            dma((4, 3)),
            dma((4, 3)),
            dma((7,)),
            dma((7,)),
        ],
        compiler_params=pltpu.CompilerParams(
            collective_id=2, has_side_effects=True, vmem_limit_bytes=50 << 20
        ),
        name="attend_backward",
    )(*args)


def block_device(
    hidden,
    segment_ids,
    out_grad,
    w_qkv,
    bias_query,
    bias_value,
    w_out,
    bias_out,
    gain_one,
    shift_one,
    w_up,
    bias_up,
    w_down,
    bias_down,
    gain_two,
    shift_two,
):
    tok, grad_out = hidden[0], out_grad[0]
    rows, width = tok.shape
    half = width // 2
    side = lax.axis_index("ctx") % 2
    ids = segment_ids[0].reshape(LINE, 2, rows)
    own_ids = lax.dynamic_index_in_dim(ids, side, 1, False).reshape(-1)
    far_ids = lax.dynamic_index_in_dim(ids, 1 - side, 1, False).reshape(-1)
    ids_row = jnp.concatenate([own_ids, far_ids])[None, :]
    ids_col = own_ids[:, None]
    small = [
        bias_query,
        bias_value,
        bias_out,
        gain_one,
        shift_one,
        bias_down,
        gain_two,
        shift_two,
        bias_up,
    ]
    vec = jnp.concatenate([v.reshape(-1, half) for v in small], axis=0).astype(F32)
    vec = jnp.pad(vec, ((0, 16 - vec.shape[0]), (0, 0)))
    (
        attended,
        tok_pair,
        vec_all,
        w_full,
        out_other,
        up_other,
        down_other,
        q_heads,
        k_heads,
        v_heads,
        att_full,
        totals,
        probs,
    ) = attend_forward(tok, ids_row, ids_col, vec, w_qkv, w_out, w_up, w_down)
    (
        result,
        normed_b,
        act_halves,
        up_halves,
        grad_ffn,
        grad_first,
        branch_halves,
        att_grads,
        vec_one,
    ) = token_local(
        attended, tok, grad_out, vec_all, w_out, out_other, w_up, up_other, w_down, down_other
    )
    (
        grad_hidden,
        mixed_halves,
        vec_two,
        normed_pair,
        act_pair,
        up_pair,
        ffn_pair,
        att_pair,
        branch_pair,
        mixed_pair,
    ) = attend_backward(
        att_grads,
        q_heads,
        k_heads,
        v_heads,
        att_full,
        totals,
        grad_first,
        probs,
        w_full,
        normed_b,
        act_halves,
        up_halves,
        grad_ffn,
        attended,
        branch_halves,
    )
    vectors = [
        vec_two[0],
        vec_two[1],
        vec_one[0],
        vec_one[1],
        vec_one[2],
        vec_one[8:12].reshape(-1),
        vec_one[3],
        vec_one[4],
        vec_one[5],
    ]
    packed = jnp.concatenate([v.reshape(16, -1) for v in vectors], axis=1)
    packed = jnp.pad(packed, ((0, 0), (0, 1024 - packed.shape[1])))
    packed = jnp.transpose(packed.reshape(LINE, 2, 2, 8, 128), (2, 0, 1, 3, 4))
    up_own, down_own, qkv_own, out_own, vec_own = weight_grads(
        [
            (normed_b, normed_pair, up_halves, up_pair),
            (act_halves, act_pair, grad_ffn, ffn_pair),
            (tok, tok_pair, mixed_halves, mixed_pair),
            (attended, att_pair, branch_halves, branch_pair),
        ],
        packed,
    )
    flat = vec_own.reshape(-1)
    summed, at = [], 0
    for v in vectors:
        summed.append(lax.slice_in_dim(flat, at, at + v.shape[0] // 16))
        at += v.shape[0] // 16
    return (
        result[None],
        grad_hidden[None],
        qkv_own.astype(F32),
        summed[0],
        summed[1],
        out_own.astype(F32),
        summed[2],
        summed[3],
        summed[4],
        up_own.astype(F32),
        summed[5],
        down_own.astype(F32),
        summed[6],
        summed[7],
        summed[8],
    )


def solution(mesh):
    small = (mesh.shape["seq"], mesh.shape["ctx"], mesh.shape["fsdp"]) == (2, 8, 2)
    return jax.shard_map(
        block_device if small else on_device,
        mesh=mesh,
        in_specs=(
            P(("seq", "fsdp"), "ctx", None),
            P(("seq", "fsdp"), None),
            P(("seq", "fsdp"), "ctx", None),
            P("fsdp", None),
            P("fsdp"),
            P("fsdp"),
            P("fsdp", None),
            P("fsdp"),
            P("fsdp"),
            P("fsdp"),
            P("fsdp", None),
            P("fsdp"),
            P("fsdp", None),
            P("fsdp"),
            P("fsdp"),
            P("fsdp"),
        ),
        out_specs=(
            P(("seq", "fsdp"), "ctx", None),
            P(("seq", "fsdp"), "ctx", None),
            P(("ctx", "fsdp"), None),
            P(("ctx", "fsdp")),
            P(("ctx", "fsdp")),
            P(("ctx", "fsdp"), None),
            P(("ctx", "fsdp")),
            P(("ctx", "fsdp")),
            P(("ctx", "fsdp")),
            P(("ctx", "fsdp"), None),
            P(("ctx", "fsdp")),
            P(("ctx", "fsdp"), None),
            P(("ctx", "fsdp")),
            P(("ctx", "fsdp")),
            P(("ctx", "fsdp")),
        ),
        check_vma=False,
    )
```

```python
import functools

import jax
import jax.numpy as jnp
from jax import lax
from jax.experimental import pallas as pl
from jax.experimental.pallas import tpu as pltpu
from jax.sharding import PartitionSpec as P

HEAD = 64


EPSILON = 1e-12
NEGATIVE = -1e30
LOG_TWO = 0.6931471805599453
LOG2_E = 1.4426950408889634


def norm_forward(rows_in, gain_vec, shift_vec):
    row_mean = jnp.mean(rows_in, axis=-1, keepdims=True)
    centered = rows_in - row_mean
    variance = jnp.mean(centered * centered, axis=-1, keepdims=True)
    scaled = lax.rsqrt(variance + EPSILON)
    normed = centered * scaled
    return (normed * gain_vec + shift_vec, normed, scaled)


def norm_backward(grad_rows, normed, scaled, gain_vec):
    grad_normed = grad_rows * gain_vec
    inner_part = (
        grad_normed
        - jnp.mean(grad_normed, axis=-1, keepdims=True)
        - normed * jnp.mean(grad_normed * normed, axis=-1, keepdims=True)
    )
    return (inner_part * scaled, jnp.sum(grad_rows * normed, axis=0), jnp.sum(grad_rows, axis=0))


def head_scores(query_heads, key_heads):
    return (
        jnp.einsum("qhd,khd->hqk", query_heads, key_heads, preferred_element_type=jnp.float32)
        * 0.125
    )


def column_sums(rows_b):
    return jnp.sum(rows_b.astype(jnp.float32), axis=0)


def sweep(steps_total, advance, start_carry):

    def advance_one(running, block_index):
        running = advance(running, block_index)
        return (running, None)

    return lax.scan(advance_one, start_carry, jnp.arange(steps_total))[0]


def local_grads(scores, allowed, shift_rows, ratio_rows, grad_heads, value_heads):
    unnorm = jnp.where(allowed, jnp.exp(scores - shift_rows[..., None]), 0.0)
    grad_weights = jnp.einsum(
        "qhd,khd->hqk", grad_heads, value_heads, preferred_element_type=jnp.float32
    )
    grad_scores = (unnorm * (grad_weights - ratio_rows[..., None])).astype(jnp.bfloat16)
    return (unnorm.astype(jnp.bfloat16), grad_scores)


def on_device(
    hidden,
    segment_ids,
    out_grad,
    w_qkv,
    bias_query,
    bias_value,
    w_out,
    bias_out,
    gain_one,
    shift_one,
    w_up,
    bias_up,
    w_down,
    bias_down,
    gain_two,
    shift_two,
):
    (
        w_qkv,
        bias_query,
        bias_value,
        w_out,
        bias_out,
        gain_one,
        shift_one,
        w_up,
        bias_up,
        w_down,
        bias_down,
        gain_two,
        shift_two,
    ) = (
        lax.all_gather(w_qkv, "fsdp", axis=0, tiled=True),
        lax.all_gather(bias_query, "fsdp", axis=0, tiled=True),
        lax.all_gather(bias_value, "fsdp", axis=0, tiled=True),
        lax.all_gather(w_out, "fsdp", axis=0, tiled=True),
        lax.all_gather(bias_out, "fsdp", axis=0, tiled=True),
        lax.all_gather(gain_one, "fsdp", axis=0, tiled=True),
        lax.all_gather(shift_one, "fsdp", axis=0, tiled=True),
        lax.all_gather(w_up, "fsdp", axis=0, tiled=True),
        lax.all_gather(bias_up, "fsdp", axis=0, tiled=True),
        lax.all_gather(w_down, "fsdp", axis=0, tiled=True),
        lax.all_gather(bias_down, "fsdp", axis=0, tiled=True),
        lax.all_gather(gain_two, "fsdp", axis=0, tiled=True),
        lax.all_gather(shift_two, "fsdp", axis=0, tiled=True),
    )
    f32 = jnp.float32
    bf16 = jnp.bfloat16
    tokens = hidden[0]
    tok_rows = tokens.shape[0]
    model_width = tokens.shape[1]
    head_count = model_width // HEAD
    seq_rows = tok_rows * lax.axis_size("ctx")
    key_span = 4 * tok_rows
    block_total = seq_rows // key_span
    doc_ids = segment_ids[0]
    own_ids = lax.dynamic_slice_in_dim(doc_ids, lax.axis_index("ctx") * tok_rows, tok_rows)
    mixed_rows = jnp.dot(tokens, w_qkv, preferred_element_type=f32)
    query_rows = (mixed_rows[:, :model_width] + bias_query.astype(f32)).astype(bf16)
    key_value = jnp.concatenate(
        [
            mixed_rows[:, model_width : 2 * model_width],
            mixed_rows[:, 2 * model_width :] + bias_value.astype(f32),
        ],
        axis=1,
    ).astype(bf16)
    all_kv = lax.all_gather(key_value, "ctx", axis=0, tiled=True)
    query_heads = query_rows.reshape(tok_rows, head_count, HEAD)

    def key_block(block_index):
        kv_piece = lax.dynamic_slice_in_dim(all_kv, block_index * key_span, key_span, 0)
        key_ids = lax.dynamic_slice_in_dim(doc_ids, block_index * key_span, key_span)
        return (
            kv_piece[:, :model_width].reshape(key_span, head_count, HEAD),
            kv_piece[:, model_width:].reshape(key_span, head_count, HEAD),
            key_ids,
        )

    def forward_step(running, block_index):
        level_run, total_run, sum_run = running
        key_heads, value_heads, key_ids = key_block(block_index)
        allowed = (own_ids[:, None] == key_ids[None, :])[None]
        scores = jnp.where(allowed, head_scores(query_heads, key_heads), NEGATIVE)
        level_new = jnp.maximum(level_run, jnp.ceil(jnp.max(scores, axis=-1) * LOG2_E))
        rescale = jnp.exp(LOG_TWO * (level_run - level_new))
        unnorm = jnp.where(allowed, jnp.exp(scores - (LOG_TWO * level_new)[..., None]), 0.0)
        total_new = total_run * rescale + jnp.sum(unnorm, axis=-1)
        sum_new = sum_run * jnp.transpose(rescale)[:, :, None] + jnp.einsum(
            "hqk,khd->qhd", unnorm.astype(bf16), value_heads, preferred_element_type=f32
        )
        return (level_new, total_new, sum_new)

    start_state = (
        jnp.full((head_count, tok_rows), NEGATIVE, f32),
        jnp.zeros((head_count, tok_rows), f32),
        jnp.zeros((tok_rows, head_count, HEAD), f32),
    )
    level_end, row_total, raw_sum = sweep(block_total, forward_step, start_state)
    row_shift = LOG_TWO * level_end
    att_sum = raw_sum / jnp.transpose(row_total)[:, :, None]
    attended = att_sum.reshape(tok_rows, model_width).astype(bf16)
    branch = jnp.dot(attended, w_out, preferred_element_type=f32) + bias_out.astype(f32)
    normed_one, norm_one, scale_one = norm_forward(
        tokens.astype(f32) + branch, gain_one.astype(f32), shift_one.astype(f32)
    )
    normed_b = normed_one.astype(bf16)
    up_rows = jnp.dot(normed_b, w_up, preferred_element_type=f32) + bias_up.astype(f32)
    active, gelu_back = jax.vjp(lambda pre_act: jax.nn.gelu(pre_act, approximate=False), up_rows)
    active_b = active.astype(bf16)
    second = (
        normed_one + jnp.dot(active_b, w_down, preferred_element_type=f32) + bias_down.astype(f32)
    )
    result, norm_two, scale_two = norm_forward(second, gain_two.astype(f32), shift_two.astype(f32))
    grad_second, grad_gain_two, grad_shift_two = norm_backward(
        out_grad[0].astype(f32), norm_two, scale_two, gain_two.astype(f32)
    )
    grad_ffn = grad_second.astype(bf16)
    grad_bias_down = column_sums(grad_ffn)
    grad_w_down = jnp.dot(active_b.T, grad_ffn, preferred_element_type=f32)
    grad_active = jnp.dot(grad_ffn, w_down.T, preferred_element_type=f32)
    grad_up = gelu_back(grad_active)[0].astype(bf16)
    grad_bias_up = column_sums(grad_up)
    grad_w_up = jnp.dot(normed_b.T, grad_up, preferred_element_type=f32)
    grad_normed = grad_second + jnp.dot(grad_up, w_up.T, preferred_element_type=f32)
    grad_first, grad_gain_one, grad_shift_one = norm_backward(
        grad_normed, norm_one, scale_one, gain_one.astype(f32)
    )
    grad_branch = grad_first.astype(bf16)
    grad_bias_out = column_sums(grad_branch)
    grad_w_out = jnp.dot(attended.T, grad_branch, preferred_element_type=f32)
    grad_attended = jnp.dot(grad_branch, w_out.T, preferred_element_type=f32).astype(bf16)
    grad_att_f32 = grad_attended.reshape(tok_rows, head_count, HEAD).astype(f32)
    delta = jnp.einsum("qhd,qhd->hq", grad_att_f32, att_sum)
    delta_ratio = delta / row_total
    grad_scaled = (grad_att_f32 / jnp.transpose(row_total)[:, :, None]).astype(bf16)
    zero_query = jnp.zeros((tok_rows, head_count, HEAD), f32)

    def full_step(running, block_index):
        grad_query, grad_kv = running
        key_heads, value_heads, key_ids = key_block(block_index)
        allowed = (own_ids[:, None] == key_ids[None, :])[None]
        unnorm_b, grad_scores = local_grads(
            head_scores(query_heads, key_heads),
            allowed,
            row_shift,
            delta_ratio,
            grad_scaled,
            value_heads,
        )
        grad_query = (
            grad_query
            + jnp.einsum("hqk,khd->qhd", grad_scores, key_heads, preferred_element_type=f32) * 0.125
        )
        grad_keys = (
            jnp.einsum("hqk,qhd->khd", grad_scores, query_heads, preferred_element_type=f32) * 0.125
        )
        grad_values = jnp.einsum("hqk,qhd->khd", unnorm_b, grad_scaled, preferred_element_type=f32)
        both_grads = jnp.concatenate(
            [grad_keys.reshape(key_span, model_width), grad_values.reshape(key_span, model_width)],
            axis=1,
        )
        grad_kv = lax.dynamic_update_slice_in_dim(grad_kv, both_grads, block_index * key_span, 0)
        return (grad_query, grad_kv)

    start_full = (zero_query, jnp.zeros((seq_rows, 2 * model_width), f32))
    grad_query, grad_kv = sweep(block_total, full_step, start_full)
    own_kv = lax.psum_scatter(grad_kv, "ctx", scatter_dimension=0, tiled=True)
    grad_query_b = grad_query.reshape(tok_rows, model_width).astype(bf16)
    grad_kv_b = own_kv.astype(bf16)
    grad_mixed = jnp.concatenate([grad_query_b, grad_kv_b], axis=1)
    grad_tokens = grad_first + jnp.dot(grad_mixed, w_qkv.T, preferred_element_type=f32)
    grad_w_qkv = jnp.dot(tokens.T, grad_mixed, preferred_element_type=f32)
    grad_bias_query = column_sums(grad_query_b)
    grad_bias_value = column_sums(grad_kv_b[:, model_width:])
    shares = (
        lax.psum_scatter(grad_w_qkv, ("ctx", "fsdp"), scatter_dimension=0, tiled=True),
        lax.psum_scatter(grad_bias_query, ("ctx", "fsdp"), scatter_dimension=0, tiled=True),
        lax.psum_scatter(grad_bias_value, ("ctx", "fsdp"), scatter_dimension=0, tiled=True),
        lax.psum_scatter(grad_w_out, ("ctx", "fsdp"), scatter_dimension=0, tiled=True),
        lax.psum_scatter(grad_bias_out, ("ctx", "fsdp"), scatter_dimension=0, tiled=True),
        lax.psum_scatter(grad_gain_one, ("ctx", "fsdp"), scatter_dimension=0, tiled=True),
        lax.psum_scatter(grad_shift_one, ("ctx", "fsdp"), scatter_dimension=0, tiled=True),
        lax.psum_scatter(grad_w_up, ("ctx", "fsdp"), scatter_dimension=0, tiled=True),
        lax.psum_scatter(grad_bias_up, ("ctx", "fsdp"), scatter_dimension=0, tiled=True),
        lax.psum_scatter(grad_w_down, ("ctx", "fsdp"), scatter_dimension=0, tiled=True),
        lax.psum_scatter(grad_bias_down, ("ctx", "fsdp"), scatter_dimension=0, tiled=True),
        lax.psum_scatter(grad_gain_two, ("ctx", "fsdp"), scatter_dimension=0, tiled=True),
        lax.psum_scatter(grad_shift_two, ("ctx", "fsdp"), scatter_dimension=0, tiled=True),
    )
    summed = (
        lax.psum(shares[0].astype(jnp.bfloat16), "seq").astype(jnp.float32),
        lax.psum(shares[1].astype(jnp.bfloat16), "seq").astype(jnp.float32),
        lax.psum(shares[2].astype(jnp.bfloat16), "seq").astype(jnp.float32),
        lax.psum(shares[3].astype(jnp.bfloat16), "seq").astype(jnp.float32),
        lax.psum(shares[4].astype(jnp.bfloat16), "seq").astype(jnp.float32),
        lax.psum(shares[5].astype(jnp.bfloat16), "seq").astype(jnp.float32),
        lax.psum(shares[6].astype(jnp.bfloat16), "seq").astype(jnp.float32),
        lax.psum(shares[7].astype(jnp.bfloat16), "seq").astype(jnp.float32),
        lax.psum(shares[8].astype(jnp.bfloat16), "seq").astype(jnp.float32),
        lax.psum(shares[9].astype(jnp.bfloat16), "seq").astype(jnp.float32),
        lax.psum(shares[10].astype(jnp.bfloat16), "seq").astype(jnp.float32),
        lax.psum(shares[11].astype(jnp.bfloat16), "seq").astype(jnp.float32),
        lax.psum(shares[12].astype(jnp.bfloat16), "seq").astype(jnp.float32),
    )
    return (
        result.astype(bf16)[None],
        grad_tokens[None],
        summed[0],
        summed[1],
        summed[2],
        summed[3],
        summed[4],
        summed[5],
        summed[6],
        summed[7],
        summed[8],
        summed[9],
        summed[10],
        summed[11],
        summed[12],
    )


MESH_ID = pl.DeviceIdType.MESH
LINE = 4


def remote(src, dst, send, recv, target):
    return pltpu.make_async_remote_copy(
        src_ref=src,
        dst_ref=dst,
        send_sem=send,
        recv_sem=recv,
        device_id=target,
        device_id_type=MESH_ID,
    )


HEADS_OWN = 3
F32 = jnp.float32
BF16 = jnp.bfloat16
ANY = pl.BlockSpec(memory_space=pl.ANY)
INNER = pl.BlockSpec(memory_space=pltpu.VMEM)


def dot_nt(a, b):
    return lax.dot_general(a, b, (((1,), (1,)), ((), ())), preferred_element_type=F32)


def dot_tn(a, b):
    return lax.dot_general(a, b, (((0,), (0,)), ((), ())), preferred_element_type=F32)


def dot_nn(a, b):
    return lax.dot_general(a, b, (((1,), (0,)), ((), ())), preferred_element_type=F32)


def greet(targets):
    barrier = pltpu.get_barrier_semaphore()
    for target in targets:
        pl.semaphore_signal(barrier, inc=1, device_id=target, device_id_type=MESH_ID)
    pl.semaphore_wait(barrier, len(targets))


def attend_kernel(
    tok,
    ids,
    small,
    w_qkv,
    w_out,
    w_up,
    w_down,
    attended,
    tok_pair,
    vec_all,
    w_full,
    out_other,
    up_other,
    down_other,
    q_heads,
    k_heads,
    v_heads,
    att_full,
    totals,
    probs_out,
    w_all,
    mixed,
    sent,
    mine,
    other,
    att_sent,
    att_land,
    probs,
    vec,
    ids_row,
    ids_col,
    local_sem,
    probs_sem,
    core_out,
    core_in,
    line_out,
    line_in,
    pair_out,
    pair_in,
    back_out,
    back_in,
    seq_out,
    seq_in,
):
    place = lax.axis_index("ctx")
    core = lax.axis_index("fsdp")
    group = lax.axis_index("seq")
    line, side = place // 2, place % 2
    to_core = {"fsdp": 1 - core}
    to_pair = {"ctx": place + 1 - 2 * side}
    to_seq = {"seq": 1 - group}
    rows = tok.shape[0]
    width = tok.shape[1]
    half = width // 2
    third = HEADS_OWN * HEAD

    def ahead(k):
        return lax.rem(line + k, LINE)

    def behind(k):
        return lax.rem(line + LINE - k, LINE)

    def to_line(k):
        return {"ctx": 2 * ahead(k) + side}

    def block(which):
        return pl.ds(pl.multiple_of(which * rows, 32), rows)

    own_rows = pl.ds(pl.multiple_of(core * half, 128), half)
    other_rows = pl.ds(pl.multiple_of((1 - core) * half, 128), half)

    own_load = pltpu.make_async_copy(w_qkv, w_all.at[own_rows], local_sem.at[0])
    own_load.start()
    at = 0
    for piece in small:
        for first in range(0, piece.shape[0], half):
            vec[at : at + 1] = piece[first : first + half].astype(F32)[None]
            at += 1
    vec[at:] = jnp.zeros((vec.shape[0] - at, half), F32)
    greet([to_core, to_pair, to_seq] + [to_line(k) for k in range(1, LINE)])
    core_copies = [
        remote(w_qkv, w_all.at[own_rows], core_out.at[0], core_in.at[0], to_core),
        remote(vec, vec_all.at[:, own_rows], core_out.at[1], core_in.at[1], to_core),
        remote(w_out, out_other, core_out.at[2], core_in.at[2], to_core),
        remote(w_up, up_other, core_out.at[3], core_in.at[3], to_core),
        remote(w_down, down_other, core_out.at[4], core_in.at[4], to_core),
    ]
    seq_copy = remote(tok, tok_pair, seq_out.at[0], seq_in.at[0], to_seq)
    core_copies[0].start()
    core_copies[1].start()
    seq_copy.start()
    vec_all[:, own_rows] = vec[...]
    own_load.wait()
    step = width // 2
    for first in range(0, 3 * width, step):
        mixed[:, first : first + step] = dot_nn(
            tok[:, own_rows], w_all[own_rows, first : first + step]
        )
    core_copies[0].wait_recv()
    core_copies[1].wait_recv()
    for copy in core_copies[2:]:
        copy.start()
    bias = vec_all[...]
    for part in (1, 2, 0):
        for first in range(part * width, (part + 1) * width, step):
            total = mixed[:, first : first + step] + dot_nn(
                tok[:, other_rows], w_all[other_rows, first : first + step]
            )
            within = first - part * width
            if part == 0:
                total += bias[0:1, within : within + step]
            if part == 2:
                total += bias[1:2, within : within + step]
            total = total.astype(BF16)
            slot = (2, 0, 1)[part] * third
            for j in range(2):
                sent[within // third + j, :, slot : slot + third] = total[
                    :, j * third : (j + 1) * third
                ]

    def line_copy(k):
        return remote(
            sent.at[ahead(k)], mine.at[block(line)], line_out.at[k - 1], line_in.at[k - 1], to_line(k)
        )

    def line_landed(k):
        return remote(
            sent.at[ahead(k)],
            mine.at[block(behind(k))],
            line_out.at[k - 1],
            line_in.at[k - 1],
            to_line(k),
        )

    def pair_copy(k):
        where = block(behind(k))
        return remote(
            mine.at[where, 0 : 2 * third],
            other.at[where],
            pair_out.at[k],
            pair_in.at[k],
            to_pair,
        )

    for k in (3, 2, 1):
        line_copy(k).start()
    full_store = pltpu.make_async_copy(w_all, w_full, local_sem.at[1])
    full_store.start()
    mine[block(line)] = sent[line]
    pair_copy(0).start()
    for k in (1, 2, 3):
        line_landed(k).wait_recv()
        pair_copy(k).start()
    seq_rows = 2 * LINE * rows
    mid = LINE * rows
    for z in range(LINE):
        even = ids[:, 2 * z * rows : (2 * z + 1) * rows].astype(F32)
        odd = ids[:, (2 * z + 1) * rows : (2 * z + 2) * rows].astype(F32)
        ids_row[:, z * rows : (z + 1) * rows] = jnp.where(side == 0, even, odd)
        ids_row[:, mid + z * rows : mid + (z + 1) * rows] = jnp.where(side == 0, odd, even)
    ids_col[...] = jnp.transpose(jnp.broadcast_to(ids_row[:, 0:mid], (8, mid)))[:, 0:1]
    for h in range(HEADS_OWN):
        q_heads[h] = mine[:, 2 * third + h * HEAD : 2 * third + (h + 1) * HEAD]
        k_heads[h, 0:mid] = mine[:, h * HEAD : (h + 1) * HEAD]
        v_heads[h, 0:mid] = mine[:, third + h * HEAD : third + (h + 1) * HEAD]
    for k in range(LINE):
        pair_copy(k).wait_recv()
    for h in range(HEADS_OWN):
        k_heads[h, mid:seq_rows] = other[:, h * HEAD : (h + 1) * HEAD]
        v_heads[h, mid:seq_rows] = other[:, third + h * HEAD : third + (h + 1) * HEAD]

    def back_copy(k):
        return remote(
            att_sent.at[ahead(k)],
            att_land.at[line],
            back_out.at[k - 1],
            back_in.at[k - 1],
            to_line(k),
        )

    def back_landed(k):
        return remote(
            att_sent.at[ahead(k)],
            att_land.at[behind(k)],
            back_out.at[k - 1],
            back_in.at[k - 1],
            to_line(k),
        )

    def probs_copy(k):
        where = block(ahead(k))
        return pltpu.make_async_copy(
            probs.at[:, where], probs_out.at[:, where], probs_sem.at[k - 1]
        )

    def attend(k, carry):
        which = ahead(k)
        where = block(which)
        allowed = ids_col[where] == ids_row[...]
        for h in range(HEADS_OWN):
            scores = dot_nt(q_heads[h, where], k_heads[h]) * 0.125
            scores = jnp.where(allowed, scores, NEGATIVE)
            level = jnp.ceil(jnp.max(scores, axis=-1, keepdims=True) * LOG2_E)
            unnorm = jnp.exp(scores - LOG_TWO * level)
            row_total = jnp.sum(unnorm, axis=-1, keepdims=True)
            unnorm_b = unnorm.astype(BF16)
            probs[h, where] = unnorm_b
            value = dot_nn(unnorm_b, v_heads[h]) / row_total
            att_full[where, h * HEAD : (h + 1) * HEAD] = value
            totals[where, h : h + 1] = row_total
            att_sent[which, :, h * HEAD : (h + 1) * HEAD] = value.astype(BF16)
        probs_copy(k).start()

        @pl.when(k < LINE)
        def _():
            back_copy(k).start()

        return carry

    lax.fori_loop(1, LINE + 1, attend, 0)
    att_land[line] = att_sent[line]
    for k in (1, 2, 3):
        back_landed(k).wait_recv()
    for d in range(LINE):
        attended[:, d * third : (d + 1) * third] = att_land[d]
    for k in (1, 2, 3):
        line_copy(k).wait_send()
        back_copy(k).wait_send()
    for k in range(LINE):
        pair_copy(k).wait_send()
        probs_copy(k + 1).wait()
    for copy in core_copies[2:]:
        copy.wait_recv()
    for copy in core_copies:
        copy.wait_send()
    seq_copy.wait()
    full_store.wait()


def attend_forward(tok, ids, small, w_qkv, w_out, w_up, w_down):
    rows, width = tok.shape
    third = HEADS_OWN * HEAD
    mid, seq_rows = LINE * rows, 2 * LINE * rows
    shape = jax.ShapeDtypeStruct
    outs = [
        (shape((rows, width), BF16), INNER),
        (shape((rows, width), BF16), INNER),
        (shape((16, width), F32), INNER),
        (shape((width, 3 * width), BF16), ANY),
        (shape(w_out.shape, BF16), ANY),
        (shape(w_up.shape, BF16), ANY),
        (shape(w_down.shape, BF16), ANY),
        (shape((HEADS_OWN, mid, HEAD), BF16), INNER),
        (shape((HEADS_OWN, seq_rows, HEAD), BF16), INNER),
        (shape((HEADS_OWN, seq_rows, HEAD), BF16), INNER),
        (shape((mid, third), F32), INNER),
        (shape((mid, 128), F32), INNER),
        (shape((HEADS_OWN, mid, seq_rows), BF16), ANY),
    ]
    dma = pltpu.SemaphoreType.DMA
    return pl.pallas_call(
        attend_kernel,
        out_shape=[o[0] for o in outs],
        in_specs=[INNER, INNER, [INNER] * len(small)] + [ANY] * 4,
        out_specs=[o[1] for o in outs],
        scratch_shapes=[
            pltpu.VMEM((width, 3 * width), BF16),
            pltpu.VMEM((rows, 3 * width), F32),
            pltpu.VMEM((LINE, rows, 3 * third), BF16),
            pltpu.VMEM((mid, 3 * third), BF16),
            pltpu.VMEM((mid, 2 * third), BF16),
            pltpu.VMEM((LINE, rows, third), BF16),
            pltpu.VMEM((LINE, rows, third), BF16),
            pltpu.VMEM((HEADS_OWN, mid, seq_rows), BF16),
            pltpu.VMEM((16, width // 2), F32),
            pltpu.VMEM((1, seq_rows), F32),
            pltpu.VMEM((mid, 1), F32),
            dma((2,)),
            dma((LINE,)),
            dma((5,)),
            dma((5,)),
            dma((3,)),
            dma((3,)),
            dma((LINE,)),
            dma((LINE,)),
            dma((3,)),
            dma((3,)),
            dma((1,)),
            dma((1,)),
        ],
        compiler_params=pltpu.CompilerParams(
            collective_id=1, has_side_effects=True, vmem_limit_bytes=63 << 20
        ),
        name="attend_forward",
    )(tok, ids, small, w_qkv, w_out, w_up, w_down)


def token_kernel(
    attended,
    tok,
    grad_out,
    vec,
    w_out,
    out_other,
    w_up,
    up_other,
    w_down,
    down_other,
    result,
    normed_o,
    act_halves,
    up_halves,
    ffn_o,
    first_o,
    branch_halves,
    att_grads,
    vec_grads,
    out_all,
    up_all,
    down_all,
    active,
    slope,
    sem,
):
    core = lax.axis_index("fsdp")
    rows, width = tok.shape
    hidden_units = up_all.shape[1]
    third = HEADS_OWN * HEAD

    def place_of(which, size):
        return pl.ds(pl.multiple_of(which * size, 128), size)

    loads = []
    for i, (own, far, full) in enumerate(
        ((w_out, out_other, out_all), (w_up, up_other, up_all), (w_down, down_other, down_all))
    ):
        size = own.shape[0]
        loads.append(
            (
                pltpu.make_async_copy(own, full.at[place_of(core, size)], sem.at[2 * i]),
                pltpu.make_async_copy(far, full.at[place_of(1 - core, size)], sem.at[2 * i + 1]),
            )
        )
    for pair in loads:
        for load in pair:
            load.start()

    def arrived(i):
        for load in loads[i]:
            load.wait()

    bias_out, gain_one, shift_one = vec[2:3], vec[3:4], vec[4:5]
    bias_down, gain_two, shift_two = vec[5:6], vec[6:7], vec[7:8]
    arrived(0)
    branch = dot_nn(attended[...], out_all[...]) + bias_out
    normed_one, norm_one, scale_one = norm_forward(tok[...].astype(F32) + branch, gain_one, shift_one)
    normed_b = normed_one.astype(BF16)
    normed_o[...] = normed_b
    arrived(1)
    step = width
    half = width // 2
    for c in range(hidden_units // step):
        at, row = (c // 2) * half, 8 + 2 * (c % 2)
        bias = jnp.concatenate([vec[row : row + 1, at : at + half], vec[row + 1 : row + 2, at : at + half]], axis=1)
        up = dot_nn(normed_b, up_all[:, c * step : (c + 1) * step]) + bias
        cdf = 0.5 * (1.0 + lax.erf(up * 0.7071067811865476))
        active[:, c * step : (c + 1) * step] = (up * cdf).astype(BF16)
        slope[:, c * step : (c + 1) * step] = cdf + up * (
            0.3989422804014327 * jnp.exp(-0.5 * up * up)
        )
    arrived(2)
    second = normed_one + bias_down
    second += dot_nn(active[...], down_all[...])
    final, norm_two, scale_two = norm_forward(second, gain_two, shift_two)
    result[...] = final.astype(BF16)
    grad_second, gain_grad, shift_grad = norm_backward(
        grad_out[...].astype(F32), norm_two, scale_two, gain_two
    )
    grad_ffn = grad_second.astype(BF16)
    ffn_o[...] = grad_ffn
    vec_grads[...] = jnp.zeros(vec_grads.shape, F32)
    vec_grads[3:4] = jnp.sum(grad_ffn.astype(F32), axis=0, keepdims=True)
    vec_grads[4:5] = gain_grad[None]
    vec_grads[5:6] = shift_grad[None]
    grad_normed = grad_second
    piece = hidden_units // (8 * LINE)
    for c in range(hidden_units // step):
        span = slice(c * step, (c + 1) * step)
        grad_up = (dot_nt(grad_ffn, down_all[span]) * slope[:, span]).astype(BF16)
        vec_grads[8 + c : 9 + c] = jnp.sum(grad_up.astype(F32), axis=0, keepdims=True)
        grad_normed += dot_nt(grad_up, up_all[:, span])
        up_halves[c // 2, :, (c % 2) * step : (c % 2 + 1) * step] = grad_up
    for j in range(4 * LINE):
        for g in range(2):
            at = (2 * j + g) * piece
            act_halves[g, :, j * piece : (j + 1) * piece] = active[:, at : at + piece]
    grad_first, gain_grad, shift_grad = norm_backward(grad_normed, norm_one, scale_one, gain_one)
    first_o[...] = grad_first
    vec_grads[1:2] = gain_grad[None]
    vec_grads[2:3] = shift_grad[None]
    grad_branch = grad_first.astype(BF16)
    vec_grads[0:1] = jnp.sum(grad_branch.astype(F32), axis=0, keepdims=True)
    for g in range(2):
        branch_halves[g] = grad_branch[:, g * half : (g + 1) * half]
    grad_att = dot_nt(grad_branch, out_all[...]).astype(BF16)
    for d in range(LINE):
        att_grads[d] = grad_att[:, d * third : (d + 1) * third]


def token_local(attended, tok, grad_out, vec, w_out, out_other, w_up, up_other, w_down, down_other):
    rows, width = tok.shape
    units = w_up.shape[1]
    shape = jax.ShapeDtypeStruct
    return pl.pallas_call(
        token_kernel,
        out_shape=[
            shape((rows, width), BF16),
            shape((rows, width), BF16),
            shape((2, rows, units // 2), BF16),
            shape((2, rows, units // 2), BF16),
            shape((rows, width), BF16),
            shape((rows, width), F32),
            shape((2, rows, width // 2), BF16),
            shape((LINE, rows, HEADS_OWN * HEAD), BF16),
            shape((16, width), F32),
        ],
        in_specs=[INNER] * 4 + [ANY] * 6,
        out_specs=[INNER] * 9,
        scratch_shapes=[
            pltpu.VMEM((width, width), BF16),
            pltpu.VMEM((width, units), BF16),
            pltpu.VMEM((units, width), BF16),
            pltpu.VMEM((rows, units), BF16),
            pltpu.VMEM((rows, units), F32),
            pltpu.SemaphoreType.DMA((6,)),
        ],
        compiler_params=pltpu.CompilerParams(vmem_limit_bytes=63 << 20),
        name="token_local",
    )(attended, tok, grad_out, vec, w_out, out_other, w_up, up_other, w_down, down_other)


UP, DOWN, QKV, OUT, VEC = range(5)


def backward_kernel(
    dims,
    att_grads,
    q_heads,
    k_heads,
    v_heads,
    att_full,
    totals,
    grad_first,
    vec_one,
    probs_in,
    w_full,
    normed_b,
    act_halves,
    up_halves,
    grad_ffn,
    attended,
    branch_halves,
    tok,
    tok_pair,
    grad_hidden,
    up_own,
    down_own,
    qkv_own,
    out_own,
    vec_own,
    w_all,
    probs,
    grad_land,
    scaled,
    score_grads,
    query_grads,
    kv_own,
    kv_sent,
    kv_pair,
    kv_sum,
    kv_land,
    query_land,
    mixed,
    operands,
    parts,
    from_core,
    from_pair,
    from_low,
    from_high,
    vec_seq,
    local_sem,
    line_out,
    line_in,
    pair_out,
    pair_in,
    back_out,
    back_in,
    seq_out,
    seq_in,
    core_sem,
    side_sem,
    low_sem,
    high_sem,
    last_sem,
):
    place = lax.axis_index("ctx")
    core = lax.axis_index("fsdp")
    group = lax.axis_index("seq")
    line, side = place // 2, place % 2
    to_core = {"fsdp": 1 - core}
    to_pair = {"ctx": place + 1 - 2 * side}
    to_seq = {"seq": 1 - group}
    to_up = {"ctx": lax.rem(place + 2, 2 * LINE)}
    to_down = {"ctx": lax.rem(place + 2 * LINE - 2, 2 * LINE)}
    rows, width = grad_hidden.shape
    third = HEADS_OWN * HEAD
    mid = LINE * rows
    middle = 3 * width // 2
    outs = (up_own, down_own, qkv_own, out_own)
    units = (UP, DOWN, QKV, OUT, VEC)

    def ahead(k):
        return lax.rem(line + k, LINE)

    def behind(k):
        return lax.rem(line + LINE - k, LINE)

    def to_line(k):
        return {"ctx": 2 * ahead(k) + side}

    def block(which):
        return pl.ds(pl.multiple_of(which * rows, 32), rows)

    own_half = pl.ds(pl.multiple_of(group * middle, 128), middle)
    far_half = pl.ds(pl.multiple_of((1 - group) * middle, 128), middle)


    def core_copy(u):
        return remote(
            parts[u].at[1 - core], from_core[u], core_sem.at[0, u], core_sem.at[1, u], to_core
        )

    def side_copy(u, k):
        return remote(
            parts[u].at[core, k, 1 - side],
            from_pair[u].at[k],
            side_sem.at[0, u, k],
            side_sem.at[1, u, k],
            to_pair,
        )

    def up_copy(u, k):
        return remote(
            parts[u].at[core, k, side],
            from_low[u].at[k - 1],
            low_sem.at[0, u, k - 1],
            low_sem.at[1, u, k - 1],
            to_up,
        )

    def down_copy(u, k):
        return remote(
            parts[u].at[core, k, side],
            from_high[u].at[k],
            high_sem.at[0, u, k],
            high_sem.at[1, u, k],
            to_down,
        )

    def last_copy(u):
        if u == VEC:
            where = vec_seq
        else:
            size, columns, wide = dims[u]
            if wide:
                where = outs[u].at[:, pl.ds(pl.multiple_of(group * columns, 128), columns)]
            else:
                where = outs[u].at[pl.ds(pl.multiple_of(group * size, 16), size)]
        return remote(
            parts[u].at[core, line, side], where, last_sem.at[0, u], last_sem.at[1, u], to_seq
        )

    def multiply(u):
        size, columns, _ = dims[u]
        a_own, a_pair, b_own, b_pair = operands[u]
        step = 384
        for first in range(0, a_own.shape[1], step):
            span = slice(first, first + step)
            product = dot_tn(a_own[:, span], b_own[...]) + dot_tn(a_pair[:, span], b_pair[...])
            product = product.astype(BF16)
            for i in range(step // size):
                j = first // size + i
                parts[u][j % 2, j // 4, (j // 2) % 2] = product[i * size : (i + 1) * size]
        core_copy(u).start()

    def add_core(u):
        core_copy(u).wait_recv()
        for k in (3, 0, 2, 1):
            parts[u][core, k, 1 - side] += from_core[u][k, 1 - side]
            side_copy(u, k).start()
        for k in range(LINE):
            parts[u][core, k, side] += from_core[u][k, side]

    def add_pair(u):
        for k in (3, 0, 2, 1):
            side_copy(u, k).wait_recv()
            parts[u][core, k, side] += from_pair[u][k]

        @pl.when(line == 0)
        def _():
            for k in range(LINE - 1, 0, -1):
                up_copy(u, k).start()

        @pl.when(line == LINE - 1)
        def _():
            for k in range(LINE - 1):
                down_copy(u, k).start()

    def pass_up(u, k):
        up_copy(u, k).wait_recv()
        parts[u][core, k, side] += from_low[u][k - 1]
        up_copy(u, k).start()

    def pass_down(u, k):
        down_copy(u, k).wait_recv()
        parts[u][core, k, side] += from_high[u][k]
        down_copy(u, k).start()

    def first_hop(u):
        @pl.when(line == 1)
        def _():
            pass_up(u, 3)
            pass_up(u, 2)

        @pl.when(line == 2)
        def _():
            pass_down(u, 0)
            pass_down(u, 1)

    def second_hop(u):
        @pl.when(line == 2)
        def _():
            pass_up(u, 3)

        @pl.when(line == 1)
        def _():
            pass_down(u, 0)

    def finish_unit(u):
        for k in range(LINE):

            @pl.when(line == k)
            def _(k=k):
                if k > 0:
                    up_copy(u, k).wait_recv()
                    parts[u][core, k, side] += from_low[u][k - 1]
                if k < LINE - 1:
                    down_copy(u, k).wait_recv()
                    parts[u][core, k, side] += from_high[u][k]

        last_copy(u).start()
        if u != VEC:
            size, columns, wide = dims[u]
            if wide:
                start = pl.multiple_of(group * columns, 128)
                outs[u][:, pl.ds(start, columns)] = parts[u][core, line, side]
            else:
                start = pl.multiple_of(group * size, 16)
                outs[u][pl.ds(start, size)] = parts[u][core, line, side]


    probs_load = pltpu.make_async_copy(probs_in, probs, local_sem.at[0])
    w_load = pltpu.make_async_copy(w_full, w_all, local_sem.at[1])
    probs_load.start()
    greet([to_core, to_pair, to_seq] + [to_line(k) for k in range(1, LINE)])

    def line_copy(k):
        return remote(
            att_grads.at[ahead(k)],
            grad_land.at[block(line)],
            line_out.at[k - 1],
            line_in.at[k - 1],
            to_line(k),
        )

    def line_landed(k):
        return remote(
            att_grads.at[ahead(k)],
            grad_land.at[block(behind(k))],
            line_out.at[k - 1],
            line_in.at[k - 1],
            to_line(k),
        )

    for k in (3, 2, 1):
        line_copy(k).start()
    sources = (
        (normed_b, normed_b, operands[UP][0], operands[UP][1]),
        (up_halves.at[group], up_halves.at[1 - group], operands[UP][2], operands[UP][3]),
        (act_halves.at[group], act_halves.at[1 - group], operands[DOWN][0], operands[DOWN][1]),
        (grad_ffn, grad_ffn, operands[DOWN][2], operands[DOWN][3]),
        (attended, attended, operands[OUT][0], operands[OUT][1]),
        (branch_halves.at[group], branch_halves.at[1 - group], operands[OUT][2], operands[OUT][3]),
    )
    seq_copies, loads = [], []
    for i, (own, far, here, there) in enumerate(sources):
        seq_copies.append(remote(far, there, seq_out.at[i], seq_in.at[i], to_seq))
        loads.append(pltpu.make_async_copy(own, here, local_sem.at[2 + i]))
    for copy in seq_copies:
        copy.start()
    tok_loads = [
        pltpu.make_async_copy(tok, operands[QKV][0], local_sem.at[8]),
        pltpu.make_async_copy(tok_pair, operands[QKV][1], local_sem.at[9]),
    ]
    mixed_copy = remote(mixed.at[:, far_half], operands[QKV][3], seq_out.at[6], seq_in.at[6], to_seq)
    w_load.start()
    for load in loads + tok_loads:
        load.start()
    grad_land[block(line)] = att_grads[line]
    for k in (1, 2, 3):
        line_landed(k).wait_recv()
    probs_load.wait()

    def pair_copy(h):
        return remote(kv_sent.at[h], kv_pair.at[h], pair_out.at[h], pair_in.at[h], to_pair)

    def head_grads(h):
        lanes = slice(h * HEAD, (h + 1) * HEAD)

        def row_grads(i, carry):
            where = block(i)
            incoming = grad_land[where, lanes].astype(F32)
            row_total = totals[where, h : h + 1]
            delta = jnp.sum(incoming * att_full[where, lanes], axis=-1, keepdims=True)
            grad_scaled = (incoming / row_total).astype(BF16)
            scaled[where] = grad_scaled
            weights = dot_nt(grad_scaled, v_heads[h])
            ds = (probs[h, where].astype(F32) * (weights - delta / row_total)).astype(BF16)
            score_grads[where] = ds
            query_grads[where, lanes] = (dot_nn(ds, k_heads[h]) * 0.125).astype(BF16)
            return carry

        lax.fori_loop(0, LINE, row_grads, 0)
        both = jnp.concatenate(
            [dot_tn(q_heads[h], score_grads[...]) * 0.125, dot_tn(scaled[...], probs[h])], axis=0
        )
        both = jnp.transpose(both)
        kv_sent[h] = both[mid:].astype(BF16)
        pair_copy(h).start()
        kv_own[h] = both[:mid]

    def query_back(k):
        return remote(
            query_grads.at[block(ahead(k))],
            query_land.at[line],
            back_out.at[HEADS_OWN, k - 1],
            back_in.at[HEADS_OWN, k - 1],
            to_line(k),
        )

    def query_landed(k):
        return remote(
            query_grads.at[block(ahead(k))],
            query_land.at[behind(k)],
            back_out.at[HEADS_OWN, k - 1],
            back_in.at[HEADS_OWN, k - 1],
            to_line(k),
        )

    def kv_back(h, k):
        return remote(
            kv_sum.at[h, block(ahead(k))],
            kv_land.at[h, line],
            back_out.at[h, k - 1],
            back_in.at[h, k - 1],
            to_line(k),
        )

    def kv_landed(h, k):
        return remote(
            kv_sum.at[h, block(ahead(k))],
            kv_land.at[h, behind(k)],
            back_out.at[h, k - 1],
            back_in.at[h, k - 1],
            to_line(k),
        )

    def ready(first, last):
        for i in range(first, last):
            seq_copies[i].wait_recv()
            loads[i].wait()

    def send_kv(h):
        pair_copy(h).wait_recv()
        kv_sum[h] = (kv_own[h] + kv_pair[h].astype(F32)).astype(BF16)
        for k in (3, 2, 1):
            kv_back(h, k).start()
        kv_land[h, line] = kv_sum[h, block(line)]

    head_grads(0)
    head_grads(1)
    send_kv(0)
    ready(0, 2)
    multiply(UP)
    head_grads(2)
    send_kv(1)
    for k in (3, 2, 1):
        query_back(k).start()
    query_land[line] = query_grads[block(line)]
    ready(2, 4)
    multiply(DOWN)
    send_kv(2)
    add_core(UP)
    ready(4, 6)
    multiply(OUT)
    for k in (1, 2, 3):
        query_landed(k).wait_recv()
    for d in range(LINE):
        mixed[:, d * third : (d + 1) * third] = query_land[d]
    for h in range(HEADS_OWN):
        for k in (1, 2, 3):
            kv_landed(h, k).wait_recv()
        for d in range(LINE):
            at = width + d * third + h * HEAD
            mixed[:, at : at + HEAD] = kv_land[h, d, :, 0:HEAD]
            mixed[:, width + at : width + at + HEAD] = kv_land[h, d, :, HEAD:]
    mixed_copy.start()
    operands[QKV][2][...] = mixed[:, own_half]
    add_core(DOWN)
    parts[VEC][...] = jnp.zeros(parts[VEC].shape, F32)
    for j in range(4 * LINE):
        slot = parts[VEC].at[j % 2, j // 4, (j // 2) % 2]
        size = width // (4 * LINE)
        slot[0:8, 0:size] = vec_one[0:8, j * size : (j + 1) * size]
        query_part = mixed[:, j * size : (j + 1) * size].astype(F32)
        slot[8:9, 0:size] = jnp.sum(query_part, axis=0, keepdims=True)
        value_part = mixed[:, 2 * width + j * size : 2 * width + (j + 1) * size].astype(F32)
        slot[9:10, 0:size] = jnp.sum(value_part, axis=0, keepdims=True)
        at = (j % 4) * 4 * size
        slot[10:11, 0 : 4 * size] = vec_one[8 + j // 4 : 9 + j // 4, at : at + 4 * size]
    w_load.wait()
    grad_hidden[...] = grad_first[...] + dot_nt(mixed[...], w_all[...])
    add_core(OUT)
    mixed_copy.wait_recv()
    for load in tok_loads:
        load.wait()
    multiply(QKV)
    core_copy(VEC).start()
    add_pair(UP)
    add_core(QKV)
    add_core(VEC)
    order = (UP, DOWN, OUT, QKV, VEC)
    for s in range(1, len(order) + 3):
        if s < len(order):
            add_pair(order[s])
        if 0 <= s - 1 < len(order):
            first_hop(order[s - 1])
        if 0 <= s - 2 < len(order):
            second_hop(order[s - 2])
        if 0 <= s - 3 < len(order):
            finish_unit(order[s - 3])
    for u in units:
        last_copy(u).wait_recv()
    vec_own[...] = parts[VEC][core, line, side] + vec_seq[...]
    for k in (1, 2, 3):
        line_copy(k).wait_send()
        query_back(k).wait_send()
        for h in range(HEADS_OWN):
            kv_back(h, k).wait_send()
    for h in range(HEADS_OWN):
        pair_copy(h).wait_send()
    for copy in seq_copies + [mixed_copy]:
        copy.wait_send()
    for u in units:
        core_copy(u).wait_send()
        last_copy(u).wait_send()
        for k in range(LINE):
            side_copy(u, k).wait_send()
        for k in range(1, LINE):

            @pl.when(line < k)
            def _(k=k):
                up_copy(u, k).wait_send()

        for k in range(LINE - 1):

            @pl.when(line > k)
            def _(k=k):
                down_copy(u, k).wait_send()


def backward(*args):
    rows, width = args[6].shape
    ffn = args[11].shape[2] * 2
    third = HEADS_OWN * HEAD
    mid, seq_rows = LINE * rows, 2 * LINE * rows
    shape = jax.ShapeDtypeStruct
    widths = ((width, ffn // 2), (ffn // 2, width), (width, 3 * width // 2), (width, width // 2))
    dims = [(a // (4 * LINE), b, a == width) for a, b in widths]
    own_shapes = [(r, 2 * c) if wide else (2 * r, c) for r, c, wide in dims]
    blocks = [((r, c), BF16) for r, c, _ in dims] + [((16, 256), F32)]
    count = len(blocks)
    vmem, dma = pltpu.VMEM, pltpu.SemaphoreType.DMA
    outs = [shape((rows, width), F32)] + [shape(own, BF16) for own in own_shapes]
    outs.append(shape((16, 256), F32))
    return pl.pallas_call(
        functools.partial(backward_kernel, dims),
        out_shape=outs,
        in_specs=[INNER] * 8 + [ANY] * 10,
        out_specs=[INNER] * len(outs),
        scratch_shapes=[
            vmem((width, 3 * width), BF16),
            vmem((HEADS_OWN, mid, seq_rows), BF16),
            vmem((mid, third), BF16),
            vmem((mid, HEAD), BF16),
            vmem((mid, seq_rows), BF16),
            vmem((mid, third), BF16),
            vmem((HEADS_OWN, mid, 128), F32),
            vmem((HEADS_OWN, mid, 128), BF16),
            vmem((HEADS_OWN, mid, 128), BF16),
            vmem((HEADS_OWN, mid, 128), BF16),
            vmem((HEADS_OWN, LINE, rows, 128), BF16),
            vmem((LINE, rows, third), BF16),
            vmem((rows, 3 * width), BF16),
            [[vmem((rows, w), BF16) for w in (a, a, b, b)] for a, b in widths],
            [vmem((2, LINE, 2) + block, kind) for block, kind in blocks],
            [vmem((LINE, 2) + block, kind) for block, kind in blocks],
            [vmem((LINE,) + block, kind) for block, kind in blocks],
            [vmem((LINE - 1,) + block, kind) for block, kind in blocks],
            [vmem((LINE - 1,) + block, kind) for block, kind in blocks],
            vmem((16, 256), F32),
            dma((10,)),
            dma((3,)),
            dma((3,)),
            dma((3,)),
            dma((3,)),
            dma((4, 3)),
            dma((4, 3)),
            dma((7,)),
            dma((7,)),
            dma((2, count)),
            dma((2, count, LINE)),
            dma((2, count, LINE - 1)),
            dma((2, count, LINE - 1)),
            dma((2, count)),
        ],
        compiler_params=pltpu.CompilerParams(
            collective_id=2, has_side_effects=True, vmem_limit_bytes=63 << 20
        ),
        name="backward",
    )(*args)


def finish_kernel(*refs):
    for i in range(5):
        refs[6 + i][...] = refs[i][...].astype(F32)
    vec = refs[5]
    for i, row in enumerate((8, 9, 0, 1, 2, 3, 4, 5, 10)):
        out = refs[11 + i]
        out[...] = vec[row, 0 : out.shape[0]]


def finish(*args):
    shape = jax.ShapeDtypeStruct
    outs = [shape(a.shape, F32) for a in args[:5]]
    size = args[2].shape[0]
    outs += [shape((size,), F32)] * 8 + [shape((4 * size,), F32)]
    return pl.pallas_call(
        finish_kernel,
        out_shape=outs,
        in_specs=[INNER] * 6,
        out_specs=[INNER] * len(outs),
        name="finish",
    )(*args)


def block_device(
    hidden,
    segment_ids,
    out_grad,
    w_qkv,
    bias_query,
    bias_value,
    w_out,
    bias_out,
    gain_one,
    shift_one,
    w_up,
    bias_up,
    w_down,
    bias_down,
    gain_two,
    shift_two,
):
    tok, grad_out = hidden[0], out_grad[0]
    small = [
        bias_query,
        bias_value,
        bias_out,
        gain_one,
        shift_one,
        bias_down,
        gain_two,
        shift_two,
        bias_up,
    ]
    (
        attended,
        tok_pair,
        vec_all,
        w_full,
        out_other,
        up_other,
        down_other,
        q_heads,
        k_heads,
        v_heads,
        att_full,
        totals,
        probs,
    ) = attend_forward(tok, segment_ids, small, w_qkv, w_out, w_up, w_down)
    (
        result,
        normed_b,
        act_halves,
        up_halves,
        grad_ffn,
        grad_first,
        branch_halves,
        att_grads,
        vec_one,
    ) = token_local(
        attended, tok, grad_out, vec_all, w_out, out_other, w_up, up_other, w_down, down_other
    )
    grad_hidden, up_own, down_own, qkv_own, out_own, vec_own = backward(
        att_grads,
        q_heads,
        k_heads,
        v_heads,
        att_full,
        totals,
        grad_first,
        vec_one,
        probs,
        w_full,
        normed_b,
        act_halves,
        up_halves,
        grad_ffn,
        attended,
        branch_halves,
        tok,
        tok_pair,
    )
    grads = finish(up_own, down_own, qkv_own, out_own, grad_hidden, vec_own)
    up_grad, down_grad, qkv_grad, out_grads, grad_hidden = grads[:5]
    (
        query_bias,
        value_bias,
        out_bias,
        gain_first,
        shift_first,
        down_bias,
        gain_second,
        shift_second,
        up_bias,
    ) = grads[5:]
    return (
        result[None],
        grad_hidden[None],
        qkv_grad,
        query_bias,
        value_bias,
        out_grads,
        out_bias,
        gain_first,
        shift_first,
        up_grad,
        up_bias,
        down_grad,
        down_bias,
        gain_second,
        shift_second,
    )


def solution(mesh):
    small = (mesh.shape["seq"], mesh.shape["ctx"], mesh.shape["fsdp"]) == (2, 8, 2)
    return jax.shard_map(
        block_device if small else on_device,
        mesh=mesh,
        in_specs=(
            P(("seq", "fsdp"), "ctx", None),
            P(("seq", "fsdp"), None),
            P(("seq", "fsdp"), "ctx", None),
            P("fsdp", None),
            P("fsdp"),
            P("fsdp"),
            P("fsdp", None),
            P("fsdp"),
            P("fsdp"),
            P("fsdp"),
            P("fsdp", None),
            P("fsdp"),
            P("fsdp", None),
            P("fsdp"),
            P("fsdp"),
            P("fsdp"),
        ),
        out_specs=(
            P(("seq", "fsdp"), "ctx", None),
            P(("seq", "fsdp"), "ctx", None),
            P(("ctx", "fsdp"), None),
            P(("ctx", "fsdp")),
            P(("ctx", "fsdp")),
            P(("ctx", "fsdp"), None),
            P(("ctx", "fsdp")),
            P(("ctx", "fsdp")),
            P(("ctx", "fsdp")),
            P(("ctx", "fsdp"), None),
            P(("ctx", "fsdp")),
            P(("ctx", "fsdp"), None),
            P(("ctx", "fsdp")),
            P(("ctx", "fsdp")),
            P(("ctx", "fsdp")),
        ),
        check_vma=False,
    )
```

```python
import functools

import jax
import jax.numpy as jnp
from jax import lax
from jax.experimental import pallas as pl
from jax.experimental.pallas import tpu as pltpu
from jax.sharding import PartitionSpec as P

HEAD = 64


EPSILON = 1e-12
NEGATIVE = -1e30
LOG_TWO = 0.6931471805599453
LOG2_E = 1.4426950408889634


def norm_forward(rows_in, gain_vec, shift_vec):
    row_mean = jnp.mean(rows_in, axis=-1, keepdims=True)
    centered = rows_in - row_mean
    variance = jnp.mean(centered * centered, axis=-1, keepdims=True)
    scaled = lax.rsqrt(variance + EPSILON)
    normed = centered * scaled
    return (normed * gain_vec + shift_vec, normed, scaled)


def norm_backward(grad_rows, normed, scaled, gain_vec):
    grad_normed = grad_rows * gain_vec
    inner_part = (
        grad_normed
        - jnp.mean(grad_normed, axis=-1, keepdims=True)
        - normed * jnp.mean(grad_normed * normed, axis=-1, keepdims=True)
    )
    return (inner_part * scaled, jnp.sum(grad_rows * normed, axis=0), jnp.sum(grad_rows, axis=0))


def head_scores(query_heads, key_heads):
    return (
        jnp.einsum("qhd,khd->hqk", query_heads, key_heads, preferred_element_type=jnp.float32)
        * 0.125
    )


def column_sums(rows_b):
    return jnp.sum(rows_b.astype(jnp.float32), axis=0)


def sweep(steps_total, advance, start_carry):

    def advance_one(running, block_index):
        running = advance(running, block_index)
        return (running, None)

    return lax.scan(advance_one, start_carry, jnp.arange(steps_total))[0]


def local_grads(scores, allowed, shift_rows, ratio_rows, grad_heads, value_heads):
    unnorm = jnp.where(allowed, jnp.exp(scores - shift_rows[..., None]), 0.0)
    grad_weights = jnp.einsum(
        "qhd,khd->hqk", grad_heads, value_heads, preferred_element_type=jnp.float32
    )
    grad_scores = (unnorm * (grad_weights - ratio_rows[..., None])).astype(jnp.bfloat16)
    return (unnorm.astype(jnp.bfloat16), grad_scores)


def on_device(
    hidden,
    segment_ids,
    out_grad,
    w_qkv,
    bias_query,
    bias_value,
    w_out,
    bias_out,
    gain_one,
    shift_one,
    w_up,
    bias_up,
    w_down,
    bias_down,
    gain_two,
    shift_two,
):
    (
        w_qkv,
        bias_query,
        bias_value,
        w_out,
        bias_out,
        gain_one,
        shift_one,
        w_up,
        bias_up,
        w_down,
        bias_down,
        gain_two,
        shift_two,
    ) = (
        lax.all_gather(w_qkv, "fsdp", axis=0, tiled=True),
        lax.all_gather(bias_query, "fsdp", axis=0, tiled=True),
        lax.all_gather(bias_value, "fsdp", axis=0, tiled=True),
        lax.all_gather(w_out, "fsdp", axis=0, tiled=True),
        lax.all_gather(bias_out, "fsdp", axis=0, tiled=True),
        lax.all_gather(gain_one, "fsdp", axis=0, tiled=True),
        lax.all_gather(shift_one, "fsdp", axis=0, tiled=True),
        lax.all_gather(w_up, "fsdp", axis=0, tiled=True),
        lax.all_gather(bias_up, "fsdp", axis=0, tiled=True),
        lax.all_gather(w_down, "fsdp", axis=0, tiled=True),
        lax.all_gather(bias_down, "fsdp", axis=0, tiled=True),
        lax.all_gather(gain_two, "fsdp", axis=0, tiled=True),
        lax.all_gather(shift_two, "fsdp", axis=0, tiled=True),
    )
    f32 = jnp.float32
    bf16 = jnp.bfloat16
    tokens = hidden[0]
    tok_rows = tokens.shape[0]
    model_width = tokens.shape[1]
    head_count = model_width // HEAD
    seq_rows = tok_rows * lax.axis_size("ctx")
    key_span = 4 * tok_rows
    block_total = seq_rows // key_span
    doc_ids = segment_ids[0]
    own_ids = lax.dynamic_slice_in_dim(doc_ids, lax.axis_index("ctx") * tok_rows, tok_rows)
    mixed_rows = jnp.dot(tokens, w_qkv, preferred_element_type=f32)
    query_rows = (mixed_rows[:, :model_width] + bias_query.astype(f32)).astype(bf16)
    key_value = jnp.concatenate(
        [
            mixed_rows[:, model_width : 2 * model_width],
            mixed_rows[:, 2 * model_width :] + bias_value.astype(f32),
        ],
        axis=1,
    ).astype(bf16)
    all_kv = lax.all_gather(key_value, "ctx", axis=0, tiled=True)
    query_heads = query_rows.reshape(tok_rows, head_count, HEAD)

    def key_block(block_index):
        kv_piece = lax.dynamic_slice_in_dim(all_kv, block_index * key_span, key_span, 0)
        key_ids = lax.dynamic_slice_in_dim(doc_ids, block_index * key_span, key_span)
        return (
            kv_piece[:, :model_width].reshape(key_span, head_count, HEAD),
            kv_piece[:, model_width:].reshape(key_span, head_count, HEAD),
            key_ids,
        )

    def forward_step(running, block_index):
        level_run, total_run, sum_run = running
        key_heads, value_heads, key_ids = key_block(block_index)
        allowed = (own_ids[:, None] == key_ids[None, :])[None]
        scores = jnp.where(allowed, head_scores(query_heads, key_heads), NEGATIVE)
        level_new = jnp.maximum(level_run, jnp.ceil(jnp.max(scores, axis=-1) * LOG2_E))
        rescale = jnp.exp(LOG_TWO * (level_run - level_new))
        unnorm = jnp.where(allowed, jnp.exp(scores - (LOG_TWO * level_new)[..., None]), 0.0)
        total_new = total_run * rescale + jnp.sum(unnorm, axis=-1)
        sum_new = sum_run * jnp.transpose(rescale)[:, :, None] + jnp.einsum(
            "hqk,khd->qhd", unnorm.astype(bf16), value_heads, preferred_element_type=f32
        )
        return (level_new, total_new, sum_new)

    start_state = (
        jnp.full((head_count, tok_rows), NEGATIVE, f32),
        jnp.zeros((head_count, tok_rows), f32),
        jnp.zeros((tok_rows, head_count, HEAD), f32),
    )
    level_end, row_total, raw_sum = sweep(block_total, forward_step, start_state)
    row_shift = LOG_TWO * level_end
    att_sum = raw_sum / jnp.transpose(row_total)[:, :, None]
    attended = att_sum.reshape(tok_rows, model_width).astype(bf16)
    branch = jnp.dot(attended, w_out, preferred_element_type=f32) + bias_out.astype(f32)
    normed_one, norm_one, scale_one = norm_forward(
        tokens.astype(f32) + branch, gain_one.astype(f32), shift_one.astype(f32)
    )
    normed_b = normed_one.astype(bf16)
    up_rows = jnp.dot(normed_b, w_up, preferred_element_type=f32) + bias_up.astype(f32)
    active, gelu_back = jax.vjp(lambda pre_act: jax.nn.gelu(pre_act, approximate=False), up_rows)
    active_b = active.astype(bf16)
    second = (
        normed_one + jnp.dot(active_b, w_down, preferred_element_type=f32) + bias_down.astype(f32)
    )
    result, norm_two, scale_two = norm_forward(second, gain_two.astype(f32), shift_two.astype(f32))
    grad_second, grad_gain_two, grad_shift_two = norm_backward(
        out_grad[0].astype(f32), norm_two, scale_two, gain_two.astype(f32)
    )
    grad_ffn = grad_second.astype(bf16)
    grad_bias_down = column_sums(grad_ffn)
    grad_w_down = jnp.dot(active_b.T, grad_ffn, preferred_element_type=f32)
    grad_active = jnp.dot(grad_ffn, w_down.T, preferred_element_type=f32)
    grad_up = gelu_back(grad_active)[0].astype(bf16)
    grad_bias_up = column_sums(grad_up)
    grad_w_up = jnp.dot(normed_b.T, grad_up, preferred_element_type=f32)
    grad_normed = grad_second + jnp.dot(grad_up, w_up.T, preferred_element_type=f32)
    grad_first, grad_gain_one, grad_shift_one = norm_backward(
        grad_normed, norm_one, scale_one, gain_one.astype(f32)
    )
    grad_branch = grad_first.astype(bf16)
    grad_bias_out = column_sums(grad_branch)
    grad_w_out = jnp.dot(attended.T, grad_branch, preferred_element_type=f32)
    grad_attended = jnp.dot(grad_branch, w_out.T, preferred_element_type=f32).astype(bf16)
    grad_att_f32 = grad_attended.reshape(tok_rows, head_count, HEAD).astype(f32)
    delta = jnp.einsum("qhd,qhd->hq", grad_att_f32, att_sum)
    delta_ratio = delta / row_total
    grad_scaled = (grad_att_f32 / jnp.transpose(row_total)[:, :, None]).astype(bf16)
    zero_query = jnp.zeros((tok_rows, head_count, HEAD), f32)

    def full_step(running, block_index):
        grad_query, grad_kv = running
        key_heads, value_heads, key_ids = key_block(block_index)
        allowed = (own_ids[:, None] == key_ids[None, :])[None]
        unnorm_b, grad_scores = local_grads(
            head_scores(query_heads, key_heads),
            allowed,
            row_shift,
            delta_ratio,
            grad_scaled,
            value_heads,
        )
        grad_query = (
            grad_query
            + jnp.einsum("hqk,khd->qhd", grad_scores, key_heads, preferred_element_type=f32) * 0.125
        )
        grad_keys = (
            jnp.einsum("hqk,qhd->khd", grad_scores, query_heads, preferred_element_type=f32) * 0.125
        )
        grad_values = jnp.einsum("hqk,qhd->khd", unnorm_b, grad_scaled, preferred_element_type=f32)
        both_grads = jnp.concatenate(
            [grad_keys.reshape(key_span, model_width), grad_values.reshape(key_span, model_width)],
            axis=1,
        )
        grad_kv = lax.dynamic_update_slice_in_dim(grad_kv, both_grads, block_index * key_span, 0)
        return (grad_query, grad_kv)

    start_full = (zero_query, jnp.zeros((seq_rows, 2 * model_width), f32))
    grad_query, grad_kv = sweep(block_total, full_step, start_full)
    own_kv = lax.psum_scatter(grad_kv, "ctx", scatter_dimension=0, tiled=True)
    grad_query_b = grad_query.reshape(tok_rows, model_width).astype(bf16)
    grad_kv_b = own_kv.astype(bf16)
    grad_mixed = jnp.concatenate([grad_query_b, grad_kv_b], axis=1)
    grad_tokens = grad_first + jnp.dot(grad_mixed, w_qkv.T, preferred_element_type=f32)
    grad_w_qkv = jnp.dot(tokens.T, grad_mixed, preferred_element_type=f32)
    grad_bias_query = column_sums(grad_query_b)
    grad_bias_value = column_sums(grad_kv_b[:, model_width:])
    shares = (
        lax.psum_scatter(grad_w_qkv, ("ctx", "fsdp"), scatter_dimension=0, tiled=True),
        lax.psum_scatter(grad_bias_query, ("ctx", "fsdp"), scatter_dimension=0, tiled=True),
        lax.psum_scatter(grad_bias_value, ("ctx", "fsdp"), scatter_dimension=0, tiled=True),
        lax.psum_scatter(grad_w_out, ("ctx", "fsdp"), scatter_dimension=0, tiled=True),
        lax.psum_scatter(grad_bias_out, ("ctx", "fsdp"), scatter_dimension=0, tiled=True),
        lax.psum_scatter(grad_gain_one, ("ctx", "fsdp"), scatter_dimension=0, tiled=True),
        lax.psum_scatter(grad_shift_one, ("ctx", "fsdp"), scatter_dimension=0, tiled=True),
        lax.psum_scatter(grad_w_up, ("ctx", "fsdp"), scatter_dimension=0, tiled=True),
        lax.psum_scatter(grad_bias_up, ("ctx", "fsdp"), scatter_dimension=0, tiled=True),
        lax.psum_scatter(grad_w_down, ("ctx", "fsdp"), scatter_dimension=0, tiled=True),
        lax.psum_scatter(grad_bias_down, ("ctx", "fsdp"), scatter_dimension=0, tiled=True),
        lax.psum_scatter(grad_gain_two, ("ctx", "fsdp"), scatter_dimension=0, tiled=True),
        lax.psum_scatter(grad_shift_two, ("ctx", "fsdp"), scatter_dimension=0, tiled=True),
    )
    summed = (
        lax.psum(shares[0].astype(jnp.bfloat16), "seq").astype(jnp.float32),
        lax.psum(shares[1].astype(jnp.bfloat16), "seq").astype(jnp.float32),
        lax.psum(shares[2].astype(jnp.bfloat16), "seq").astype(jnp.float32),
        lax.psum(shares[3].astype(jnp.bfloat16), "seq").astype(jnp.float32),
        lax.psum(shares[4].astype(jnp.bfloat16), "seq").astype(jnp.float32),
        lax.psum(shares[5].astype(jnp.bfloat16), "seq").astype(jnp.float32),
        lax.psum(shares[6].astype(jnp.bfloat16), "seq").astype(jnp.float32),
        lax.psum(shares[7].astype(jnp.bfloat16), "seq").astype(jnp.float32),
        lax.psum(shares[8].astype(jnp.bfloat16), "seq").astype(jnp.float32),
        lax.psum(shares[9].astype(jnp.bfloat16), "seq").astype(jnp.float32),
        lax.psum(shares[10].astype(jnp.bfloat16), "seq").astype(jnp.float32),
        lax.psum(shares[11].astype(jnp.bfloat16), "seq").astype(jnp.float32),
        lax.psum(shares[12].astype(jnp.bfloat16), "seq").astype(jnp.float32),
    )
    return (
        result.astype(bf16)[None],
        grad_tokens[None],
        summed[0],
        summed[1],
        summed[2],
        summed[3],
        summed[4],
        summed[5],
        summed[6],
        summed[7],
        summed[8],
        summed[9],
        summed[10],
        summed[11],
        summed[12],
    )


MESH_ID = pl.DeviceIdType.MESH
LINE = 4


def remote(src, dst, send, recv, target):
    return pltpu.make_async_remote_copy(
        src_ref=src,
        dst_ref=dst,
        send_sem=send,
        recv_sem=recv,
        device_id=target,
        device_id_type=MESH_ID,
    )


HEADS_OWN = 3
F32 = jnp.float32
BF16 = jnp.bfloat16
ANY = pl.BlockSpec(memory_space=pl.ANY)
INNER = pl.BlockSpec(memory_space=pltpu.VMEM)


def dot_nt(a, b):
    return lax.dot_general(a, b, (((1,), (1,)), ((), ())), preferred_element_type=F32)


def dot_tn(a, b):
    return lax.dot_general(a, b, (((0,), (0,)), ((), ())), preferred_element_type=F32)


def dot_nn(a, b):
    return lax.dot_general(a, b, (((1,), (0,)), ((), ())), preferred_element_type=F32)


def greet(targets):
    barrier = pltpu.get_barrier_semaphore()
    for target in targets:
        pl.semaphore_signal(barrier, inc=1, device_id=target, device_id_type=MESH_ID)
    pl.semaphore_wait(barrier, len(targets))


def attend_kernel(
    tok,
    ids,
    small,
    w_qkv,
    w_out,
    w_up,
    w_down,
    attended,
    tok_pair,
    vec_all,
    w_full,
    out_other,
    up_other,
    down_other,
    q_heads,
    k_heads,
    v_heads,
    att_full,
    totals,
    probs_out,
    w_all,
    mixed,
    sent_kv,
    sent_q,
    mine,
    mine_q,
    other,
    att_sent,
    att_land,
    probs,
    vec,
    ids_row,
    ids_col,
    local_sem,
    probs_sem,
    core_out,
    core_in,
    line_out,
    line_in,
    pair_out,
    pair_in,
    back_out,
    back_in,
    seq_out,
    seq_in,
):
    place = lax.axis_index("ctx")
    core = lax.axis_index("fsdp")
    group = lax.axis_index("seq")
    line, side = place // 2, place % 2
    to_core = {"fsdp": 1 - core}
    to_pair = {"ctx": place + 1 - 2 * side}
    to_seq = {"seq": 1 - group}
    rows = tok.shape[0]
    width = tok.shape[1]
    half = width // 2
    third = HEADS_OWN * HEAD

    def ahead(k):
        return lax.rem(line + k, LINE)

    def behind(k):
        return lax.rem(line + LINE - k, LINE)

    def to_line(k):
        return {"ctx": 2 * ahead(k) + side}

    def block(which):
        return pl.ds(pl.multiple_of(which * rows, 32), rows)

    def half_block(which):
        return pl.ds(pl.multiple_of(which * (rows // 2), 16), rows // 2)

    own_rows = pl.ds(pl.multiple_of(core * half, 128), half)
    other_rows = pl.ds(pl.multiple_of((1 - core) * half, 128), half)

    own_load = pltpu.make_async_copy(w_qkv, w_all.at[own_rows], local_sem.at[0])
    own_load.start()
    at = 0
    for piece in small:
        for first in range(0, piece.shape[0], half):
            vec[at : at + 1] = piece[first : first + half].astype(F32)[None]
            at += 1
    vec[at:] = jnp.zeros((vec.shape[0] - at, half), F32)
    greet([to_core, to_pair, to_seq] + [to_line(k) for k in range(1, LINE)])
    core_copies = [
        remote(w_qkv, w_all.at[own_rows], core_out.at[0], core_in.at[0], to_core),
        remote(vec, vec_all.at[:, own_rows], core_out.at[1], core_in.at[1], to_core),
        remote(w_out, out_other, core_out.at[2], core_in.at[2], to_core),
        remote(w_up, up_other, core_out.at[3], core_in.at[3], to_core),
        remote(w_down, down_other, core_out.at[4], core_in.at[4], to_core),
    ]
    seq_copy = remote(tok, tok_pair, seq_out.at[0], seq_in.at[0], to_seq)
    core_copies[0].start()
    core_copies[1].start()
    seq_copy.start()
    vec_all[:, own_rows] = vec[...]
    own_load.wait()
    step = width // 2
    for first in range(0, 3 * width, step):
        mixed[:, first : first + step] = dot_nn(
            tok[:, own_rows], w_all[own_rows, first : first + step]
        )
    core_copies[0].wait_recv()
    core_copies[1].wait_recv()
    for copy in core_copies[2:]:
        copy.start()

    def kv_copy(k, to):
        return remote(
            sent_kv.at[ahead(k)],
            mine.at[block(to)],
            line_out.at[0, k - 1],
            line_in.at[0, k - 1],
            to_line(k),
        )

    def q_copy(k, to):
        return remote(
            sent_q.at[ahead(k)],
            mine_q.at[half_block(to)],
            line_out.at[1, k - 1],
            line_in.at[1, k - 1],
            to_line(k),
        )

    def pair_copy(k):
        where = block(behind(k))
        return remote(mine.at[where], other.at[where], pair_out.at[k], pair_in.at[k], to_pair)

    bias = vec_all[...]
    for part in (1, 2, 0):
        for first in range(part * width, (part + 1) * width, step):
            total = mixed[:, first : first + step] + dot_nn(
                tok[:, other_rows], w_all[other_rows, first : first + step]
            )
            within = first - part * width
            if part == 0:
                total += bias[0:1, within : within + step]
            if part == 2:
                total += bias[1:2, within : within + step]
            total = total.astype(BF16)
            for j in range(2):
                d, piece = within // third + j, total[:, j * third : (j + 1) * third]
                if part == 0:
                    sent_q[d, :, 0:third] = piece[: rows // 2]
                    sent_q[d, :, third:] = piece[rows // 2 :]
                else:
                    sent_kv[d, :, (part - 1) * third : part * third] = piece
        for k in (3, 2, 1):
            if part == 2:
                kv_copy(k, line).start()
            if part == 0:
                q_copy(k, line).start()
        if part == 2:
            mine[block(line)] = sent_kv[line]
            pair_copy(0).start()
    full_store = pltpu.make_async_copy(w_all, w_full, local_sem.at[1])
    full_store.start()
    mine_q[half_block(line)] = sent_q[line]
    for k in (1, 2, 3):
        kv_copy(k, behind(k)).wait_recv()
        pair_copy(k).start()
    seq_rows = 2 * LINE * rows
    mid = LINE * rows
    for z in range(LINE):
        even = ids[:, 2 * z * rows : (2 * z + 1) * rows].astype(F32)
        odd = ids[:, (2 * z + 1) * rows : (2 * z + 2) * rows].astype(F32)
        ids_row[:, z * rows : (z + 1) * rows] = jnp.where(side == 0, even, odd)
        ids_row[:, mid + z * rows : mid + (z + 1) * rows] = jnp.where(side == 0, odd, even)
    ids_col[...] = jnp.transpose(jnp.broadcast_to(ids_row[:, 0:mid], (8, mid)))[:, 0:1]
    for h in range(HEADS_OWN):
        k_heads[h, 0:mid] = mine[:, h * HEAD : (h + 1) * HEAD]
        v_heads[h, 0:mid] = mine[:, third + h * HEAD : third + (h + 1) * HEAD]
    for k in (1, 2, 3):
        q_copy(k, behind(k)).wait_recv()
    for h in range(HEADS_OWN):
        for i in range(2 * LINE):
            from_rows = slice((i // 2) * rows // 2, (i // 2 + 1) * rows // 2)
            at = (i % 2) * third + h * HEAD
            q_heads[h, i * rows // 2 : (i + 1) * rows // 2] = mine_q[from_rows, at : at + HEAD]
    for k in range(LINE):
        pair_copy(k).wait_recv()
    for h in range(HEADS_OWN):
        k_heads[h, mid:seq_rows] = other[:, h * HEAD : (h + 1) * HEAD]
        v_heads[h, mid:seq_rows] = other[:, third + h * HEAD : third + (h + 1) * HEAD]

    def back_copy(k):
        return remote(
            att_sent.at[ahead(k)],
            att_land.at[line],
            back_out.at[k - 1],
            back_in.at[k - 1],
            to_line(k),
        )

    def back_landed(k):
        return remote(
            att_sent.at[ahead(k)],
            att_land.at[behind(k)],
            back_out.at[k - 1],
            back_in.at[k - 1],
            to_line(k),
        )

    def probs_copy(k):
        where = block(ahead(k))
        return pltpu.make_async_copy(
            probs.at[:, where], probs_out.at[:, where], probs_sem.at[k - 1]
        )

    def attend(k, carry):
        which = ahead(k)
        where = block(which)
        allowed = ids_col[where] == ids_row[...]
        for h in range(HEADS_OWN):
            scores = dot_nt(q_heads[h, where], k_heads[h]) * 0.125
            scores = jnp.where(allowed, scores, NEGATIVE)
            level = jnp.ceil(jnp.max(scores, axis=-1, keepdims=True) * LOG2_E)
            unnorm = jnp.exp(scores - LOG_TWO * level)
            row_total = jnp.sum(unnorm, axis=-1, keepdims=True)
            unnorm_b = unnorm.astype(BF16)
            probs[h, where] = unnorm_b
            value = dot_nn(unnorm_b, v_heads[h]) / row_total
            att_full[where, h * HEAD : (h + 1) * HEAD] = value
            totals[where, h : h + 1] = row_total
            value_b = value.astype(BF16)
            for i in range(2):
                att_sent[which, :, i * third + h * HEAD : i * third + (h + 1) * HEAD] = value_b[
                    i * rows // 2 : (i + 1) * rows // 2
                ]
        probs_copy(k).start()

        @pl.when(k < LINE)
        def _():
            back_copy(k).start()

        return carry

    lax.fori_loop(1, LINE + 1, attend, 0)
    att_land[line] = att_sent[line]
    for k in (1, 2, 3):
        back_landed(k).wait_recv()
    for d in range(LINE):
        for i in range(2):
            attended[i * rows // 2 : (i + 1) * rows // 2, d * third : (d + 1) * third] = att_land[
                d, :, i * third : (i + 1) * third
            ]
    for k in (1, 2, 3):
        kv_copy(k, line).wait_send()
        q_copy(k, line).wait_send()
        back_copy(k).wait_send()
    for k in range(LINE):
        pair_copy(k).wait_send()
        probs_copy(k + 1).wait()
    for copy in core_copies[2:]:
        copy.wait_recv()
    for copy in core_copies:
        copy.wait_send()
    seq_copy.wait()
    full_store.wait()


def attend_forward(tok, ids, small, w_qkv, w_out, w_up, w_down):
    rows, width = tok.shape
    third = HEADS_OWN * HEAD
    mid, seq_rows = LINE * rows, 2 * LINE * rows
    shape = jax.ShapeDtypeStruct
    outs = [
        (shape((rows, width), BF16), INNER),
        (shape((rows, width), BF16), INNER),
        (shape((16, width), F32), INNER),
        (shape((width, 3 * width), BF16), ANY),
        (shape(w_out.shape, BF16), ANY),
        (shape(w_up.shape, BF16), ANY),
        (shape(w_down.shape, BF16), ANY),
        (shape((HEADS_OWN, mid, HEAD), BF16), INNER),
        (shape((HEADS_OWN, seq_rows, HEAD), BF16), INNER),
        (shape((HEADS_OWN, seq_rows, HEAD), BF16), INNER),
        (shape((mid, third), F32), INNER),
        (shape((mid, 128), F32), INNER),
        (shape((HEADS_OWN, mid, seq_rows), BF16), ANY),
    ]
    dma = pltpu.SemaphoreType.DMA
    return pl.pallas_call(
        attend_kernel,
        out_shape=[o[0] for o in outs],
        in_specs=[INNER, INNER, [INNER] * len(small)] + [ANY] * 4,
        out_specs=[o[1] for o in outs],
        scratch_shapes=[
            pltpu.VMEM((width, 3 * width), BF16),
            pltpu.VMEM((rows, 3 * width), F32),
            pltpu.VMEM((LINE, rows, 2 * third), BF16),
            pltpu.VMEM((LINE, rows // 2, 2 * third), BF16),
            pltpu.VMEM((mid, 2 * third), BF16),
            pltpu.VMEM((mid // 2, 2 * third), BF16),
            pltpu.VMEM((mid, 2 * third), BF16),
            pltpu.VMEM((LINE, rows // 2, 2 * third), BF16),
            pltpu.VMEM((LINE, rows // 2, 2 * third), BF16),
            pltpu.VMEM((HEADS_OWN, mid, seq_rows), BF16),
            pltpu.VMEM((16, width // 2), F32),
            pltpu.VMEM((1, seq_rows), F32),
            pltpu.VMEM((mid, 1), F32),
            dma((2,)),
            dma((LINE,)),
            dma((5,)),
            dma((5,)),
            dma((2, 3)),
            dma((2, 3)),
            dma((LINE,)),
            dma((LINE,)),
            dma((3,)),
            dma((3,)),
            dma((1,)),
            dma((1,)),
        ],
        compiler_params=pltpu.CompilerParams(
            collective_id=1, has_side_effects=True, vmem_limit_bytes=63 << 20
        ),
        name="attend_forward",
    )(tok, ids, small, w_qkv, w_out, w_up, w_down)


DOWN, UP, OUT, QUERY, KEY, VALUE, VEC = range(7)


def backward_kernel(
    dims,
    attended,
    tok,
    grad_out,
    vec_in,
    w_out,
    out_other,
    w_up,
    up_other,
    w_down,
    down_other,
    q_in,
    k_in,
    v_in,
    att_in,
    totals_in,
    probs_in,
    w_full,
    tok_pair,
    result,
    grad_hidden,
    down_own,
    up_own,
    qkv_own,
    out_own,
    vec_own,
    out_all,
    up_all,
    down_all,
    active,
    slope,
    first,
    vec_one,
    att_grads,
    act_halves,
    up_halves,
    branch_halves,
    q_heads,
    k_heads,
    v_heads,
    att_full,
    totals,
    w_all,
    probs,
    grad_land,
    scaled,
    score_grads,
    query_grads,
    kv_own,
    kv_sent,
    kv_pair,
    kv_sum,
    kv_land,
    query_land,
    mixed,
    left_refs,
    right_refs,
    parts,
    from_core,
    from_pair,
    from_low,
    from_high,
    vec_seq,
    sem,
    local_sem,
    line_out,
    line_in,
    pair_out,
    pair_in,
    back_out,
    back_in,
    seq_out,
    seq_in,
    core_sem,
    side_sem,
    low_sem,
    high_sem,
    last_sem,
):
    place = lax.axis_index("ctx")
    core = lax.axis_index("fsdp")
    group = lax.axis_index("seq")
    line, side = place // 2, place % 2
    to_core = {"fsdp": 1 - core}
    to_pair = {"ctx": place + 1 - 2 * side}
    to_seq = {"seq": 1 - group}
    to_up = {"ctx": lax.rem(place + 2, 2 * LINE)}
    to_down = {"ctx": lax.rem(place + 2 * LINE - 2, 2 * LINE)}
    rows, width = grad_hidden.shape
    third = HEADS_OWN * HEAD
    mid = LINE * rows
    half = width // 2
    hidden_units = active.shape[1]
    outs = (down_own, up_own, out_own, qkv_own, qkv_own, qkv_own)
    left = [
        (act_halves.at[group], left_refs[0]),
        (left_refs[1], left_refs[2]),
        (attended, left_refs[3]),
        (tok, left_refs[4]),
    ]
    right = [
        (right_refs[0], right_refs[1]),
        (up_halves.at[group], right_refs[2]),
        (branch_halves.at[group], right_refs[3]),
    ]
    units = range(VEC + 1)

    def ahead(k):
        return lax.rem(line + k, LINE)

    def behind(k):
        return lax.rem(line + LINE - k, LINE)

    def to_line(k):
        return {"ctx": 2 * ahead(k) + side}

    def block(which):
        return pl.ds(pl.multiple_of(which * rows, 32), rows)

    def half_block(which):
        return pl.ds(pl.multiple_of(which * (rows // 2), 16), rows // 2)

    def half_of(part, which):
        return pl.ds(pl.multiple_of(part * width + which * half, 128), half)

    for part in range(3):
        right.append((mixed.at[:, half_of(part, group)], right_refs[4 + part]))


    def own_place(u):
        size, columns, wide = dims[u]
        if not wide:
            return (pl.ds(pl.multiple_of(group * size, 16), size), slice(None))
        if u >= QUERY:
            return (slice(None), half_of(u - QUERY, group))
        return (slice(None), pl.ds(pl.multiple_of(group * columns, 128), columns))

    def core_copy(u):
        return remote(
            parts[u].at[1 - core], from_core[u], core_sem.at[0, u], core_sem.at[1, u], to_core
        )

    def side_copy(u, k):
        return remote(
            parts[u].at[core, k, 1 - side],
            from_pair[u].at[k],
            side_sem.at[0, u, k],
            side_sem.at[1, u, k],
            to_pair,
        )

    def up_copy(u, k):
        return remote(
            parts[u].at[core, k, side],
            from_low[u].at[k - 1],
            low_sem.at[0, u, k - 1],
            low_sem.at[1, u, k - 1],
            to_up,
        )

    def down_copy(u, k):
        return remote(
            parts[u].at[core, k, side],
            from_high[u].at[k],
            high_sem.at[0, u, k],
            high_sem.at[1, u, k],
            to_down,
        )

    def last_copy(u):
        if u == VEC:
            where = vec_seq
        else:
            where = outs[u].at[own_place(u)]
        return remote(
            parts[u].at[core, line, side], where, last_sem.at[0, u], last_sem.at[1, u], to_seq
        )

    def multiply(u):
        size, columns, _ = dims[u]
        (a_own, a_pair), (b_own, b_pair) = left[min(u, QUERY)], right[u]
        step = 384
        for first in range(0, a_own.shape[1], step):
            span = slice(first, first + step)
            product = dot_tn(a_own[:, span], b_own[...]) + dot_tn(a_pair[:, span], b_pair[...])
            product = product.astype(BF16)
            for i in range(step // size):
                j = first // size + i
                parts[u][j % 2, j // 4, (j // 2) % 2] = product[i * size : (i + 1) * size]
        core_copy(u).start()

    def add_core(u):
        core_copy(u).wait_recv()
        for k in (3, 0, 2, 1):
            parts[u][core, k, 1 - side] += from_core[u][k, 1 - side]
            side_copy(u, k).start()
        for k in range(LINE):
            parts[u][core, k, side] += from_core[u][k, side]

    def add_pair(u):
        for k in (3, 0, 2, 1):
            side_copy(u, k).wait_recv()
            parts[u][core, k, side] += from_pair[u][k]

        @pl.when(line == 0)
        def _():
            for k in range(LINE - 1, 0, -1):
                up_copy(u, k).start()

        @pl.when(line == LINE - 1)
        def _():
            for k in range(LINE - 1):
                down_copy(u, k).start()

    def pass_up(u, k):
        up_copy(u, k).wait_recv()
        parts[u][core, k, side] += from_low[u][k - 1]
        up_copy(u, k).start()

    def pass_down(u, k):
        down_copy(u, k).wait_recv()
        parts[u][core, k, side] += from_high[u][k]
        down_copy(u, k).start()

    def first_hop(u):
        @pl.when(line == 1)
        def _():
            pass_up(u, 3)
            pass_up(u, 2)

        @pl.when(line == 2)
        def _():
            pass_down(u, 0)
            pass_down(u, 1)

    def second_hop(u):
        @pl.when(line == 2)
        def _():
            pass_up(u, 3)

        @pl.when(line == 1)
        def _():
            pass_down(u, 0)

    def finish_unit(u):
        for k in range(LINE):

            @pl.when(line == k)
            def _(k=k):
                if k > 0:
                    up_copy(u, k).wait_recv()
                    parts[u][core, k, side] += from_low[u][k - 1]
                if k < LINE - 1:
                    down_copy(u, k).wait_recv()
                    parts[u][core, k, side] += from_high[u][k]

        last_copy(u).start()
        if u != VEC:
            outs[u][own_place(u)] = parts[u][core, line, side]


    seq_copies = []
    for i, (src, dst) in enumerate(
        (
            (act_halves.at[1 - group], left[DOWN][1]),
            (right[DOWN][0], right[DOWN][1]),
            (left[UP][0], left[UP][1]),
            (up_halves.at[1 - group], right[UP][1]),
            (attended, left[OUT][1]),
            (branch_halves.at[1 - group], right[OUT][1]),
        )
    ):
        seq_copies.append(remote(src, dst, seq_out.at[i], seq_in.at[i], to_seq))

    def place_of(which, size):
        return pl.ds(pl.multiple_of(which * size, 128), size)

    loads = []
    for i, (own, far, full) in enumerate(
        ((w_out, out_other, out_all), (w_up, up_other, up_all), (w_down, down_other, down_all))
    ):
        size = own.shape[0]
        loads.append(
            (
                pltpu.make_async_copy(own, full.at[place_of(core, size)], sem.at[2 * i]),
                pltpu.make_async_copy(far, full.at[place_of(1 - core, size)], sem.at[2 * i + 1]),
            )
        )
    for pair in loads:
        for load in pair:
            load.start()
    late_loads = []
    for i, (src, dst) in enumerate(
        (
            (q_in, q_heads),
            (k_in, k_heads),
            (v_in, v_heads),
            (att_in, att_full),
            (totals_in, totals),
            (probs_in, probs),
            (w_full, w_all),
            (tok_pair, left[QUERY][1]),
        )
    ):
        late_loads.append(pltpu.make_async_copy(src, dst, local_sem.at[i]))
    for load in late_loads:
        load.start()
    greet([to_core, to_pair, to_seq] + [to_line(k) for k in range(1, LINE)])

    def arrived(i):
        for load in loads[i]:
            load.wait()

    bias_out, gain_one, shift_one = vec_in[2:3], vec_in[3:4], vec_in[4:5]
    bias_down, gain_two, shift_two = vec_in[5:6], vec_in[6:7], vec_in[7:8]
    arrived(0)
    branch = dot_nn(attended[...], out_all[...]) + bias_out
    normed_one, norm_one, scale_one = norm_forward(tok[...].astype(F32) + branch, gain_one, shift_one)
    normed_b = normed_one.astype(BF16)
    left[UP][0][...] = normed_b
    arrived(1)
    step = width
    for c in range(hidden_units // step):
        at, row = (c // 2) * half, 8 + 2 * (c % 2)
        bias = jnp.concatenate([vec_in[row : row + 1, at : at + half], vec_in[row + 1 : row + 2, at : at + half]], axis=1)
        up = dot_nn(normed_b, up_all[:, c * step : (c + 1) * step]) + bias
        cdf = 0.5 * (1.0 + lax.erf(up * 0.7071067811865476))
        active[:, c * step : (c + 1) * step] = (up * cdf).astype(BF16)
        slope[:, c * step : (c + 1) * step] = cdf + up * (
            0.3989422804014327 * jnp.exp(-0.5 * up * up)
        )
    piece = hidden_units // (8 * LINE)
    for j in range(4 * LINE):
        for g in range(2):
            at = (2 * j + g) * piece
            act_halves[g, :, j * piece : (j + 1) * piece] = active[:, at : at + piece]
    seq_copies[0].start()
    arrived(2)
    second = normed_one + bias_down
    second += dot_nn(active[...], down_all[...])
    final, norm_two, scale_two = norm_forward(second, gain_two, shift_two)
    result[...] = final.astype(BF16)
    grad_second, gain_grad, shift_grad = norm_backward(
        grad_out[...].astype(F32), norm_two, scale_two, gain_two
    )
    grad_ffn = grad_second.astype(BF16)
    right[DOWN][0][...] = grad_ffn
    seq_copies[1].start()
    seq_copies[2].start()
    vec_one[...] = jnp.zeros(vec_one.shape, F32)
    vec_one[3:4] = jnp.sum(grad_ffn.astype(F32), axis=0, keepdims=True)
    vec_one[4:5] = gain_grad[None]
    vec_one[5:6] = shift_grad[None]
    grad_normed = grad_second
    for c in range(hidden_units // step):
        span = slice(c * step, (c + 1) * step)
        grad_up = (dot_nt(grad_ffn, down_all[span]) * slope[:, span]).astype(BF16)
        vec_one[8 + c : 9 + c] = jnp.sum(grad_up.astype(F32), axis=0, keepdims=True)
        grad_normed += dot_nt(grad_up, up_all[:, span])
        up_halves[c // 2, :, (c % 2) * step : (c % 2 + 1) * step] = grad_up
    seq_copies[3].start()
    seq_copies[4].start()
    grad_first, gain_grad, shift_grad = norm_backward(grad_normed, norm_one, scale_one, gain_one)
    first[...] = grad_first
    vec_one[1:2] = gain_grad[None]
    vec_one[2:3] = shift_grad[None]
    grad_branch = grad_first.astype(BF16)
    vec_one[0:1] = jnp.sum(grad_branch.astype(F32), axis=0, keepdims=True)
    for g in range(2):
        branch_halves[g] = grad_branch[:, g * half : (g + 1) * half]
    seq_copies[5].start()
    grad_att = dot_nt(grad_branch, out_all[...]).astype(BF16)
    for d in range(LINE):
        for i in range(2):
            att_grads[d, :, i * third : (i + 1) * third] = grad_att[
                i * rows // 2 : (i + 1) * rows // 2, d * third : (d + 1) * third
            ]


    def line_copy(k):
        return remote(
            att_grads.at[ahead(k)],
            grad_land.at[half_block(line)],
            line_out.at[k - 1],
            line_in.at[k - 1],
            to_line(k),
        )

    def line_landed(k):
        return remote(
            att_grads.at[ahead(k)],
            grad_land.at[half_block(behind(k))],
            line_out.at[k - 1],
            line_in.at[k - 1],
            to_line(k),
        )

    for k in (3, 2, 1):
        line_copy(k).start()
    mixed_copies = []
    for part in range(3):
        mixed_copies.append(
            remote(
                mixed.at[:, half_of(part, 1 - group)],
                right[QUERY + part][1],
                seq_out.at[6 + part],
                seq_in.at[6 + part],
                to_seq,
            )
        )
    grad_land[half_block(line)] = att_grads[line]
    for k in (1, 2, 3):
        line_landed(k).wait_recv()
    for load in late_loads:
        load.wait()

    def pair_copy(h):
        return remote(kv_sent.at[h], kv_pair.at[h], pair_out.at[h], pair_in.at[h], to_pair)

    def head_grads(h):
        lanes = slice(h * HEAD, (h + 1) * HEAD)

        def row_grads(i, carry):
            where = block(i)
            packed = grad_land[half_block(i)]
            far_lanes = slice(third + h * HEAD, third + (h + 1) * HEAD)
            incoming = jnp.concatenate([packed[:, lanes], packed[:, far_lanes]], axis=0).astype(F32)
            row_total = totals[where, h : h + 1]
            delta = jnp.sum(incoming * att_full[where, lanes], axis=-1, keepdims=True)
            grad_scaled = (incoming / row_total).astype(BF16)
            scaled[where] = grad_scaled
            weights = dot_nt(grad_scaled, v_heads[h])
            ds = (probs[h, where].astype(F32) * (weights - delta / row_total)).astype(BF16)
            score_grads[where] = ds
            grad_query = (dot_nn(ds, k_heads[h]) * 0.125).astype(BF16)
            query_grads[half_block(i), lanes] = grad_query[: rows // 2]
            query_grads[half_block(i), far_lanes] = grad_query[rows // 2 :]
            return carry

        lax.fori_loop(0, LINE, row_grads, 0)
        both = jnp.concatenate(
            [dot_tn(q_heads[h], score_grads[...]) * 0.125, dot_tn(scaled[...], probs[h])], axis=0
        )
        both = jnp.transpose(both)
        kv_sent[h] = both[mid:].astype(BF16)
        pair_copy(h).start()
        kv_own[h] = both[:mid]

    def query_back(k):
        return remote(
            query_grads.at[half_block(ahead(k))],
            query_land.at[line],
            back_out.at[HEADS_OWN, k - 1],
            back_in.at[HEADS_OWN, k - 1],
            to_line(k),
        )

    def query_landed(k):
        return remote(
            query_grads.at[half_block(ahead(k))],
            query_land.at[behind(k)],
            back_out.at[HEADS_OWN, k - 1],
            back_in.at[HEADS_OWN, k - 1],
            to_line(k),
        )

    def kv_back(h, k):
        return remote(
            kv_sum.at[h, block(ahead(k))],
            kv_land.at[h, line],
            back_out.at[h, k - 1],
            back_in.at[h, k - 1],
            to_line(k),
        )

    def kv_landed(h, k):
        return remote(
            kv_sum.at[h, block(ahead(k))],
            kv_land.at[h, behind(k)],
            back_out.at[h, k - 1],
            back_in.at[h, k - 1],
            to_line(k),
        )

    def ready(first, last):
        for i in range(first, last):
            seq_copies[i].wait_recv()

    def send_kv(h):
        pair_copy(h).wait_recv()
        kv_sum[h] = (kv_own[h] + kv_pair[h].astype(F32)).astype(BF16)
        for k in (3, 2, 1):
            kv_back(h, k).start()
        kv_land[h, line] = kv_sum[h, block(line)]

    head_grads(0)
    ready(0, 2)
    multiply(DOWN)
    head_grads(1)
    send_kv(0)
    add_core(DOWN)
    head_grads(2)
    for k in (3, 2, 1):
        query_back(k).start()
    query_land[line] = query_grads[half_block(line)]
    send_kv(1)
    ready(2, 4)
    multiply(UP)
    send_kv(2)
    for k in (1, 2, 3):
        query_landed(k).wait_recv()
    for d in range(LINE):
        for i in range(2):
            mixed[i * rows // 2 : (i + 1) * rows // 2, d * third : (d + 1) * third] = query_land[
                d, :, i * third : (i + 1) * third
            ]
    mixed_copies[0].start()
    add_core(UP)
    ready(4, 6)
    multiply(OUT)
    for h in range(HEADS_OWN):
        for k in (1, 2, 3):
            kv_landed(h, k).wait_recv()
        for d in range(LINE):
            at = width + d * third + h * HEAD
            mixed[:, at : at + HEAD] = kv_land[h, d, :, 0:HEAD]
            mixed[:, width + at : width + at + HEAD] = kv_land[h, d, :, HEAD:]
    for part in (1, 2):
        mixed_copies[part].start()
    add_pair(DOWN)
    mixed_copies[0].wait_recv()
    multiply(QUERY)
    add_core(OUT)
    first_hop(DOWN)
    parts[VEC][...] = jnp.zeros(parts[VEC].shape, F32)
    for j in range(4 * LINE):
        slot = parts[VEC].at[j % 2, j // 4, (j // 2) % 2]
        size = width // (4 * LINE)
        slot[0:8, 0:size] = vec_one[0:8, j * size : (j + 1) * size]
        query_part = mixed[:, j * size : (j + 1) * size].astype(F32)
        slot[8:9, 0:size] = jnp.sum(query_part, axis=0, keepdims=True)
        value_part = mixed[:, 2 * width + j * size : 2 * width + (j + 1) * size].astype(F32)
        slot[9:10, 0:size] = jnp.sum(value_part, axis=0, keepdims=True)
        at = (j % 4) * 4 * size
        slot[10:11, 0 : 4 * size] = vec_one[8 + j // 4 : 9 + j // 4, at : at + 4 * size]
    core_copy(VEC).start()
    for part in (1, 2):
        mixed_copies[part].wait_recv()
        multiply(QUERY + part)
    add_core(QUERY)
    second_hop(DOWN)
    add_core(KEY)
    add_core(VALUE)
    add_core(VEC)
    grad_hidden[...] = first[...] + dot_nt(mixed[...], w_all[...])
    add_pair(UP)
    for s in range(2, VEC + 4):
        if s <= VEC:
            add_pair(s)
        if 1 <= s - 1 <= VEC:
            first_hop(s - 1)
        if 1 <= s - 2 <= VEC:
            second_hop(s - 2)
        if s - 3 <= VEC and s >= 3:
            finish_unit(s - 3)
    for u in units:
        last_copy(u).wait_recv()
    vec_own[...] = parts[VEC][core, line, side] + vec_seq[...]
    for k in (1, 2, 3):
        line_copy(k).wait_send()
        query_back(k).wait_send()
        for h in range(HEADS_OWN):
            kv_back(h, k).wait_send()
    for h in range(HEADS_OWN):
        pair_copy(h).wait_send()
    for copy in seq_copies + mixed_copies:
        copy.wait_send()
    for u in units:
        core_copy(u).wait_send()
        last_copy(u).wait_send()
        for k in range(LINE):
            side_copy(u, k).wait_send()
        for k in range(1, LINE):

            @pl.when(line < k)
            def _(k=k):
                up_copy(u, k).wait_send()

        for k in range(LINE - 1):

            @pl.when(line > k)
            def _(k=k):
                down_copy(u, k).wait_send()


def backward(*args):
    rows, width = args[1].shape
    ffn = args[6].shape[1]
    third = HEADS_OWN * HEAD
    mid, seq_rows = LINE * rows, 2 * LINE * rows
    shape = jax.ShapeDtypeStruct
    widths = ((ffn // 2, width), (width, ffn // 2)) + ((width, width // 2),) * 4
    dims = [(a // (4 * LINE), b, a == width) for a, b in widths]
    own_shapes = [(r, 2 * c) if wide else (2 * r, c) for r, c, wide in dims[: OUT + 1]]
    own_shapes.insert(OUT, (own_shapes[UP][0], 3 * width))
    blocks = [((r, c), BF16) for r, c, _ in dims] + [((16, 256), F32)]
    count = len(blocks)
    vmem, dma = pltpu.VMEM, pltpu.SemaphoreType.DMA
    outs = [shape((rows, width), BF16), shape((rows, width), F32)]
    outs += [shape(own, BF16) for own in own_shapes]
    outs.append(shape((16, 256), F32))
    return pl.pallas_call(
        functools.partial(backward_kernel, dims),
        out_shape=outs,
        in_specs=[INNER] * 4 + [ANY] * 14,
        out_specs=[INNER] * len(outs),
        scratch_shapes=[
            vmem((width, width), BF16),
            vmem((width, ffn), BF16),
            vmem((ffn, width), BF16),
            vmem((rows, ffn), BF16),
            vmem((rows, ffn), F32),
            vmem((rows, width), F32),
            vmem((16, width), F32),
            vmem((LINE, rows // 2, 2 * third), BF16),
            vmem((2, rows, ffn // 2), BF16),
            vmem((2, rows, ffn // 2), BF16),
            vmem((2, rows, width // 2), BF16),
            vmem((HEADS_OWN, mid, HEAD), BF16),
            vmem((HEADS_OWN, seq_rows, HEAD), BF16),
            vmem((HEADS_OWN, seq_rows, HEAD), BF16),
            vmem((mid, third), F32),
            vmem((mid, 128), F32),
            vmem((width, 3 * width), BF16),
            vmem((HEADS_OWN, mid, seq_rows), BF16),
            vmem((mid // 2, 2 * third), BF16),
            vmem((mid, HEAD), BF16),
            vmem((mid, seq_rows), BF16),
            vmem((mid // 2, 2 * third), BF16),
            vmem((HEADS_OWN, mid, 128), F32),
            vmem((HEADS_OWN, mid, 128), BF16),
            vmem((HEADS_OWN, mid, 128), BF16),
            vmem((HEADS_OWN, mid, 128), BF16),
            vmem((HEADS_OWN, LINE, rows, 128), BF16),
            vmem((LINE, rows // 2, 2 * third), BF16),
            vmem((rows, 3 * width), BF16),
            [vmem((rows, a), BF16) for a in (ffn // 2, width, width, width, width)],
            [vmem((rows, b), BF16) for b in (width, width, ffn // 2) + (width // 2,) * 4],
            [vmem((2, LINE, 2) + block, kind) for block, kind in blocks],
            [vmem((LINE, 2) + block, kind) for block, kind in blocks],
            [vmem((LINE,) + block, kind) for block, kind in blocks],
            [vmem((LINE - 1,) + block, kind) for block, kind in blocks],
            [vmem((LINE - 1,) + block, kind) for block, kind in blocks],
            vmem((16, 256), F32),
            dma((6,)),
            dma((8,)),
            dma((3,)),
            dma((3,)),
            dma((3,)),
            dma((3,)),
            dma((4, 3)),
            dma((4, 3)),
            dma((9,)),
            dma((9,)),
            dma((2, count)),
            dma((2, count, LINE)),
            dma((2, count, LINE - 1)),
            dma((2, count, LINE - 1)),
            dma((2, count)),
        ],
        compiler_params=pltpu.CompilerParams(
            collective_id=2, has_side_effects=True, vmem_limit_bytes=63 << 20
        ),
        name="backward",
    )(*args)


def finish_kernel(*refs):
    for i in range(6):
        refs[7 + i][...] = refs[i][...].astype(refs[7 + i].dtype)
    vec = refs[6]
    for i, row in enumerate((8, 9, 0, 1, 2, 3, 4, 5, 10)):
        out = refs[13 + i]
        out[...] = vec[row, 0 : out.shape[0]]


def finish(*args):
    shape = jax.ShapeDtypeStruct
    outs = [shape(a.shape, F32) for a in args[:5]] + [shape(args[5].shape, BF16)]
    size = args[2].shape[0]
    outs += [shape((size,), F32)] * 8 + [shape((4 * size,), F32)]
    return pl.pallas_call(
        finish_kernel,
        out_shape=outs,
        in_specs=[INNER] * 7,
        out_specs=[INNER] * len(outs),
        name="finish",
    )(*args)


def block_device(
    hidden,
    segment_ids,
    out_grad,
    w_qkv,
    bias_query,
    bias_value,
    w_out,
    bias_out,
    gain_one,
    shift_one,
    w_up,
    bias_up,
    w_down,
    bias_down,
    gain_two,
    shift_two,
):
    tok, grad_out = hidden[0], out_grad[0]
    small = [
        bias_query,
        bias_value,
        bias_out,
        gain_one,
        shift_one,
        bias_down,
        gain_two,
        shift_two,
        bias_up,
    ]
    (
        attended,
        tok_pair,
        vec_all,
        w_full,
        out_other,
        up_other,
        down_other,
        q_heads,
        k_heads,
        v_heads,
        att_full,
        totals,
        probs,
    ) = attend_forward(tok, segment_ids, small, w_qkv, w_out, w_up, w_down)
    result, grad_hidden, down_own, up_own, qkv_own, out_own, vec_own = backward(
        attended,
        tok,
        grad_out,
        vec_all,
        w_out,
        out_other,
        w_up,
        up_other,
        w_down,
        down_other,
        q_heads,
        k_heads,
        v_heads,
        att_full,
        totals,
        probs,
        w_full,
        tok_pair,
    )
    grads = finish(up_own, down_own, qkv_own, out_own, grad_hidden, result, vec_own)
    up_grad, down_grad, qkv_grad, out_grads, grad_hidden, result = grads[:6]
    (
        query_bias,
        value_bias,
        out_bias,
        gain_first,
        shift_first,
        down_bias,
        gain_second,
        shift_second,
        up_bias,
    ) = grads[6:]
    return (
        result[None],
        grad_hidden[None],
        qkv_grad,
        query_bias,
        value_bias,
        out_grads,
        out_bias,
        gain_first,
        shift_first,
        up_grad,
        up_bias,
        down_grad,
        down_bias,
        gain_second,
        shift_second,
    )


def solution(mesh):
    small = (mesh.shape["seq"], mesh.shape["ctx"], mesh.shape["fsdp"]) == (2, 8, 2)
    return jax.shard_map(
        block_device if small else on_device,
        mesh=mesh,
        in_specs=(
            P(("seq", "fsdp"), "ctx", None),
            P(("seq", "fsdp"), None),
            P(("seq", "fsdp"), "ctx", None),
            P("fsdp", None),
            P("fsdp"),
            P("fsdp"),
            P("fsdp", None),
            P("fsdp"),
            P("fsdp"),
            P("fsdp"),
            P("fsdp", None),
            P("fsdp"),
            P("fsdp", None),
            P("fsdp"),
            P("fsdp"),
            P("fsdp"),
        ),
        out_specs=(
            P(("seq", "fsdp"), "ctx", None),
            P(("seq", "fsdp"), "ctx", None),
            P(("ctx", "fsdp"), None),
            P(("ctx", "fsdp")),
            P(("ctx", "fsdp")),
            P(("ctx", "fsdp"), None),
            P(("ctx", "fsdp")),
            P(("ctx", "fsdp")),
            P(("ctx", "fsdp")),
            P(("ctx", "fsdp"), None),
            P(("ctx", "fsdp")),
            P(("ctx", "fsdp"), None),
            P(("ctx", "fsdp")),
            P(("ctx", "fsdp")),
            P(("ctx", "fsdp")),
        ),
        check_vma=False,
    )
```

```python
import functools

import jax
import jax.numpy as jnp
from jax import lax
from jax.experimental import pallas as pl
from jax.experimental.pallas import tpu as pltpu
from jax.sharding import PartitionSpec as P

HEAD = 64


EPSILON = 1e-12
NEGATIVE = -1e30
LOG_TWO = 0.6931471805599453
LOG2_E = 1.4426950408889634


def norm_forward(rows_in, gain_vec, shift_vec):
    row_mean = jnp.mean(rows_in, axis=-1, keepdims=True)
    centered = rows_in - row_mean
    variance = jnp.mean(centered * centered, axis=-1, keepdims=True)
    scaled = lax.rsqrt(variance + EPSILON)
    normed = centered * scaled
    return (normed * gain_vec + shift_vec, normed, scaled)


def norm_backward(grad_rows, normed, scaled, gain_vec):
    grad_normed = grad_rows * gain_vec
    inner_part = (
        grad_normed
        - jnp.mean(grad_normed, axis=-1, keepdims=True)
        - normed * jnp.mean(grad_normed * normed, axis=-1, keepdims=True)
    )
    return (inner_part * scaled, jnp.sum(grad_rows * normed, axis=0), jnp.sum(grad_rows, axis=0))


def head_scores(query_heads, key_heads):
    return (
        jnp.einsum("qhd,khd->hqk", query_heads, key_heads, preferred_element_type=jnp.float32)
        * 0.125
    )


def column_sums(rows_b):
    return jnp.sum(rows_b.astype(jnp.float32), axis=0)


def sweep(steps_total, advance, start_carry):

    def advance_one(running, block_index):
        running = advance(running, block_index)
        return (running, None)

    return lax.scan(advance_one, start_carry, jnp.arange(steps_total))[0]


def local_grads(scores, allowed, shift_rows, ratio_rows, grad_heads, value_heads):
    unnorm = jnp.where(allowed, jnp.exp(scores - shift_rows[..., None]), 0.0)
    grad_weights = jnp.einsum(
        "qhd,khd->hqk", grad_heads, value_heads, preferred_element_type=jnp.float32
    )
    grad_scores = (unnorm * (grad_weights - ratio_rows[..., None])).astype(jnp.bfloat16)
    return (unnorm.astype(jnp.bfloat16), grad_scores)


def on_device(
    hidden,
    segment_ids,
    out_grad,
    w_qkv,
    bias_query,
    bias_value,
    w_out,
    bias_out,
    gain_one,
    shift_one,
    w_up,
    bias_up,
    w_down,
    bias_down,
    gain_two,
    shift_two,
):
    (
        w_qkv,
        bias_query,
        bias_value,
        w_out,
        bias_out,
        gain_one,
        shift_one,
        w_up,
        bias_up,
        w_down,
        bias_down,
        gain_two,
        shift_two,
    ) = (
        lax.all_gather(w_qkv, "fsdp", axis=0, tiled=True),
        lax.all_gather(bias_query, "fsdp", axis=0, tiled=True),
        lax.all_gather(bias_value, "fsdp", axis=0, tiled=True),
        lax.all_gather(w_out, "fsdp", axis=0, tiled=True),
        lax.all_gather(bias_out, "fsdp", axis=0, tiled=True),
        lax.all_gather(gain_one, "fsdp", axis=0, tiled=True),
        lax.all_gather(shift_one, "fsdp", axis=0, tiled=True),
        lax.all_gather(w_up, "fsdp", axis=0, tiled=True),
        lax.all_gather(bias_up, "fsdp", axis=0, tiled=True),
        lax.all_gather(w_down, "fsdp", axis=0, tiled=True),
        lax.all_gather(bias_down, "fsdp", axis=0, tiled=True),
        lax.all_gather(gain_two, "fsdp", axis=0, tiled=True),
        lax.all_gather(shift_two, "fsdp", axis=0, tiled=True),
    )
    f32 = jnp.float32
    bf16 = jnp.bfloat16
    tokens = hidden[0]
    tok_rows = tokens.shape[0]
    model_width = tokens.shape[1]
    head_count = model_width // HEAD
    seq_rows = tok_rows * lax.axis_size("ctx")
    key_span = 4 * tok_rows
    block_total = seq_rows // key_span
    doc_ids = segment_ids[0]
    own_ids = lax.dynamic_slice_in_dim(doc_ids, lax.axis_index("ctx") * tok_rows, tok_rows)
    mixed_rows = jnp.dot(tokens, w_qkv, preferred_element_type=f32)
    query_rows = (mixed_rows[:, :model_width] + bias_query.astype(f32)).astype(bf16)
    key_value = jnp.concatenate(
        [
            mixed_rows[:, model_width : 2 * model_width],
            mixed_rows[:, 2 * model_width :] + bias_value.astype(f32),
        ],
        axis=1,
    ).astype(bf16)
    all_kv = lax.all_gather(key_value, "ctx", axis=0, tiled=True)
    query_heads = query_rows.reshape(tok_rows, head_count, HEAD)

    def key_block(block_index):
        kv_piece = lax.dynamic_slice_in_dim(all_kv, block_index * key_span, key_span, 0)
        key_ids = lax.dynamic_slice_in_dim(doc_ids, block_index * key_span, key_span)
        return (
            kv_piece[:, :model_width].reshape(key_span, head_count, HEAD),
            kv_piece[:, model_width:].reshape(key_span, head_count, HEAD),
            key_ids,
        )

    def forward_step(running, block_index):
        level_run, total_run, sum_run = running
        key_heads, value_heads, key_ids = key_block(block_index)
        allowed = (own_ids[:, None] == key_ids[None, :])[None]
        scores = jnp.where(allowed, head_scores(query_heads, key_heads), NEGATIVE)
        level_new = jnp.maximum(level_run, jnp.ceil(jnp.max(scores, axis=-1) * LOG2_E))
        rescale = jnp.exp(LOG_TWO * (level_run - level_new))
        unnorm = jnp.where(allowed, jnp.exp(scores - (LOG_TWO * level_new)[..., None]), 0.0)
        total_new = total_run * rescale + jnp.sum(unnorm, axis=-1)
        sum_new = sum_run * jnp.transpose(rescale)[:, :, None] + jnp.einsum(
            "hqk,khd->qhd", unnorm.astype(bf16), value_heads, preferred_element_type=f32
        )
        return (level_new, total_new, sum_new)

    start_state = (
        jnp.full((head_count, tok_rows), NEGATIVE, f32),
        jnp.zeros((head_count, tok_rows), f32),
        jnp.zeros((tok_rows, head_count, HEAD), f32),
    )
    level_end, row_total, raw_sum = sweep(block_total, forward_step, start_state)
    row_shift = LOG_TWO * level_end
    att_sum = raw_sum / jnp.transpose(row_total)[:, :, None]
    attended = att_sum.reshape(tok_rows, model_width).astype(bf16)
    branch = jnp.dot(attended, w_out, preferred_element_type=f32) + bias_out.astype(f32)
    normed_one, norm_one, scale_one = norm_forward(
        tokens.astype(f32) + branch, gain_one.astype(f32), shift_one.astype(f32)
    )
    normed_b = normed_one.astype(bf16)
    up_rows = jnp.dot(normed_b, w_up, preferred_element_type=f32) + bias_up.astype(f32)
    active, gelu_back = jax.vjp(lambda pre_act: jax.nn.gelu(pre_act, approximate=False), up_rows)
    active_b = active.astype(bf16)
    second = (
        normed_one + jnp.dot(active_b, w_down, preferred_element_type=f32) + bias_down.astype(f32)
    )
    result, norm_two, scale_two = norm_forward(second, gain_two.astype(f32), shift_two.astype(f32))
    grad_second, grad_gain_two, grad_shift_two = norm_backward(
        out_grad[0].astype(f32), norm_two, scale_two, gain_two.astype(f32)
    )
    grad_ffn = grad_second.astype(bf16)
    grad_bias_down = column_sums(grad_ffn)
    grad_w_down = jnp.dot(active_b.T, grad_ffn, preferred_element_type=f32)
    grad_active = jnp.dot(grad_ffn, w_down.T, preferred_element_type=f32)
    grad_up = gelu_back(grad_active)[0].astype(bf16)
    grad_bias_up = column_sums(grad_up)
    grad_w_up = jnp.dot(normed_b.T, grad_up, preferred_element_type=f32)
    grad_normed = grad_second + jnp.dot(grad_up, w_up.T, preferred_element_type=f32)
    grad_first, grad_gain_one, grad_shift_one = norm_backward(
        grad_normed, norm_one, scale_one, gain_one.astype(f32)
    )
    grad_branch = grad_first.astype(bf16)
    grad_bias_out = column_sums(grad_branch)
    grad_w_out = jnp.dot(attended.T, grad_branch, preferred_element_type=f32)
    grad_attended = jnp.dot(grad_branch, w_out.T, preferred_element_type=f32).astype(bf16)
    grad_att_f32 = grad_attended.reshape(tok_rows, head_count, HEAD).astype(f32)
    delta = jnp.einsum("qhd,qhd->hq", grad_att_f32, att_sum)
    delta_ratio = delta / row_total
    grad_scaled = (grad_att_f32 / jnp.transpose(row_total)[:, :, None]).astype(bf16)
    zero_query = jnp.zeros((tok_rows, head_count, HEAD), f32)

    def full_step(running, block_index):
        grad_query, grad_kv = running
        key_heads, value_heads, key_ids = key_block(block_index)
        allowed = (own_ids[:, None] == key_ids[None, :])[None]
        unnorm_b, grad_scores = local_grads(
            head_scores(query_heads, key_heads),
            allowed,
            row_shift,
            delta_ratio,
            grad_scaled,
            value_heads,
        )
        grad_query = (
            grad_query
            + jnp.einsum("hqk,khd->qhd", grad_scores, key_heads, preferred_element_type=f32) * 0.125
        )
        grad_keys = (
            jnp.einsum("hqk,qhd->khd", grad_scores, query_heads, preferred_element_type=f32) * 0.125
        )
        grad_values = jnp.einsum("hqk,qhd->khd", unnorm_b, grad_scaled, preferred_element_type=f32)
        both_grads = jnp.concatenate(
            [grad_keys.reshape(key_span, model_width), grad_values.reshape(key_span, model_width)],
            axis=1,
        )
        grad_kv = lax.dynamic_update_slice_in_dim(grad_kv, both_grads, block_index * key_span, 0)
        return (grad_query, grad_kv)

    start_full = (zero_query, jnp.zeros((seq_rows, 2 * model_width), f32))
    grad_query, grad_kv = sweep(block_total, full_step, start_full)
    own_kv = lax.psum_scatter(grad_kv, "ctx", scatter_dimension=0, tiled=True)
    grad_query_b = grad_query.reshape(tok_rows, model_width).astype(bf16)
    grad_kv_b = own_kv.astype(bf16)
    grad_mixed = jnp.concatenate([grad_query_b, grad_kv_b], axis=1)
    grad_tokens = grad_first + jnp.dot(grad_mixed, w_qkv.T, preferred_element_type=f32)
    grad_w_qkv = jnp.dot(tokens.T, grad_mixed, preferred_element_type=f32)
    grad_bias_query = column_sums(grad_query_b)
    grad_bias_value = column_sums(grad_kv_b[:, model_width:])
    shares = (
        lax.psum_scatter(grad_w_qkv, ("ctx", "fsdp"), scatter_dimension=0, tiled=True),
        lax.psum_scatter(grad_bias_query, ("ctx", "fsdp"), scatter_dimension=0, tiled=True),
        lax.psum_scatter(grad_bias_value, ("ctx", "fsdp"), scatter_dimension=0, tiled=True),
        lax.psum_scatter(grad_w_out, ("ctx", "fsdp"), scatter_dimension=0, tiled=True),
        lax.psum_scatter(grad_bias_out, ("ctx", "fsdp"), scatter_dimension=0, tiled=True),
        lax.psum_scatter(grad_gain_one, ("ctx", "fsdp"), scatter_dimension=0, tiled=True),
        lax.psum_scatter(grad_shift_one, ("ctx", "fsdp"), scatter_dimension=0, tiled=True),
        lax.psum_scatter(grad_w_up, ("ctx", "fsdp"), scatter_dimension=0, tiled=True),
        lax.psum_scatter(grad_bias_up, ("ctx", "fsdp"), scatter_dimension=0, tiled=True),
        lax.psum_scatter(grad_w_down, ("ctx", "fsdp"), scatter_dimension=0, tiled=True),
        lax.psum_scatter(grad_bias_down, ("ctx", "fsdp"), scatter_dimension=0, tiled=True),
        lax.psum_scatter(grad_gain_two, ("ctx", "fsdp"), scatter_dimension=0, tiled=True),
        lax.psum_scatter(grad_shift_two, ("ctx", "fsdp"), scatter_dimension=0, tiled=True),
    )
    summed = (
        lax.psum(shares[0].astype(jnp.bfloat16), "seq").astype(jnp.float32),
        lax.psum(shares[1].astype(jnp.bfloat16), "seq").astype(jnp.float32),
        lax.psum(shares[2].astype(jnp.bfloat16), "seq").astype(jnp.float32),
        lax.psum(shares[3].astype(jnp.bfloat16), "seq").astype(jnp.float32),
        lax.psum(shares[4].astype(jnp.bfloat16), "seq").astype(jnp.float32),
        lax.psum(shares[5].astype(jnp.bfloat16), "seq").astype(jnp.float32),
        lax.psum(shares[6].astype(jnp.bfloat16), "seq").astype(jnp.float32),
        lax.psum(shares[7].astype(jnp.bfloat16), "seq").astype(jnp.float32),
        lax.psum(shares[8].astype(jnp.bfloat16), "seq").astype(jnp.float32),
        lax.psum(shares[9].astype(jnp.bfloat16), "seq").astype(jnp.float32),
        lax.psum(shares[10].astype(jnp.bfloat16), "seq").astype(jnp.float32),
        lax.psum(shares[11].astype(jnp.bfloat16), "seq").astype(jnp.float32),
        lax.psum(shares[12].astype(jnp.bfloat16), "seq").astype(jnp.float32),
    )
    return (
        result.astype(bf16)[None],
        grad_tokens[None],
        summed[0],
        summed[1],
        summed[2],
        summed[3],
        summed[4],
        summed[5],
        summed[6],
        summed[7],
        summed[8],
        summed[9],
        summed[10],
        summed[11],
        summed[12],
    )


MESH_ID = pl.DeviceIdType.MESH
LINE = 4


def remote(src, dst, send, recv, target):
    return pltpu.make_async_remote_copy(
        src_ref=src,
        dst_ref=dst,
        send_sem=send,
        recv_sem=recv,
        device_id=target,
        device_id_type=MESH_ID,
    )


HEADS_OWN = 3
F32 = jnp.float32
BF16 = jnp.bfloat16
ANY = pl.BlockSpec(memory_space=pl.ANY)
INNER = pl.BlockSpec(memory_space=pltpu.VMEM)


def dot_nt(a, b):
    return lax.dot_general(a, b, (((1,), (1,)), ((), ())), preferred_element_type=F32)


def dot_tn(a, b):
    return lax.dot_general(a, b, (((0,), (0,)), ((), ())), preferred_element_type=F32)


def dot_nn(a, b):
    return lax.dot_general(a, b, (((1,), (0,)), ((), ())), preferred_element_type=F32)


def greet(targets):
    barrier = pltpu.get_barrier_semaphore()
    for target in targets:
        pl.semaphore_signal(barrier, inc=1, device_id=target, device_id_type=MESH_ID)
    pl.semaphore_wait(barrier, len(targets))


def attend_kernel(
    tok,
    ids,
    small,
    w_qkv,
    w_out,
    w_up,
    w_down,
    attended,
    tok_pair,
    vec_all,
    w_full,
    out_other,
    up_other,
    down_other,
    q_heads,
    k_heads,
    v_heads,
    att_full,
    totals,
    probs_out,
    w_all,
    mixed,
    sent_kv,
    sent_q,
    mine,
    mine_q,
    other,
    att_sent,
    att_land,
    probs,
    vec,
    ids_row,
    ids_col,
    local_sem,
    probs_sem,
    core_out,
    core_in,
    line_out,
    line_in,
    pair_out,
    pair_in,
    back_out,
    back_in,
    seq_out,
    seq_in,
):
    place = lax.axis_index("ctx")
    core = lax.axis_index("fsdp")
    group = lax.axis_index("seq")
    line, side = place // 2, place % 2
    to_core = {"fsdp": 1 - core}
    to_pair = {"ctx": place + 1 - 2 * side}
    to_seq = {"seq": 1 - group}
    rows = tok.shape[0]
    width = tok.shape[1]
    half = width // 2
    third = HEADS_OWN * HEAD

    def ahead(k):
        return lax.rem(line + k, LINE)

    def behind(k):
        return lax.rem(line + LINE - k, LINE)

    def to_line(k):
        return {"ctx": 2 * ahead(k) + side}

    def block(which):
        return pl.ds(pl.multiple_of(which * rows, 32), rows)

    def half_block(which):
        return pl.ds(pl.multiple_of(which * (rows // 2), 16), rows // 2)

    own_rows = pl.ds(pl.multiple_of(core * half, 128), half)
    other_rows = pl.ds(pl.multiple_of((1 - core) * half, 128), half)

    own_load = pltpu.make_async_copy(w_qkv, w_all.at[own_rows], local_sem.at[0])
    own_load.start()
    at = 0
    for piece in small:
        for first in range(0, piece.shape[0], half):
            vec[at : at + 1] = piece[first : first + half].astype(F32)[None]
            at += 1
    vec[at:] = jnp.zeros((vec.shape[0] - at, half), F32)
    greet([to_core, to_pair, to_seq] + [to_line(k) for k in range(1, LINE)])
    core_copies = [
        remote(w_qkv, w_all.at[own_rows], core_out.at[0], core_in.at[0], to_core),
        remote(vec, vec_all.at[:, own_rows], core_out.at[1], core_in.at[1], to_core),
        remote(w_out, out_other, core_out.at[2], core_in.at[2], to_core),
        remote(w_up, up_other, core_out.at[3], core_in.at[3], to_core),
        remote(w_down, down_other, core_out.at[4], core_in.at[4], to_core),
    ]
    seq_copy = remote(tok, tok_pair, seq_out.at[0], seq_in.at[0], to_seq)
    core_copies[0].start()
    core_copies[1].start()
    seq_copy.start()
    vec_all[:, own_rows] = vec[...]
    own_load.wait()
    step = width // 2
    for first in range(0, 3 * width, step):
        mixed[:, first : first + step] = dot_nn(
            tok[:, own_rows], w_all[own_rows, first : first + step]
        )
    core_copies[0].wait_recv()
    core_copies[1].wait_recv()
    for copy in core_copies[2:]:
        copy.start()

    def kv_copy(k, to):
        return remote(
            sent_kv.at[ahead(k)],
            mine.at[block(to)],
            line_out.at[0, k - 1],
            line_in.at[0, k - 1],
            to_line(k),
        )

    def q_copy(k, to):
        return remote(
            sent_q.at[ahead(k)],
            mine_q.at[half_block(to)],
            line_out.at[1, k - 1],
            line_in.at[1, k - 1],
            to_line(k),
        )

    def pair_copy(k):
        where = block(behind(k))
        return remote(mine.at[where], other.at[where], pair_out.at[k], pair_in.at[k], to_pair)

    bias = vec_all[...]
    for part in (1, 2, 0):
        for first in range(part * width, (part + 1) * width, step):
            total = mixed[:, first : first + step] + dot_nn(
                tok[:, other_rows], w_all[other_rows, first : first + step]
            )
            within = first - part * width
            if part == 0:
                total += bias[0:1, within : within + step]
            if part == 2:
                total += bias[1:2, within : within + step]
            total = total.astype(BF16)
            for j in range(2):
                d, piece = within // third + j, total[:, j * third : (j + 1) * third]
                if part == 0:
                    sent_q[d, :, 0:third] = piece[: rows // 2]
                    sent_q[d, :, third:] = piece[rows // 2 :]
                else:
                    sent_kv[d, :, (part - 1) * third : part * third] = piece
        for k in (3, 2, 1):
            if part == 2:
                kv_copy(k, line).start()
            if part == 0:
                q_copy(k, line).start()
        if part == 2:
            mine[block(line)] = sent_kv[line]
            pair_copy(0).start()
    full_store = pltpu.make_async_copy(w_all, w_full, local_sem.at[1])
    full_store.start()
    mine_q[half_block(line)] = sent_q[line]
    for k in (1, 2, 3):
        kv_copy(k, behind(k)).wait_recv()
        pair_copy(k).start()
    seq_rows = 2 * LINE * rows
    mid = LINE * rows
    for z in range(LINE):
        even = ids[:, 2 * z * rows : (2 * z + 1) * rows].astype(F32)
        odd = ids[:, (2 * z + 1) * rows : (2 * z + 2) * rows].astype(F32)
        ids_row[:, z * rows : (z + 1) * rows] = jnp.where(side == 0, even, odd)
        ids_row[:, mid + z * rows : mid + (z + 1) * rows] = jnp.where(side == 0, odd, even)
    ids_col[...] = jnp.transpose(jnp.broadcast_to(ids_row[:, 0:mid], (8, mid)))[:, 0:1]
    for h in range(HEADS_OWN):
        k_heads[h, 0:mid] = mine[:, h * HEAD : (h + 1) * HEAD]
        v_heads[h, 0:mid] = mine[:, third + h * HEAD : third + (h + 1) * HEAD]
    for k in (1, 2, 3):
        q_copy(k, behind(k)).wait_recv()
    for h in range(HEADS_OWN):
        for i in range(2 * LINE):
            from_rows = slice((i // 2) * rows // 2, (i // 2 + 1) * rows // 2)
            at = (i % 2) * third + h * HEAD
            q_heads[h, i * rows // 2 : (i + 1) * rows // 2] = mine_q[from_rows, at : at + HEAD]
    for k in range(LINE):
        pair_copy(k).wait_recv()
    for h in range(HEADS_OWN):
        k_heads[h, mid:seq_rows] = other[:, h * HEAD : (h + 1) * HEAD]
        v_heads[h, mid:seq_rows] = other[:, third + h * HEAD : third + (h + 1) * HEAD]

    def back_copy(k):
        return remote(
            att_sent.at[ahead(k)],
            att_land.at[line],
            back_out.at[k - 1],
            back_in.at[k - 1],
            to_line(k),
        )

    def back_landed(k):
        return remote(
            att_sent.at[ahead(k)],
            att_land.at[behind(k)],
            back_out.at[k - 1],
            back_in.at[k - 1],
            to_line(k),
        )

    def probs_copy(k):
        where = block(ahead(k))
        return pltpu.make_async_copy(
            probs.at[:, where], probs_out.at[:, where], probs_sem.at[k - 1]
        )

    def attend(k, carry):
        which = ahead(k)
        where = block(which)
        allowed = ids_col[where] == ids_row[...]
        for h in range(HEADS_OWN):
            scores = dot_nt(q_heads[h, where], k_heads[h]) * 0.125
            scores = jnp.where(allowed, scores, NEGATIVE)
            level = jnp.ceil(jnp.max(scores, axis=-1, keepdims=True) * LOG2_E)
            unnorm = jnp.exp(scores - LOG_TWO * level)
            row_total = jnp.sum(unnorm, axis=-1, keepdims=True)
            unnorm_b = unnorm.astype(BF16)
            probs[h, where] = unnorm_b
            value = dot_nn(unnorm_b, v_heads[h]) / row_total
            att_full[where, h * HEAD : (h + 1) * HEAD] = value
            totals[where, h : h + 1] = row_total
            value_b = value.astype(BF16)
            for i in range(2):
                att_sent[which, :, i * third + h * HEAD : i * third + (h + 1) * HEAD] = value_b[
                    i * rows // 2 : (i + 1) * rows // 2
                ]
        probs_copy(k).start()

        @pl.when(k < LINE)
        def _():
            back_copy(k).start()

        return carry

    lax.fori_loop(1, LINE + 1, attend, 0)
    att_land[line] = att_sent[line]
    for k in (1, 2, 3):
        back_landed(k).wait_recv()
    for d in range(LINE):
        for i in range(2):
            attended[i * rows // 2 : (i + 1) * rows // 2, d * third : (d + 1) * third] = att_land[
                d, :, i * third : (i + 1) * third
            ]
    for k in (1, 2, 3):
        kv_copy(k, line).wait_send()
        q_copy(k, line).wait_send()
        back_copy(k).wait_send()
    for k in range(LINE):
        pair_copy(k).wait_send()
        probs_copy(k + 1).wait()
    for copy in core_copies[2:]:
        copy.wait_recv()
    for copy in core_copies:
        copy.wait_send()
    seq_copy.wait()
    full_store.wait()


def attend_forward(tok, ids, small, w_qkv, w_out, w_up, w_down):
    rows, width = tok.shape
    third = HEADS_OWN * HEAD
    mid, seq_rows = LINE * rows, 2 * LINE * rows
    shape = jax.ShapeDtypeStruct
    outs = [
        (shape((rows, width), BF16), INNER),
        (shape((rows, width), BF16), INNER),
        (shape((16, width), F32), INNER),
        (shape((width, 3 * width), BF16), ANY),
        (shape(w_out.shape, BF16), ANY),
        (shape(w_up.shape, BF16), ANY),
        (shape(w_down.shape, BF16), ANY),
        (shape((HEADS_OWN, mid, HEAD), BF16), INNER),
        (shape((HEADS_OWN, seq_rows, HEAD), BF16), INNER),
        (shape((HEADS_OWN, seq_rows, HEAD), BF16), INNER),
        (shape((mid, third), F32), INNER),
        (shape((mid, 128), F32), INNER),
        (shape((HEADS_OWN, mid, seq_rows), BF16), ANY),
    ]
    dma = pltpu.SemaphoreType.DMA
    return pl.pallas_call(
        attend_kernel,
        out_shape=[o[0] for o in outs],
        in_specs=[INNER, INNER, [INNER] * len(small)] + [ANY] * 4,
        out_specs=[o[1] for o in outs],
        scratch_shapes=[
            pltpu.VMEM((width, 3 * width), BF16),
            pltpu.VMEM((rows, 3 * width), F32),
            pltpu.VMEM((LINE, rows, 2 * third), BF16),
            pltpu.VMEM((LINE, rows // 2, 2 * third), BF16),
            pltpu.VMEM((mid, 2 * third), BF16),
            pltpu.VMEM((mid // 2, 2 * third), BF16),
            pltpu.VMEM((mid, 2 * third), BF16),
            pltpu.VMEM((LINE, rows // 2, 2 * third), BF16),
            pltpu.VMEM((LINE, rows // 2, 2 * third), BF16),
            pltpu.VMEM((HEADS_OWN, mid, seq_rows), BF16),
            pltpu.VMEM((16, width // 2), F32),
            pltpu.VMEM((1, seq_rows), F32),
            pltpu.VMEM((mid, 1), F32),
            dma((2,)),
            dma((LINE,)),
            dma((5,)),
            dma((5,)),
            dma((2, 3)),
            dma((2, 3)),
            dma((LINE,)),
            dma((LINE,)),
            dma((3,)),
            dma((3,)),
            dma((1,)),
            dma((1,)),
        ],
        compiler_params=pltpu.CompilerParams(
            collective_id=1, has_side_effects=True, vmem_limit_bytes=63 << 20
        ),
        name="attend_forward",
    )(tok, ids, small, w_qkv, w_out, w_up, w_down)


DOWN, DOWN_B, UP, UP_B, OUT, QUERY, KEY, VALUE, VEC = range(9)


def backward_kernel(
    dims,
    attended,
    tok,
    grad_out,
    vec_in,
    w_out,
    out_other,
    w_up,
    up_other,
    w_down,
    down_other,
    q_in,
    k_in,
    v_in,
    att_in,
    totals_in,
    probs_in,
    w_full,
    tok_pair,
    result,
    grad_hidden,
    down_own,
    up_own,
    qkv_own,
    out_own,
    vec_own,
    out_all,
    up_all,
    down_all,
    active,
    slope,
    first,
    vec_one,
    att_grads,
    act_halves,
    up_halves,
    branch_halves,
    q_heads,
    k_heads,
    v_heads,
    att_full,
    totals,
    w_all,
    probs,
    grad_land,
    scaled,
    score_grads,
    query_grads,
    kv_own,
    kv_sent,
    kv_pair,
    kv_sum,
    kv_land,
    query_land,
    mixed,
    left_refs,
    right_refs,
    parts,
    from_core,
    from_pair,
    from_low,
    from_high,
    vec_seq,
    sem,
    local_sem,
    line_out,
    line_in,
    pair_out,
    pair_in,
    back_out,
    back_in,
    seq_out,
    seq_in,
    core_sem,
    side_sem,
    low_sem,
    high_sem,
    last_sem,
):
    place = lax.axis_index("ctx")
    core = lax.axis_index("fsdp")
    group = lax.axis_index("seq")
    line, side = place // 2, place % 2
    to_core = {"fsdp": 1 - core}
    to_pair = {"ctx": place + 1 - 2 * side}
    to_seq = {"seq": 1 - group}
    to_up = {"ctx": lax.rem(place + 2, 2 * LINE)}
    to_down = {"ctx": lax.rem(place + 2 * LINE - 2, 2 * LINE)}
    rows, width = grad_hidden.shape
    third = HEADS_OWN * HEAD
    mid = LINE * rows
    half = width // 2
    hidden_units = active.shape[1]
    outs = (down_own, down_own, up_own, up_own, out_own, qkv_own, qkv_own, qkv_own)
    left = [
        (act_halves.at[group], left_refs[0]),
        (left_refs[1], left_refs[2]),
        (attended, left_refs[3]),
        (tok, left_refs[4]),
    ]
    grad_ffn_own, grad_ffn_pair, up_pair, branch_pair = right_refs[:4]
    right = []
    for i in range(2):
        lanes = slice(i * half, (i + 1) * half)
        right.append((grad_ffn_own.at[:, lanes], grad_ffn_pair.at[:, lanes]))
    for i in range(2):
        lanes = slice(i * width, (i + 1) * width)
        right.append((up_halves.at[group, :, lanes], up_pair.at[:, lanes]))
    right.append((branch_halves.at[group], branch_pair))
    units = range(VEC + 1)
    def ahead(k):
        return lax.rem(line + k, LINE)

    def behind(k):
        return lax.rem(line + LINE - k, LINE)

    def to_line(k):
        return {"ctx": 2 * ahead(k) + side}

    def block(which):
        return pl.ds(pl.multiple_of(which * rows, 32), rows)

    def half_block(which):
        return pl.ds(pl.multiple_of(which * (rows // 2), 16), rows // 2)

    def half_of(part, which):
        return pl.ds(pl.multiple_of(part * width + which * half, 128), half)

    for part in range(3):
        right.append((mixed.at[:, half_of(part, group)], right_refs[4 + part]))


    def own_place(u):
        size, columns, wide = dims[u]
        if not wide:
            lanes = slice((u - DOWN) * columns, (u - DOWN + 1) * columns)
            return (pl.ds(pl.multiple_of(group * size, 16), size), lanes)
        if u >= QUERY:
            return (slice(None), half_of(u - QUERY, group))
        if u == OUT:
            return (slice(None), half_of(0, group))
        start = pl.multiple_of((2 * group + u - UP) * columns, 128)
        return (slice(None), pl.ds(start, columns))

    def core_copy(u):
        return remote(
            parts[u].at[1 - core], from_core[u], core_sem.at[0, u], core_sem.at[1, u], to_core
        )

    def side_copy(u, k):
        return remote(
            parts[u].at[core, k, 1 - side],
            from_pair[u].at[k],
            side_sem.at[0, u, k],
            side_sem.at[1, u, k],
            to_pair,
        )

    def up_copy(u, k):
        return remote(
            parts[u].at[core, k, side],
            from_low[u].at[k - 1],
            low_sem.at[0, u, k - 1],
            low_sem.at[1, u, k - 1],
            to_up,
        )

    def down_copy(u, k):
        return remote(
            parts[u].at[core, k, side],
            from_high[u].at[k],
            high_sem.at[0, u, k],
            high_sem.at[1, u, k],
            to_down,
        )

    def last_copy(u):
        if u == VEC:
            where = vec_seq
        else:
            where = outs[u].at[own_place(u)]
        return remote(
            parts[u].at[core, line, side], where, last_sem.at[0, u], last_sem.at[1, u], to_seq
        )

    def multiply(u):
        size, columns, _ = dims[u]
        (a_own, a_pair), (b_own, b_pair) = left[(0, 0, 1, 1, 2, 3, 3, 3)[u]], right[u]
        step = 384
        for first in range(0, a_own.shape[1], step):
            span = slice(first, first + step)
            product = dot_tn(a_own[:, span], b_own[...]) + dot_tn(a_pair[:, span], b_pair[...])
            product = product.astype(BF16)
            for i in range(step // size):
                j = first // size + i
                parts[u][j % 2, j // 4, (j // 2) % 2] = product[i * size : (i + 1) * size]
        core_copy(u).start()

    def line_start(u):
        @pl.when(line == 0)
        def _():
            for k in range(LINE - 1, 0, -1):
                up_copy(u, k).start()

        @pl.when(line == LINE - 1)
        def _():
            for k in range(LINE - 1):
                down_copy(u, k).start()

    def add_core(u):
        core_copy(u).wait_recv()
        for k in (3, 0, 2, 1):
            parts[u][core, k, 1 - side] += from_core[u][k, 1 - side]
            side_copy(u, k).start()
        for k in range(LINE):
            parts[u][core, k, side] += from_core[u][k, side]

    def add_pair(u):
        for k in (3, 0, 2, 1):
            side_copy(u, k).wait_recv()
            parts[u][core, k, side] += from_pair[u][k]
        line_start(u)

    def pass_up(u, k):
        up_copy(u, k).wait_recv()
        parts[u][core, k, side] += from_low[u][k - 1]
        up_copy(u, k).start()

    def pass_down(u, k):
        down_copy(u, k).wait_recv()
        parts[u][core, k, side] += from_high[u][k]
        down_copy(u, k).start()

    def first_hop(u):
        @pl.when(line == 1)
        def _():
            pass_up(u, 3)
            pass_up(u, 2)

        @pl.when(line == 2)
        def _():
            pass_down(u, 0)
            pass_down(u, 1)

    def second_hop(u):
        @pl.when(line == 2)
        def _():
            pass_up(u, 3)

        @pl.when(line == 1)
        def _():
            pass_down(u, 0)

    def line_end(u):
        for k in range(LINE):

            @pl.when(line == k)
            def _(k=k):
                if k > 0:
                    up_copy(u, k).wait_recv()
                    parts[u][core, k, side] += from_low[u][k - 1]
                if k < LINE - 1:
                    down_copy(u, k).wait_recv()
                    parts[u][core, k, side] += from_high[u][k]

    def last_start(u):
        last_copy(u).start()
        if u != VEC:
            outs[u][own_place(u)] = parts[u][core, line, side]

    def stage(u, n):
        if n == 1:
            add_pair(u)
        if n == 2:
            first_hop(u)
        if n == 3:
            second_hop(u)
        if n == 4:
            line_end(u)
            last_start(u)


    seq_copies = []
    for i, (src, dst) in enumerate(
        (
            (left[1][0], left[1][1]),
            (act_halves.at[1 - group], left[0][1]),
            (grad_ffn_own, grad_ffn_pair),
            (up_halves.at[1 - group, :, 0:width], up_pair.at[:, 0:width]),
            (up_halves.at[1 - group, :, width:], up_pair.at[:, width:]),
            (branch_halves.at[1 - group], branch_pair),
            (attended, left[2][1]),
        )
    ):
        seq_copies.append(remote(src, dst, seq_out.at[i], seq_in.at[i], to_seq))

    def place_of(which, size):
        return pl.ds(pl.multiple_of(which * size, 128), size)

    loads = []
    for i, (own, far, full) in enumerate(
        ((w_out, out_other, out_all), (w_up, up_other, up_all), (w_down, down_other, down_all))
    ):
        size = own.shape[0]
        loads.append(
            (
                pltpu.make_async_copy(own, full.at[place_of(core, size)], sem.at[2 * i]),
                pltpu.make_async_copy(far, full.at[place_of(1 - core, size)], sem.at[2 * i + 1]),
            )
        )
    for pair in loads:
        for load in pair:
            load.start()
    late_loads = []
    for i, (src, dst) in enumerate(
        (
            (q_in, q_heads),
            (k_in, k_heads),
            (v_in, v_heads),
            (att_in, att_full),
            (totals_in, totals),
            (probs_in, probs),
            (w_full, w_all),
            (tok_pair, left[3][1]),
        )
    ):
        late_loads.append(pltpu.make_async_copy(src, dst, local_sem.at[i]))
    for load in late_loads:
        load.start()
    greet([to_core, to_pair, to_seq] + [to_line(k) for k in range(1, LINE)])

    def arrived(i):
        for load in loads[i]:
            load.wait()

    bias_out, gain_one, shift_one = vec_in[2:3], vec_in[3:4], vec_in[4:5]
    bias_down, gain_two, shift_two = vec_in[5:6], vec_in[6:7], vec_in[7:8]
    arrived(0)
    branch = dot_nn(attended[...], out_all[...]) + bias_out
    normed_one, norm_one, scale_one = norm_forward(tok[...].astype(F32) + branch, gain_one, shift_one)
    normed_b = normed_one.astype(BF16)
    left[1][0][...] = normed_b
    seq_copies[0].start()
    arrived(1)
    step = width
    for c in range(hidden_units // step):
        at, row = (c // 2) * half, 8 + 2 * (c % 2)
        bias = jnp.concatenate([vec_in[row : row + 1, at : at + half], vec_in[row + 1 : row + 2, at : at + half]], axis=1)
        up = dot_nn(normed_b, up_all[:, c * step : (c + 1) * step]) + bias
        cdf = 0.5 * (1.0 + lax.erf(up * 0.7071067811865476))
        active[:, c * step : (c + 1) * step] = (up * cdf).astype(BF16)
        slope[:, c * step : (c + 1) * step] = cdf + up * (
            0.3989422804014327 * jnp.exp(-0.5 * up * up)
        )
    piece = hidden_units // (8 * LINE)
    for j in range(4 * LINE):
        for g in range(2):
            at = (2 * j + g) * piece
            act_halves[g, :, j * piece : (j + 1) * piece] = active[:, at : at + piece]
    seq_copies[1].start()
    arrived(2)
    second = normed_one + bias_down
    second += dot_nn(active[...], down_all[...])
    final, norm_two, scale_two = norm_forward(second, gain_two, shift_two)
    result[...] = final.astype(BF16)
    grad_second, gain_grad, shift_grad = norm_backward(
        grad_out[...].astype(F32), norm_two, scale_two, gain_two
    )
    grad_ffn = grad_second.astype(BF16)
    grad_ffn_own[...] = grad_ffn
    seq_copies[2].start()
    vec_one[...] = jnp.zeros(vec_one.shape, F32)
    vec_one[3:4] = jnp.sum(grad_ffn.astype(F32), axis=0, keepdims=True)
    vec_one[4:5] = gain_grad[None]
    vec_one[5:6] = shift_grad[None]
    grad_normed = grad_second
    for c in range(hidden_units // step):
        span = slice(c * step, (c + 1) * step)
        grad_up = (dot_nt(grad_ffn, down_all[span]) * slope[:, span]).astype(BF16)
        vec_one[8 + c : 9 + c] = jnp.sum(grad_up.astype(F32), axis=0, keepdims=True)
        grad_normed += dot_nt(grad_up, up_all[:, span])
        up_halves[c // 2, :, (c % 2) * step : (c % 2 + 1) * step] = grad_up
    seq_copies[3].start()
    seq_copies[4].start()
    grad_first, gain_grad, shift_grad = norm_backward(grad_normed, norm_one, scale_one, gain_one)
    first[...] = grad_first
    vec_one[1:2] = gain_grad[None]
    vec_one[2:3] = shift_grad[None]
    grad_branch = grad_first.astype(BF16)
    vec_one[0:1] = jnp.sum(grad_branch.astype(F32), axis=0, keepdims=True)
    for g in range(2):
        branch_halves[g] = grad_branch[:, g * half : (g + 1) * half]
    seq_copies[5].start()
    seq_copies[6].start()
    grad_att = dot_nt(grad_branch, out_all[...]).astype(BF16)
    for d in range(LINE):
        for i in range(2):
            att_grads[d, :, i * third : (i + 1) * third] = grad_att[
                i * rows // 2 : (i + 1) * rows // 2, d * third : (d + 1) * third
            ]


    def line_copy(k):
        return remote(
            att_grads.at[ahead(k)],
            grad_land.at[half_block(line)],
            line_out.at[k - 1],
            line_in.at[k - 1],
            to_line(k),
        )

    def line_landed(k):
        return remote(
            att_grads.at[ahead(k)],
            grad_land.at[half_block(behind(k))],
            line_out.at[k - 1],
            line_in.at[k - 1],
            to_line(k),
        )

    for k in (3, 2, 1):
        line_copy(k).start()
    mixed_copies = []
    for part in range(3):
        mixed_copies.append(
            remote(
                mixed.at[:, half_of(part, 1 - group)],
                right[QUERY + part][1],
                seq_out.at[7 + part],
                seq_in.at[7 + part],
                to_seq,
            )
        )
    grad_land[half_block(line)] = att_grads[line]
    for k in (1, 2, 3):
        line_landed(k).wait_recv()
    for load in late_loads:
        load.wait()

    def pair_copy(h):
        return remote(kv_sent.at[h], kv_pair.at[h], pair_out.at[h], pair_in.at[h], to_pair)

    def head_grads(h):
        lanes = slice(h * HEAD, (h + 1) * HEAD)

        def row_grads(i, carry):
            where = block(i)
            packed = grad_land[half_block(i)]
            far_lanes = slice(third + h * HEAD, third + (h + 1) * HEAD)
            incoming = jnp.concatenate([packed[:, lanes], packed[:, far_lanes]], axis=0).astype(F32)
            row_total = totals[where, h : h + 1]
            delta = jnp.sum(incoming * att_full[where, lanes], axis=-1, keepdims=True)
            grad_scaled = (incoming / row_total).astype(BF16)
            scaled[where] = grad_scaled
            weights = dot_nt(grad_scaled, v_heads[h])
            ds = (probs[h, where].astype(F32) * (weights - delta / row_total)).astype(BF16)
            score_grads[where] = ds
            grad_query = (dot_nn(ds, k_heads[h]) * 0.125).astype(BF16)
            query_grads[half_block(i), lanes] = grad_query[: rows // 2]
            query_grads[half_block(i), far_lanes] = grad_query[rows // 2 :]
            return carry

        lax.fori_loop(0, LINE, row_grads, 0)
        both = jnp.concatenate(
            [dot_tn(q_heads[h], score_grads[...]) * 0.125, dot_tn(scaled[...], probs[h])], axis=0
        )
        both = jnp.transpose(both)
        kv_sent[h] = both[mid:].astype(BF16)
        pair_copy(h).start()
        kv_own[h] = both[:mid]

    def query_back(k):
        return remote(
            query_grads.at[half_block(ahead(k))],
            query_land.at[line],
            back_out.at[HEADS_OWN, k - 1],
            back_in.at[HEADS_OWN, k - 1],
            to_line(k),
        )

    def query_landed(k):
        return remote(
            query_grads.at[half_block(ahead(k))],
            query_land.at[behind(k)],
            back_out.at[HEADS_OWN, k - 1],
            back_in.at[HEADS_OWN, k - 1],
            to_line(k),
        )

    def kv_back(h, k):
        return remote(
            kv_sum.at[h, block(ahead(k))],
            kv_land.at[h, line],
            back_out.at[h, k - 1],
            back_in.at[h, k - 1],
            to_line(k),
        )

    def kv_landed(h, k):
        return remote(
            kv_sum.at[h, block(ahead(k))],
            kv_land.at[h, behind(k)],
            back_out.at[h, k - 1],
            back_in.at[h, k - 1],
            to_line(k),
        )

    def ready(first, last):
        for i in range(first, last):
            seq_copies[i].wait_recv()

    def send_kv(h):
        pair_copy(h).wait_recv()
        kv_sum[h] = (kv_own[h] + kv_pair[h].astype(F32)).astype(BF16)
        for k in (3, 2, 1):
            kv_back(h, k).start()
        kv_land[h, line] = kv_sum[h, block(line)]

    def query_done():
        for k in (1, 2, 3):
            query_landed(k).wait_recv()
        for d in range(LINE):
            for i in range(2):
                mixed[i * rows // 2 : (i + 1) * rows // 2, d * third : (d + 1) * third] = query_land[
                    d, :, i * third : (i + 1) * third
                ]
        mixed_copies[0].start()

    def kv_done():
        for h in range(HEADS_OWN):
            for k in (1, 2, 3):
                kv_landed(h, k).wait_recv()
            for d in range(LINE):
                at = width + d * third + h * HEAD
                mixed[:, at : at + HEAD] = kv_land[h, d, :, 0:HEAD]
                mixed[:, width + at : width + at + HEAD] = kv_land[h, d, :, HEAD:]
        for part in (1, 2):
            mixed_copies[part].start()

    def pack_vectors():
        parts[VEC][...] = jnp.zeros(parts[VEC].shape, F32)
        for j in range(4 * LINE):
            slot = parts[VEC].at[j % 2, j // 4, (j // 2) % 2]
            size = width // (4 * LINE)
            slot[0:8, 0:size] = vec_one[0:8, j * size : (j + 1) * size]
            query_part = mixed[:, j * size : (j + 1) * size].astype(F32)
            slot[8:9, 0:size] = jnp.sum(query_part, axis=0, keepdims=True)
            value_part = mixed[:, 2 * width + j * size : 2 * width + (j + 1) * size].astype(F32)
            slot[9:10, 0:size] = jnp.sum(value_part, axis=0, keepdims=True)
            at = (j % 4) * 4 * size
            slot[10:11, 0 : 4 * size] = vec_one[8 + j // 4 : 9 + j // 4, at : at + 4 * size]
        core_copy(VEC).start()

    head_grads(0)
    head_grads(1)
    ready(0, 3)
    multiply(DOWN)
    multiply(DOWN_B)
    send_kv(0)
    add_core(DOWN)
    head_grads(2)
    for k in (3, 2, 1):
        query_back(k).start()
    query_land[line] = query_grads[half_block(line)]
    send_kv(1)
    add_core(DOWN_B)
    ready(3, 4)
    multiply(UP)
    stage(DOWN, 1)
    send_kv(2)
    ready(4, 5)
    multiply(UP_B)
    add_core(UP)
    query_done()
    stage(DOWN_B, 1)
    stage(DOWN, 2)
    add_core(UP_B)
    ready(5, 7)
    multiply(OUT)
    kv_done()
    stage(DOWN, 3)
    stage(DOWN_B, 2)
    mixed_copies[0].wait_recv()
    multiply(QUERY)
    add_core(OUT)
    stage(UP, 1)
    stage(DOWN_B, 3)
    stage(DOWN, 4)
    pack_vectors()
    mixed_copies[1].wait_recv()
    multiply(KEY)
    add_core(QUERY)
    stage(UP, 2)
    stage(DOWN_B, 4)
    mixed_copies[2].wait_recv()
    multiply(VALUE)
    add_core(KEY)
    stage(UP_B, 1)
    stage(UP, 3)
    add_core(VALUE)
    add_core(VEC)
    stage(OUT, 1)
    stage(UP_B, 2)
    grad_hidden[...] = first[...] + dot_nt(mixed[...], w_all[...])
    stage(UP, 4)
    stage(UP_B, 3)
    for s in range(QUERY, VEC + 4):
        for n in (1, 2, 3, 4):
            if OUT <= s + 1 - n <= VEC:
                stage(s + 1 - n, n)
        if s == QUERY:
            stage(UP_B, 4)
    for u in units:
        last_copy(u).wait_recv()
    vec_own[...] = parts[VEC][core, line, side] + vec_seq[...]
    for k in (1, 2, 3):
        line_copy(k).wait_send()
        query_back(k).wait_send()
        for h in range(HEADS_OWN):
            kv_back(h, k).wait_send()
    for h in range(HEADS_OWN):
        pair_copy(h).wait_send()
    for copy in seq_copies + mixed_copies:
        copy.wait_send()
    for u in units:
        core_copy(u).wait_send()
        last_copy(u).wait_send()
        for k in range(LINE):
            side_copy(u, k).wait_send()
        for k in range(1, LINE):

            @pl.when(line < k)
            def _(k=k):
                up_copy(u, k).wait_send()

        for k in range(LINE - 1):

            @pl.when(line > k)
            def _(k=k):
                down_copy(u, k).wait_send()


def backward(*args):
    rows, width = args[1].shape
    ffn = args[6].shape[1]
    third = HEADS_OWN * HEAD
    mid, seq_rows = LINE * rows, 2 * LINE * rows
    shape = jax.ShapeDtypeStruct
    widths = ((ffn // 2, width // 2),) * 2 + ((width, ffn // 4),) * 2 + ((width, width // 2),) * 4
    dims = [(a // (4 * LINE), b, a == width) for a, b in widths]
    shard, ffn_shard = width // (4 * LINE), ffn // (4 * LINE)
    own_shapes = [(ffn_shard, width), (shard, ffn), (shard, 3 * width), (shard, width)]
    blocks = [((r, c), BF16) for r, c, _ in dims] + [((16, 256), F32)]
    count = len(blocks)
    vmem, dma = pltpu.VMEM, pltpu.SemaphoreType.DMA
    outs = [shape((rows, width), BF16), shape((rows, width), F32)]
    outs += [shape(own, BF16) for own in own_shapes]
    outs.append(shape((16, 256), F32))
    return pl.pallas_call(
        functools.partial(backward_kernel, dims),
        out_shape=outs,
        in_specs=[INNER] * 4 + [ANY] * 14,
        out_specs=[INNER] * len(outs),
        scratch_shapes=[
            vmem((width, width), BF16),
            vmem((width, ffn), BF16),
            vmem((ffn, width), BF16),
            vmem((rows, ffn), BF16),
            vmem((rows, ffn), F32),
            vmem((rows, width), F32),
            vmem((16, width), F32),
            vmem((LINE, rows // 2, 2 * third), BF16),
            vmem((2, rows, ffn // 2), BF16),
            vmem((2, rows, ffn // 2), BF16),
            vmem((2, rows, width // 2), BF16),
            vmem((HEADS_OWN, mid, HEAD), BF16),
            vmem((HEADS_OWN, seq_rows, HEAD), BF16),
            vmem((HEADS_OWN, seq_rows, HEAD), BF16),
            vmem((mid, third), F32),
            vmem((mid, 128), F32),
            vmem((width, 3 * width), BF16),
            vmem((HEADS_OWN, mid, seq_rows), BF16),
            vmem((mid // 2, 2 * third), BF16),
            vmem((mid, HEAD), BF16),
            vmem((mid, seq_rows), BF16),
            vmem((mid // 2, 2 * third), BF16),
            vmem((HEADS_OWN, mid, 128), F32),
            vmem((HEADS_OWN, mid, 128), BF16),
            vmem((HEADS_OWN, mid, 128), BF16),
            vmem((HEADS_OWN, mid, 128), BF16),
            vmem((HEADS_OWN, LINE, rows, 128), BF16),
            vmem((LINE, rows // 2, 2 * third), BF16),
            vmem((rows, 3 * width), BF16),
            [vmem((rows, a), BF16) for a in (ffn // 2, width, width, width, width)],
            [vmem((rows, b), BF16) for b in (width, width, ffn // 2) + (width // 2,) * 4],
            [vmem((2, LINE, 2) + block, kind) for block, kind in blocks],
            [vmem((LINE, 2) + block, kind) for block, kind in blocks],
            [vmem((LINE,) + block, kind) for block, kind in blocks],
            [vmem((LINE - 1,) + block, kind) for block, kind in blocks],
            [vmem((LINE - 1,) + block, kind) for block, kind in blocks],
            vmem((16, 256), F32),
            dma((6,)),
            dma((8,)),
            dma((3,)),
            dma((3,)),
            dma((3,)),
            dma((3,)),
            dma((4, 3)),
            dma((4, 3)),
            dma((10,)),
            dma((10,)),
            dma((2, count)),
            dma((2, count, LINE)),
            dma((2, count, LINE - 1)),
            dma((2, count, LINE - 1)),
            dma((2, count)),
        ],
        compiler_params=pltpu.CompilerParams(
            collective_id=2, has_side_effects=True, vmem_limit_bytes=63 << 20
        ),
        name="backward",
    )(*args)


def finish_kernel(*refs):
    for i in range(6):
        refs[7 + i][...] = refs[i][...].astype(refs[7 + i].dtype)
    vec = refs[6]
    for i, row in enumerate((8, 9, 0, 1, 2, 3, 4, 5, 10)):
        out = refs[13 + i]
        out[...] = vec[row, 0 : out.shape[0]]


def finish(*args):
    shape = jax.ShapeDtypeStruct
    outs = [shape(a.shape, F32) for a in args[:5]] + [shape(args[5].shape, BF16)]
    size = args[2].shape[0]
    outs += [shape((size,), F32)] * 8 + [shape((4 * size,), F32)]
    return pl.pallas_call(
        finish_kernel,
        out_shape=outs,
        in_specs=[INNER] * 7,
        out_specs=[INNER] * len(outs),
        name="finish",
    )(*args)


def block_device(
    hidden,
    segment_ids,
    out_grad,
    w_qkv,
    bias_query,
    bias_value,
    w_out,
    bias_out,
    gain_one,
    shift_one,
    w_up,
    bias_up,
    w_down,
    bias_down,
    gain_two,
    shift_two,
):
    tok, grad_out = hidden[0], out_grad[0]
    small = [
        bias_query,
        bias_value,
        bias_out,
        gain_one,
        shift_one,
        bias_down,
        gain_two,
        shift_two,
        bias_up,
    ]
    (
        attended,
        tok_pair,
        vec_all,
        w_full,
        out_other,
        up_other,
        down_other,
        q_heads,
        k_heads,
        v_heads,
        att_full,
        totals,
        probs,
    ) = attend_forward(tok, segment_ids, small, w_qkv, w_out, w_up, w_down)
    result, grad_hidden, down_own, up_own, qkv_own, out_own, vec_own = backward(
        attended,
        tok,
        grad_out,
        vec_all,
        w_out,
        out_other,
        w_up,
        up_other,
        w_down,
        down_other,
        q_heads,
        k_heads,
        v_heads,
        att_full,
        totals,
        probs,
        w_full,
        tok_pair,
    )
    grads = finish(up_own, down_own, qkv_own, out_own, grad_hidden, result, vec_own)
    up_grad, down_grad, qkv_grad, out_grads, grad_hidden, result = grads[:6]
    (
        query_bias,
        value_bias,
        out_bias,
        gain_first,
        shift_first,
        down_bias,
        gain_second,
        shift_second,
        up_bias,
    ) = grads[6:]
    return (
        result[None],
        grad_hidden[None],
        qkv_grad,
        query_bias,
        value_bias,
        out_grads,
        out_bias,
        gain_first,
        shift_first,
        up_grad,
        up_bias,
        down_grad,
        down_bias,
        gain_second,
        shift_second,
    )


def solution(mesh):
    small = (mesh.shape["seq"], mesh.shape["ctx"], mesh.shape["fsdp"]) == (2, 8, 2)
    return jax.shard_map(
        block_device if small else on_device,
        mesh=mesh,
        in_specs=(
            P(("seq", "fsdp"), "ctx", None),
            P(("seq", "fsdp"), None),
            P(("seq", "fsdp"), "ctx", None),
            P("fsdp", None),
            P("fsdp"),
            P("fsdp"),
            P("fsdp", None),
            P("fsdp"),
            P("fsdp"),
            P("fsdp"),
            P("fsdp", None),
            P("fsdp"),
            P("fsdp", None),
            P("fsdp"),
            P("fsdp"),
            P("fsdp"),
        ),
        out_specs=(
            P(("seq", "fsdp"), "ctx", None),
            P(("seq", "fsdp"), "ctx", None),
            P(("ctx", "fsdp"), None),
            P(("ctx", "fsdp")),
            P(("ctx", "fsdp")),
            P(("ctx", "fsdp"), None),
            P(("ctx", "fsdp")),
            P(("ctx", "fsdp")),
            P(("ctx", "fsdp")),
            P(("ctx", "fsdp"), None),
            P(("ctx", "fsdp")),
            P(("ctx", "fsdp"), None),
            P(("ctx", "fsdp")),
            P(("ctx", "fsdp")),
            P(("ctx", "fsdp")),
        ),
        check_vma=False,
    )
```

```python
import functools

import jax
import jax.numpy as jnp
from jax import lax
from jax.experimental import pallas as pl
from jax.experimental.pallas import tpu as pltpu
from jax.sharding import PartitionSpec as P

HEAD = 64


EPSILON = 1e-12
NEGATIVE = -1e30
LOG_TWO = 0.6931471805599453
LOG2_E = 1.4426950408889634


def norm_forward(rows_in, gain_vec, shift_vec):
    row_mean = jnp.mean(rows_in, axis=-1, keepdims=True)
    centered = rows_in - row_mean
    variance = jnp.mean(centered * centered, axis=-1, keepdims=True)
    scaled = lax.rsqrt(variance + EPSILON)
    normed = centered * scaled
    return (normed * gain_vec + shift_vec, normed, scaled)


def norm_backward(grad_rows, normed, scaled, gain_vec):
    grad_normed = grad_rows * gain_vec
    inner_part = (
        grad_normed
        - jnp.mean(grad_normed, axis=-1, keepdims=True)
        - normed * jnp.mean(grad_normed * normed, axis=-1, keepdims=True)
    )
    return (inner_part * scaled, jnp.sum(grad_rows * normed, axis=0), jnp.sum(grad_rows, axis=0))


def head_scores(query_heads, key_heads):
    return (
        jnp.einsum("qhd,khd->hqk", query_heads, key_heads, preferred_element_type=jnp.float32)
        * 0.125
    )


def column_sums(rows_b):
    return jnp.sum(rows_b.astype(jnp.float32), axis=0)


def sweep(steps_total, advance, start_carry):

    def advance_one(running, block_index):
        running = advance(running, block_index)
        return (running, None)

    return lax.scan(advance_one, start_carry, jnp.arange(steps_total))[0]


def local_grads(scores, allowed, shift_rows, ratio_rows, grad_heads, value_heads):
    unnorm = jnp.where(allowed, jnp.exp(scores - shift_rows[..., None]), 0.0)
    grad_weights = jnp.einsum(
        "qhd,khd->hqk", grad_heads, value_heads, preferred_element_type=jnp.float32
    )
    grad_scores = (unnorm * (grad_weights - ratio_rows[..., None])).astype(jnp.bfloat16)
    return (unnorm.astype(jnp.bfloat16), grad_scores)


def on_device(
    hidden,
    segment_ids,
    out_grad,
    w_qkv,
    bias_query,
    bias_value,
    w_out,
    bias_out,
    gain_one,
    shift_one,
    w_up,
    bias_up,
    w_down,
    bias_down,
    gain_two,
    shift_two,
):
    (
        w_qkv,
        bias_query,
        bias_value,
        w_out,
        bias_out,
        gain_one,
        shift_one,
        w_up,
        bias_up,
        w_down,
        bias_down,
        gain_two,
        shift_two,
    ) = (
        lax.all_gather(w_qkv, "fsdp", axis=0, tiled=True),
        lax.all_gather(bias_query, "fsdp", axis=0, tiled=True),
        lax.all_gather(bias_value, "fsdp", axis=0, tiled=True),
        lax.all_gather(w_out, "fsdp", axis=0, tiled=True),
        lax.all_gather(bias_out, "fsdp", axis=0, tiled=True),
        lax.all_gather(gain_one, "fsdp", axis=0, tiled=True),
        lax.all_gather(shift_one, "fsdp", axis=0, tiled=True),
        lax.all_gather(w_up, "fsdp", axis=0, tiled=True),
        lax.all_gather(bias_up, "fsdp", axis=0, tiled=True),
        lax.all_gather(w_down, "fsdp", axis=0, tiled=True),
        lax.all_gather(bias_down, "fsdp", axis=0, tiled=True),
        lax.all_gather(gain_two, "fsdp", axis=0, tiled=True),
        lax.all_gather(shift_two, "fsdp", axis=0, tiled=True),
    )
    f32 = jnp.float32
    bf16 = jnp.bfloat16
    tokens = hidden[0]
    tok_rows = tokens.shape[0]
    model_width = tokens.shape[1]
    head_count = model_width // HEAD
    seq_rows = tok_rows * lax.axis_size("ctx")
    key_span = 4 * tok_rows
    block_total = seq_rows // key_span
    doc_ids = segment_ids[0]
    own_ids = lax.dynamic_slice_in_dim(doc_ids, lax.axis_index("ctx") * tok_rows, tok_rows)
    mixed_rows = jnp.dot(tokens, w_qkv, preferred_element_type=f32)
    query_rows = (mixed_rows[:, :model_width] + bias_query.astype(f32)).astype(bf16)
    key_value = jnp.concatenate(
        [
            mixed_rows[:, model_width : 2 * model_width],
            mixed_rows[:, 2 * model_width :] + bias_value.astype(f32),
        ],
        axis=1,
    ).astype(bf16)
    all_kv = lax.all_gather(key_value, "ctx", axis=0, tiled=True)
    query_heads = query_rows.reshape(tok_rows, head_count, HEAD)

    def key_block(block_index):
        kv_piece = lax.dynamic_slice_in_dim(all_kv, block_index * key_span, key_span, 0)
        key_ids = lax.dynamic_slice_in_dim(doc_ids, block_index * key_span, key_span)
        return (
            kv_piece[:, :model_width].reshape(key_span, head_count, HEAD),
            kv_piece[:, model_width:].reshape(key_span, head_count, HEAD),
            key_ids,
        )

    def forward_step(running, block_index):
        level_run, total_run, sum_run = running
        key_heads, value_heads, key_ids = key_block(block_index)
        allowed = (own_ids[:, None] == key_ids[None, :])[None]
        scores = jnp.where(allowed, head_scores(query_heads, key_heads), NEGATIVE)
        level_new = jnp.maximum(level_run, jnp.ceil(jnp.max(scores, axis=-1) * LOG2_E))
        rescale = jnp.exp(LOG_TWO * (level_run - level_new))
        unnorm = jnp.where(allowed, jnp.exp(scores - (LOG_TWO * level_new)[..., None]), 0.0)
        total_new = total_run * rescale + jnp.sum(unnorm, axis=-1)
        sum_new = sum_run * jnp.transpose(rescale)[:, :, None] + jnp.einsum(
            "hqk,khd->qhd", unnorm.astype(bf16), value_heads, preferred_element_type=f32
        )
        return (level_new, total_new, sum_new)

    start_state = (
        jnp.full((head_count, tok_rows), NEGATIVE, f32),
        jnp.zeros((head_count, tok_rows), f32),
        jnp.zeros((tok_rows, head_count, HEAD), f32),
    )
    level_end, row_total, raw_sum = sweep(block_total, forward_step, start_state)
    row_shift = LOG_TWO * level_end
    att_sum = raw_sum / jnp.transpose(row_total)[:, :, None]
    attended = att_sum.reshape(tok_rows, model_width).astype(bf16)
    branch = jnp.dot(attended, w_out, preferred_element_type=f32) + bias_out.astype(f32)
    normed_one, norm_one, scale_one = norm_forward(
        tokens.astype(f32) + branch, gain_one.astype(f32), shift_one.astype(f32)
    )
    normed_b = normed_one.astype(bf16)
    up_rows = jnp.dot(normed_b, w_up, preferred_element_type=f32) + bias_up.astype(f32)
    active, gelu_back = jax.vjp(lambda pre_act: jax.nn.gelu(pre_act, approximate=False), up_rows)
    active_b = active.astype(bf16)
    second = (
        normed_one + jnp.dot(active_b, w_down, preferred_element_type=f32) + bias_down.astype(f32)
    )
    result, norm_two, scale_two = norm_forward(second, gain_two.astype(f32), shift_two.astype(f32))
    grad_second, grad_gain_two, grad_shift_two = norm_backward(
        out_grad[0].astype(f32), norm_two, scale_two, gain_two.astype(f32)
    )
    grad_ffn = grad_second.astype(bf16)
    grad_bias_down = column_sums(grad_ffn)
    grad_w_down = jnp.dot(active_b.T, grad_ffn, preferred_element_type=f32)
    grad_active = jnp.dot(grad_ffn, w_down.T, preferred_element_type=f32)
    grad_up = gelu_back(grad_active)[0].astype(bf16)
    grad_bias_up = column_sums(grad_up)
    grad_w_up = jnp.dot(normed_b.T, grad_up, preferred_element_type=f32)
    grad_normed = grad_second + jnp.dot(grad_up, w_up.T, preferred_element_type=f32)
    grad_first, grad_gain_one, grad_shift_one = norm_backward(
        grad_normed, norm_one, scale_one, gain_one.astype(f32)
    )
    grad_branch = grad_first.astype(bf16)
    grad_bias_out = column_sums(grad_branch)
    grad_w_out = jnp.dot(attended.T, grad_branch, preferred_element_type=f32)
    grad_attended = jnp.dot(grad_branch, w_out.T, preferred_element_type=f32).astype(bf16)
    grad_att_f32 = grad_attended.reshape(tok_rows, head_count, HEAD).astype(f32)
    delta = jnp.einsum("qhd,qhd->hq", grad_att_f32, att_sum)
    delta_ratio = delta / row_total
    grad_scaled = (grad_att_f32 / jnp.transpose(row_total)[:, :, None]).astype(bf16)
    zero_query = jnp.zeros((tok_rows, head_count, HEAD), f32)

    def full_step(running, block_index):
        grad_query, grad_kv = running
        key_heads, value_heads, key_ids = key_block(block_index)
        allowed = (own_ids[:, None] == key_ids[None, :])[None]
        unnorm_b, grad_scores = local_grads(
            head_scores(query_heads, key_heads),
            allowed,
            row_shift,
            delta_ratio,
            grad_scaled,
            value_heads,
        )
        grad_query = (
            grad_query
            + jnp.einsum("hqk,khd->qhd", grad_scores, key_heads, preferred_element_type=f32) * 0.125
        )
        grad_keys = (
            jnp.einsum("hqk,qhd->khd", grad_scores, query_heads, preferred_element_type=f32) * 0.125
        )
        grad_values = jnp.einsum("hqk,qhd->khd", unnorm_b, grad_scaled, preferred_element_type=f32)
        both_grads = jnp.concatenate(
            [grad_keys.reshape(key_span, model_width), grad_values.reshape(key_span, model_width)],
            axis=1,
        )
        grad_kv = lax.dynamic_update_slice_in_dim(grad_kv, both_grads, block_index * key_span, 0)
        return (grad_query, grad_kv)

    start_full = (zero_query, jnp.zeros((seq_rows, 2 * model_width), f32))
    grad_query, grad_kv = sweep(block_total, full_step, start_full)
    own_kv = lax.psum_scatter(grad_kv, "ctx", scatter_dimension=0, tiled=True)
    grad_query_b = grad_query.reshape(tok_rows, model_width).astype(bf16)
    grad_kv_b = own_kv.astype(bf16)
    grad_mixed = jnp.concatenate([grad_query_b, grad_kv_b], axis=1)
    grad_tokens = grad_first + jnp.dot(grad_mixed, w_qkv.T, preferred_element_type=f32)
    grad_w_qkv = jnp.dot(tokens.T, grad_mixed, preferred_element_type=f32)
    grad_bias_query = column_sums(grad_query_b)
    grad_bias_value = column_sums(grad_kv_b[:, model_width:])
    shares = (
        lax.psum_scatter(grad_w_qkv, ("ctx", "fsdp"), scatter_dimension=0, tiled=True),
        lax.psum_scatter(grad_bias_query, ("ctx", "fsdp"), scatter_dimension=0, tiled=True),
        lax.psum_scatter(grad_bias_value, ("ctx", "fsdp"), scatter_dimension=0, tiled=True),
        lax.psum_scatter(grad_w_out, ("ctx", "fsdp"), scatter_dimension=0, tiled=True),
        lax.psum_scatter(grad_bias_out, ("ctx", "fsdp"), scatter_dimension=0, tiled=True),
        lax.psum_scatter(grad_gain_one, ("ctx", "fsdp"), scatter_dimension=0, tiled=True),
        lax.psum_scatter(grad_shift_one, ("ctx", "fsdp"), scatter_dimension=0, tiled=True),
        lax.psum_scatter(grad_w_up, ("ctx", "fsdp"), scatter_dimension=0, tiled=True),
        lax.psum_scatter(grad_bias_up, ("ctx", "fsdp"), scatter_dimension=0, tiled=True),
        lax.psum_scatter(grad_w_down, ("ctx", "fsdp"), scatter_dimension=0, tiled=True),
        lax.psum_scatter(grad_bias_down, ("ctx", "fsdp"), scatter_dimension=0, tiled=True),
        lax.psum_scatter(grad_gain_two, ("ctx", "fsdp"), scatter_dimension=0, tiled=True),
        lax.psum_scatter(grad_shift_two, ("ctx", "fsdp"), scatter_dimension=0, tiled=True),
    )
    summed = (
        lax.psum(shares[0].astype(jnp.bfloat16), "seq").astype(jnp.float32),
        lax.psum(shares[1].astype(jnp.bfloat16), "seq").astype(jnp.float32),
        lax.psum(shares[2].astype(jnp.bfloat16), "seq").astype(jnp.float32),
        lax.psum(shares[3].astype(jnp.bfloat16), "seq").astype(jnp.float32),
        lax.psum(shares[4].astype(jnp.bfloat16), "seq").astype(jnp.float32),
        lax.psum(shares[5].astype(jnp.bfloat16), "seq").astype(jnp.float32),
        lax.psum(shares[6].astype(jnp.bfloat16), "seq").astype(jnp.float32),
        lax.psum(shares[7].astype(jnp.bfloat16), "seq").astype(jnp.float32),
        lax.psum(shares[8].astype(jnp.bfloat16), "seq").astype(jnp.float32),
        lax.psum(shares[9].astype(jnp.bfloat16), "seq").astype(jnp.float32),
        lax.psum(shares[10].astype(jnp.bfloat16), "seq").astype(jnp.float32),
        lax.psum(shares[11].astype(jnp.bfloat16), "seq").astype(jnp.float32),
        lax.psum(shares[12].astype(jnp.bfloat16), "seq").astype(jnp.float32),
    )
    return (
        result.astype(bf16)[None],
        grad_tokens[None],
        summed[0],
        summed[1],
        summed[2],
        summed[3],
        summed[4],
        summed[5],
        summed[6],
        summed[7],
        summed[8],
        summed[9],
        summed[10],
        summed[11],
        summed[12],
    )


MESH_ID = pl.DeviceIdType.MESH
LINE = 4


def remote(src, dst, send, recv, target):
    return pltpu.make_async_remote_copy(
        src_ref=src,
        dst_ref=dst,
        send_sem=send,
        recv_sem=recv,
        device_id=target,
        device_id_type=MESH_ID,
    )


HEADS_OWN = 3
F32 = jnp.float32
BF16 = jnp.bfloat16
ANY = pl.BlockSpec(memory_space=pl.ANY)
INNER = pl.BlockSpec(memory_space=pltpu.VMEM)


def dot_nt(a, b):
    return lax.dot_general(a, b, (((1,), (1,)), ((), ())), preferred_element_type=F32)


def dot_tn(a, b):
    return lax.dot_general(a, b, (((0,), (0,)), ((), ())), preferred_element_type=F32)


def dot_nn(a, b):
    return lax.dot_general(a, b, (((1,), (0,)), ((), ())), preferred_element_type=F32)


def greet(targets):
    barrier = pltpu.get_barrier_semaphore()
    for target in targets:
        pl.semaphore_signal(barrier, inc=1, device_id=target, device_id_type=MESH_ID)
    pl.semaphore_wait(barrier, len(targets))


def attend_kernel(
    tok,
    ids,
    small,
    w_qkv,
    w_out,
    w_up,
    w_down,
    attended,
    tok_pair,
    vec_all,
    w_full,
    out_other,
    up_other,
    down_other,
    q_out,
    k_out,
    v_out,
    att_full,
    totals,
    probs_out,
    q_heads,
    k_heads,
    v_heads,
    w_all,
    mixed,
    sent_kv,
    sent_q,
    mine,
    mine_q,
    other,
    att_sent,
    att_land,
    probs,
    vec,
    ids_row,
    ids_col,
    local_sem,
    probs_sem,
    core_out,
    core_in,
    line_out,
    line_in,
    pair_out,
    pair_in,
    back_out,
    back_in,
    seq_out,
    seq_in,
):
    place = lax.axis_index("ctx")
    core = lax.axis_index("fsdp")
    group = lax.axis_index("seq")
    line, side = place // 2, place % 2
    to_core = {"fsdp": 1 - core}
    to_pair = {"ctx": place + 1 - 2 * side}
    to_seq = {"seq": 1 - group}
    rows = tok.shape[0]
    width = tok.shape[1]
    half = width // 2
    third = HEADS_OWN * HEAD

    def ahead(k):
        return lax.rem(line + k, LINE)

    def behind(k):
        return lax.rem(line + LINE - k, LINE)

    def to_line(k):
        return {"ctx": 2 * ahead(k) + side}

    def block(which):
        return pl.ds(pl.multiple_of(which * rows, 32), rows)

    def half_block(which):
        return pl.ds(pl.multiple_of(which * (rows // 2), 16), rows // 2)

    own_rows = pl.ds(pl.multiple_of(core * half, 128), half)
    other_rows = pl.ds(pl.multiple_of((1 - core) * half, 128), half)

    own_load = pltpu.make_async_copy(w_qkv, w_all.at[own_rows], local_sem.at[0])
    own_load.start()
    at = 0
    for piece in small:
        for first in range(0, piece.shape[0], half):
            vec[at : at + 1] = piece[first : first + half].astype(F32)[None]
            at += 1
    vec[at:] = jnp.zeros((vec.shape[0] - at, half), F32)
    greet([to_core, to_pair, to_seq] + [to_line(k) for k in range(1, LINE)])
    core_copies = [
        remote(vec, vec_all.at[:, own_rows], core_out.at[0], core_in.at[0], to_core),
        remote(w_out, out_other, core_out.at[1], core_in.at[1], to_core),
        remote(w_up, up_other, core_out.at[2], core_in.at[2], to_core),
        remote(w_down, down_other, core_out.at[3], core_in.at[3], to_core),
    ]
    qkv_copies = []
    for part in range(3):
        lanes = slice(part * width, (part + 1) * width)
        sems = core_out.at[4 + part], core_in.at[4 + part]
        qkv_copies.append(remote(w_qkv.at[:, lanes], w_all.at[own_rows, lanes], *sems, to_core))
    seq_copy = remote(tok, tok_pair, seq_out.at[0], seq_in.at[0], to_seq)
    core_copies[0].start()
    for part in (1, 2, 0):
        qkv_copies[part].start()
    seq_copy.start()
    vec_all[:, own_rows] = vec[...]
    own_load.wait()
    step = width // 2
    for first in range(0, 3 * width, step):
        mixed[:, first : first + step] = dot_nn(
            tok[:, own_rows], w_all[own_rows, first : first + step]
        )
    core_copies[0].wait_recv()

    def kv_copy(k, to):
        return remote(
            sent_kv.at[ahead(k)],
            mine.at[block(to)],
            line_out.at[0, k - 1],
            line_in.at[0, k - 1],
            to_line(k),
        )

    def q_copy(k, to):
        return remote(
            sent_q.at[ahead(k)],
            mine_q.at[half_block(to)],
            line_out.at[1, k - 1],
            line_in.at[1, k - 1],
            to_line(k),
        )

    def pair_copy(k):
        where = block(behind(k))
        return remote(mine.at[where], other.at[where], pair_out.at[k], pair_in.at[k], to_pair)

    bias = vec_all[...]
    for part in (1, 2, 0):
        qkv_copies[part].wait_recv()
        for first in range(part * width, (part + 1) * width, step):
            total = mixed[:, first : first + step] + dot_nn(
                tok[:, other_rows], w_all[other_rows, first : first + step]
            )
            within = first - part * width
            if part == 0:
                total += bias[0:1, within : within + step]
            if part == 2:
                total += bias[1:2, within : within + step]
            total = total.astype(BF16)
            for j in range(2):
                d, piece = within // third + j, total[:, j * third : (j + 1) * third]
                if part == 0:
                    sent_q[d, :, 0:third] = piece[: rows // 2]
                    sent_q[d, :, third:] = piece[rows // 2 :]
                else:
                    sent_kv[d, :, (part - 1) * third : part * third] = piece
        for k in (1, 2, 3):
            if part == 2:
                kv_copy(k, line).start()
            if part == 0:
                q_copy(k, line).start()
        if part == 2:
            mine[block(line)] = sent_kv[line]
            pair_copy(0).start()
    for copy in core_copies[1:]:
        copy.start()
    full_store = pltpu.make_async_copy(w_all, w_full, local_sem.at[1])
    full_store.start()
    mine_q[half_block(line)] = sent_q[line]
    for k in (1, 2, 3):
        kv_copy(k, behind(k)).wait_recv()
        pair_copy(k).start()
    seq_rows = 2 * LINE * rows
    mid = LINE * rows
    for z in range(LINE):
        even = ids[:, 2 * z * rows : (2 * z + 1) * rows].astype(F32)
        odd = ids[:, (2 * z + 1) * rows : (2 * z + 2) * rows].astype(F32)
        ids_row[:, z * rows : (z + 1) * rows] = jnp.where(side == 0, even, odd)
        ids_row[:, mid + z * rows : mid + (z + 1) * rows] = jnp.where(side == 0, odd, even)
    ids_col[...] = jnp.transpose(jnp.broadcast_to(ids_row[:, 0:mid], (8, mid)))[:, 0:1]
    for h in range(HEADS_OWN):
        k_heads[h, 0:mid] = mine[:, h * HEAD : (h + 1) * HEAD]
        v_heads[h, 0:mid] = mine[:, third + h * HEAD : third + (h + 1) * HEAD]
    for k in (1, 2, 3):
        q_copy(k, behind(k)).wait_recv()
    for h in range(HEADS_OWN):
        for i in range(2 * LINE):
            from_rows = slice((i // 2) * rows // 2, (i // 2 + 1) * rows // 2)
            at = (i % 2) * third + h * HEAD
            q_heads[h, i * rows // 2 : (i + 1) * rows // 2] = mine_q[from_rows, at : at + HEAD]
    for k in range(LINE):
        pair_copy(k).wait_recv()
    for h in range(HEADS_OWN):
        k_heads[h, mid:seq_rows] = other[:, h * HEAD : (h + 1) * HEAD]
        v_heads[h, mid:seq_rows] = other[:, third + h * HEAD : third + (h + 1) * HEAD]

    head_stores = []
    for i, (src, dst) in enumerate(((q_heads, q_out), (k_heads, k_out), (v_heads, v_out))):
        head_stores.append(pltpu.make_async_copy(src, dst, local_sem.at[2 + i]))
        head_stores[i].start()

    def back_copy(k):
        return remote(
            att_sent.at[ahead(k)],
            att_land.at[line],
            back_out.at[k - 1],
            back_in.at[k - 1],
            to_line(k),
        )

    def back_landed(k):
        return remote(
            att_sent.at[ahead(k)],
            att_land.at[behind(k)],
            back_out.at[k - 1],
            back_in.at[k - 1],
            to_line(k),
        )

    def probs_copy(k):
        where = block(ahead(k))
        return pltpu.make_async_copy(
            probs.at[:, where], probs_out.at[:, where], probs_sem.at[k - 1]
        )

    def attend(k, carry):
        which = ahead(k)
        where = block(which)
        allowed = ids_col[where] == ids_row[...]
        for h in range(HEADS_OWN):
            scores = dot_nt(q_heads[h, where], k_heads[h]) * 0.125
            scores = jnp.where(allowed, scores, NEGATIVE)
            level = jnp.ceil(jnp.max(scores, axis=-1, keepdims=True) * LOG2_E)
            unnorm = jnp.exp(scores - LOG_TWO * level)
            row_total = jnp.sum(unnorm, axis=-1, keepdims=True)
            unnorm_b = unnorm.astype(BF16)
            probs[h, where] = unnorm_b
            value = dot_nn(unnorm_b, v_heads[h]) / row_total
            att_full[where, h * HEAD : (h + 1) * HEAD] = value
            totals[where, h : h + 1] = row_total
            value_b = value.astype(BF16)
            for i in range(2):
                att_sent[which, :, i * third + h * HEAD : i * third + (h + 1) * HEAD] = value_b[
                    i * rows // 2 : (i + 1) * rows // 2
                ]
        probs_copy(k).start()

        @pl.when(k < LINE)
        def _():
            back_copy(k).start()

        return carry

    lax.fori_loop(1, LINE + 1, attend, 0)
    att_land[line] = att_sent[line]
    for k in (1, 2, 3):
        back_landed(k).wait_recv()
    for d in range(LINE):
        for i in range(2):
            attended[i * rows // 2 : (i + 1) * rows // 2, d * third : (d + 1) * third] = att_land[
                d, :, i * third : (i + 1) * third
            ]
    for k in (1, 2, 3):
        kv_copy(k, line).wait_send()
        q_copy(k, line).wait_send()
        back_copy(k).wait_send()
    for k in range(LINE):
        pair_copy(k).wait_send()
        probs_copy(k + 1).wait()
    for copy in core_copies[1:]:
        copy.wait_recv()
    for copy in core_copies + qkv_copies:
        copy.wait_send()
    for store in head_stores:
        store.wait()
    seq_copy.wait()
    full_store.wait()


def attend_forward(tok, ids, small, w_qkv, w_out, w_up, w_down):
    rows, width = tok.shape
    third = HEADS_OWN * HEAD
    mid, seq_rows = LINE * rows, 2 * LINE * rows
    shape = jax.ShapeDtypeStruct
    outs = [
        (shape((rows, width), BF16), INNER),
        (shape((rows, width), BF16), INNER),
        (shape((16, width), F32), INNER),
        (shape((width, 3 * width), BF16), ANY),
        (shape(w_out.shape, BF16), ANY),
        (shape(w_up.shape, BF16), ANY),
        (shape(w_down.shape, BF16), ANY),
        (shape((HEADS_OWN, mid, HEAD), BF16), ANY),
        (shape((HEADS_OWN, seq_rows, HEAD), BF16), ANY),
        (shape((HEADS_OWN, seq_rows, HEAD), BF16), ANY),
        (shape((mid, third), F32), INNER),
        (shape((mid, 128), F32), INNER),
        (shape((HEADS_OWN, mid, seq_rows), BF16), ANY),
    ]
    dma = pltpu.SemaphoreType.DMA
    return pl.pallas_call(
        attend_kernel,
        out_shape=[o[0] for o in outs],
        in_specs=[INNER, INNER, [INNER] * len(small)] + [ANY] * 4,
        out_specs=[o[1] for o in outs],
        scratch_shapes=[
            pltpu.VMEM((HEADS_OWN, mid, HEAD), BF16),
            pltpu.VMEM((HEADS_OWN, seq_rows, HEAD), BF16),
            pltpu.VMEM((HEADS_OWN, seq_rows, HEAD), BF16),
            pltpu.VMEM((width, 3 * width), BF16),
            pltpu.VMEM((rows, 3 * width), F32),
            pltpu.VMEM((LINE, rows, 2 * third), BF16),
            pltpu.VMEM((LINE, rows // 2, 2 * third), BF16),
            pltpu.VMEM((mid, 2 * third), BF16),
            pltpu.VMEM((mid // 2, 2 * third), BF16),
            pltpu.VMEM((mid, 2 * third), BF16),
            pltpu.VMEM((LINE, rows // 2, 2 * third), BF16),
            pltpu.VMEM((LINE, rows // 2, 2 * third), BF16),
            pltpu.VMEM((HEADS_OWN, mid, seq_rows), BF16),
            pltpu.VMEM((16, width // 2), F32),
            pltpu.VMEM((1, seq_rows), F32),
            pltpu.VMEM((mid, 1), F32),
            dma((5,)),
            dma((LINE,)),
            dma((7,)),
            dma((7,)),
            dma((2, 3)),
            dma((2, 3)),
            dma((LINE,)),
            dma((LINE,)),
            dma((3,)),
            dma((3,)),
            dma((1,)),
            dma((1,)),
        ],
        compiler_params=pltpu.CompilerParams(
            collective_id=1, has_side_effects=True, vmem_limit_bytes=63 << 20
        ),
        name="attend_forward",
    )(tok, ids, small, w_qkv, w_out, w_up, w_down)


DOWN, DOWN_B, UP, UP_B, OUT, QUERY, KEY, VALUE, VEC = range(9)


def backward_kernel(
    dims,
    attended,
    tok,
    grad_out,
    vec_in,
    w_out,
    out_other,
    w_up,
    up_other,
    w_down,
    down_other,
    q_in,
    k_in,
    v_in,
    att_in,
    totals_in,
    probs_in,
    w_full,
    tok_pair,
    result,
    grad_hidden,
    down_own,
    up_own,
    qkv_own,
    out_own,
    vec_own,
    out_all,
    up_all,
    down_all,
    active,
    slope,
    first,
    vec_one,
    att_grads,
    act_halves,
    up_halves,
    branch_halves,
    q_heads,
    k_heads,
    v_heads,
    att_full,
    totals,
    w_all,
    probs,
    grad_land,
    scaled,
    score_grads,
    query_grads,
    kv_own,
    kv_sent,
    kv_pair,
    kv_sum,
    kv_land,
    query_land,
    mixed,
    left_refs,
    right_refs,
    parts,
    from_core,
    from_pair,
    from_low,
    from_high,
    vec_seq,
    sem,
    local_sem,
    line_out,
    line_in,
    pair_out,
    pair_in,
    back_out,
    back_in,
    seq_out,
    seq_in,
    core_sem,
    side_sem,
    low_sem,
    high_sem,
    last_sem,
):
    place = lax.axis_index("ctx")
    core = lax.axis_index("fsdp")
    group = lax.axis_index("seq")
    line, side = place // 2, place % 2
    to_core = {"fsdp": 1 - core}
    to_pair = {"ctx": place + 1 - 2 * side}
    to_seq = {"seq": 1 - group}
    to_up = {"ctx": lax.rem(place + 2, 2 * LINE)}
    to_down = {"ctx": lax.rem(place + 2 * LINE - 2, 2 * LINE)}
    rows, width = grad_hidden.shape
    third = HEADS_OWN * HEAD
    mid = LINE * rows
    half = width // 2
    hidden_units = active.shape[1]
    outs = (down_own, down_own, up_own, up_own, out_own, qkv_own, qkv_own, qkv_own)
    left = [
        (act_halves.at[group], left_refs[0]),
        (left_refs[1], left_refs[2]),
        (attended, left_refs[3]),
        (tok, left_refs[4]),
    ]
    grad_ffn_own, grad_ffn_pair, up_pair, branch_pair = right_refs[:4]
    right = []
    for i in range(2):
        lanes = slice(i * half, (i + 1) * half)
        right.append((grad_ffn_own.at[:, lanes], grad_ffn_pair.at[:, lanes]))
    for i in range(2):
        lanes = slice(i * width, (i + 1) * width)
        right.append((up_halves.at[group, :, lanes], up_pair.at[:, lanes]))
    right.append((branch_halves.at[group], branch_pair))
    units = range(VEC + 1)
    def ahead(k):
        return lax.rem(line + k, LINE)

    def behind(k):
        return lax.rem(line + LINE - k, LINE)

    def to_line(k):
        return {"ctx": 2 * ahead(k) + side}

    def block(which):
        return pl.ds(pl.multiple_of(which * rows, 32), rows)

    def half_block(which):
        return pl.ds(pl.multiple_of(which * (rows // 2), 16), rows // 2)

    def half_of(part, which):
        return pl.ds(pl.multiple_of(part * width + which * half, 128), half)

    for part in range(3):
        right.append((mixed.at[:, half_of(part, group)], right_refs[4 + part]))


    def own_place(u):
        size, columns, wide = dims[u]
        if not wide:
            lanes = slice((u - DOWN) * columns, (u - DOWN + 1) * columns)
            return (pl.ds(pl.multiple_of(group * size, 16), size), lanes)
        if u >= QUERY:
            return (slice(None), half_of(u - QUERY, group))
        if u == OUT:
            return (slice(None), half_of(0, group))
        start = pl.multiple_of((2 * group + u - UP) * columns, 128)
        return (slice(None), pl.ds(start, columns))

    def core_copy(u):
        return remote(
            parts[u].at[1 - core], from_core[u], core_sem.at[0, u], core_sem.at[1, u], to_core
        )

    def side_copy(u, k):
        return remote(
            parts[u].at[core, k, 1 - side],
            from_pair[u].at[k],
            side_sem.at[0, u, k],
            side_sem.at[1, u, k],
            to_pair,
        )

    def up_copy(u, k):
        return remote(
            parts[u].at[core, k, side],
            from_low[u].at[k - 1],
            low_sem.at[0, u, k - 1],
            low_sem.at[1, u, k - 1],
            to_up,
        )

    def down_copy(u, k):
        return remote(
            parts[u].at[core, k, side],
            from_high[u].at[k],
            high_sem.at[0, u, k],
            high_sem.at[1, u, k],
            to_down,
        )

    def last_copy(u):
        if u == VEC:
            where = vec_seq
        else:
            where = outs[u].at[own_place(u)]
        return remote(
            parts[u].at[core, line, side], where, last_sem.at[0, u], last_sem.at[1, u], to_seq
        )

    def multiply(u):
        size, columns, _ = dims[u]
        (a_own, a_pair), (b_own, b_pair) = left[(0, 0, 1, 1, 2, 3, 3, 3)[u]], right[u]
        step = 384
        for first in range(0, a_own.shape[1], step):
            span = slice(first, first + step)
            product = dot_tn(a_own[:, span], b_own[...]) + dot_tn(a_pair[:, span], b_pair[...])
            product = product.astype(BF16)
            for i in range(step // size):
                j = first // size + i
                parts[u][j % 2, j // 4, (j // 2) % 2] = product[i * size : (i + 1) * size]
        core_copy(u).start()

    def line_start(u):
        @pl.when(line == 0)
        def _():
            for k in range(LINE - 1, 0, -1):
                up_copy(u, k).start()

        @pl.when(line == LINE - 1)
        def _():
            for k in range(LINE - 1):
                down_copy(u, k).start()

    def add_core(u):
        core_copy(u).wait_recv()
        for k in (3, 0, 2, 1):
            parts[u][core, k, 1 - side] += from_core[u][k, 1 - side]
            side_copy(u, k).start()
        for k in range(LINE):
            parts[u][core, k, side] += from_core[u][k, side]

    def add_pair(u):
        for k in (3, 0, 2, 1):
            side_copy(u, k).wait_recv()
            parts[u][core, k, side] += from_pair[u][k]
        line_start(u)

    def pass_up(u, k):
        up_copy(u, k).wait_recv()
        parts[u][core, k, side] += from_low[u][k - 1]
        up_copy(u, k).start()

    def pass_down(u, k):
        down_copy(u, k).wait_recv()
        parts[u][core, k, side] += from_high[u][k]
        down_copy(u, k).start()

    def first_hop(u):
        @pl.when(line == 1)
        def _():
            pass_up(u, 3)
            pass_up(u, 2)

        @pl.when(line == 2)
        def _():
            pass_down(u, 0)
            pass_down(u, 1)

    def second_hop(u):
        @pl.when(line == 2)
        def _():
            pass_up(u, 3)

        @pl.when(line == 1)
        def _():
            pass_down(u, 0)

    def line_end(u):
        for k in range(LINE):

            @pl.when(line == k)
            def _(k=k):
                if k > 0:
                    up_copy(u, k).wait_recv()
                    parts[u][core, k, side] += from_low[u][k - 1]
                if k < LINE - 1:
                    down_copy(u, k).wait_recv()
                    parts[u][core, k, side] += from_high[u][k]

    def last_start(u):
        last_copy(u).start()
        if u != VEC:
            outs[u][own_place(u)] = parts[u][core, line, side]

    def stage(u, n):
        if n == 1:
            add_pair(u)
        if n == 2:
            first_hop(u)
        if n == 3:
            second_hop(u)
        if n == 4:
            line_end(u)
            last_start(u)


    seq_copies = []
    for i, (src, dst) in enumerate(
        (
            (left[1][0], left[1][1]),
            (act_halves.at[1 - group], left[0][1]),
            (grad_ffn_own, grad_ffn_pair),
            (up_halves.at[1 - group, :, 0:width], up_pair.at[:, 0:width]),
            (up_halves.at[1 - group, :, width:], up_pair.at[:, width:]),
            (branch_halves.at[1 - group], branch_pair),
            (attended, left[2][1]),
        )
    ):
        seq_copies.append(remote(src, dst, seq_out.at[i], seq_in.at[i], to_seq))

    def place_of(which, size):
        return pl.ds(pl.multiple_of(which * size, 128), size)

    loads = []
    for i, (own, far, full) in enumerate(
        ((w_out, out_other, out_all), (w_up, up_other, up_all), (w_down, down_other, down_all))
    ):
        size = own.shape[0]
        loads.append(
            (
                pltpu.make_async_copy(own, full.at[place_of(core, size)], sem.at[2 * i]),
                pltpu.make_async_copy(far, full.at[place_of(1 - core, size)], sem.at[2 * i + 1]),
            )
        )
    for pair in loads:
        for load in pair:
            load.start()
    late_loads = []
    for i, (src, dst) in enumerate(
        (
            (q_in, q_heads),
            (k_in, k_heads),
            (v_in, v_heads),
            (att_in, att_full),
            (totals_in, totals),
            (probs_in, probs),
            (w_full, w_all),
            (tok_pair, left[3][1]),
        )
    ):
        late_loads.append(pltpu.make_async_copy(src, dst, local_sem.at[i]))
    greet([to_core, to_pair, to_seq] + [to_line(k) for k in range(1, LINE)])

    def arrived(i):
        for load in loads[i]:
            load.wait()

    bias_out, gain_one, shift_one = vec_in[2:3], vec_in[3:4], vec_in[4:5]
    bias_down, gain_two, shift_two = vec_in[5:6], vec_in[6:7], vec_in[7:8]
    arrived(0)
    branch = dot_nn(attended[...], out_all[...]) + bias_out
    normed_one, norm_one, scale_one = norm_forward(tok[...].astype(F32) + branch, gain_one, shift_one)
    normed_b = normed_one.astype(BF16)
    left[1][0][...] = normed_b
    seq_copies[0].start()
    arrived(1)
    step = width
    for c in range(hidden_units // step):
        at, row = (c // 2) * half, 8 + 2 * (c % 2)
        bias = jnp.concatenate([vec_in[row : row + 1, at : at + half], vec_in[row + 1 : row + 2, at : at + half]], axis=1)
        up = dot_nn(normed_b, up_all[:, c * step : (c + 1) * step]) + bias
        cdf = 0.5 * (1.0 + lax.erf(up * 0.7071067811865476))
        active[:, c * step : (c + 1) * step] = (up * cdf).astype(BF16)
        slope[:, c * step : (c + 1) * step] = cdf + up * (
            0.3989422804014327 * jnp.exp(-0.5 * up * up)
        )
    piece = hidden_units // (8 * LINE)
    for j in range(4 * LINE):
        for g in range(2):
            at = (2 * j + g) * piece
            act_halves[g, :, j * piece : (j + 1) * piece] = active[:, at : at + piece]
    seq_copies[1].start()
    arrived(2)
    for load in late_loads:
        load.start()
    second = normed_one + bias_down
    second += dot_nn(active[...], down_all[...])
    final, norm_two, scale_two = norm_forward(second, gain_two, shift_two)
    result[...] = final.astype(BF16)
    grad_second, gain_grad, shift_grad = norm_backward(
        grad_out[...].astype(F32), norm_two, scale_two, gain_two
    )
    grad_ffn = grad_second.astype(BF16)
    grad_ffn_own[...] = grad_ffn
    seq_copies[2].start()
    vec_one[...] = jnp.zeros(vec_one.shape, F32)
    vec_one[3:4] = jnp.sum(grad_ffn.astype(F32), axis=0, keepdims=True)
    vec_one[4:5] = gain_grad[None]
    vec_one[5:6] = shift_grad[None]
    grad_normed = grad_second
    for c in range(hidden_units // step):
        span = slice(c * step, (c + 1) * step)
        grad_up = (dot_nt(grad_ffn, down_all[span]) * slope[:, span]).astype(BF16)
        vec_one[8 + c : 9 + c] = jnp.sum(grad_up.astype(F32), axis=0, keepdims=True)
        grad_normed += dot_nt(grad_up, up_all[:, span])
        up_halves[c // 2, :, (c % 2) * step : (c % 2 + 1) * step] = grad_up
    seq_copies[3].start()
    seq_copies[4].start()
    grad_first, gain_grad, shift_grad = norm_backward(grad_normed, norm_one, scale_one, gain_one)
    first[...] = grad_first
    vec_one[1:2] = gain_grad[None]
    vec_one[2:3] = shift_grad[None]
    grad_branch = grad_first.astype(BF16)
    vec_one[0:1] = jnp.sum(grad_branch.astype(F32), axis=0, keepdims=True)
    for g in range(2):
        branch_halves[g] = grad_branch[:, g * half : (g + 1) * half]
    seq_copies[5].start()
    seq_copies[6].start()
    grad_att = dot_nt(grad_branch, out_all[...]).astype(BF16)
    for d in range(LINE):
        for i in range(2):
            att_grads[d, :, i * third : (i + 1) * third] = grad_att[
                i * rows // 2 : (i + 1) * rows // 2, d * third : (d + 1) * third
            ]


    def line_copy(k):
        return remote(
            att_grads.at[ahead(k)],
            grad_land.at[half_block(line)],
            line_out.at[k - 1],
            line_in.at[k - 1],
            to_line(k),
        )

    def line_landed(k):
        return remote(
            att_grads.at[ahead(k)],
            grad_land.at[half_block(behind(k))],
            line_out.at[k - 1],
            line_in.at[k - 1],
            to_line(k),
        )

    for k in (1, 2, 3):
        line_copy(k).start()
    mixed_copies = []
    for part in range(3):
        mixed_copies.append(
            remote(
                mixed.at[:, half_of(part, 1 - group)],
                right[QUERY + part][1],
                seq_out.at[7 + part],
                seq_in.at[7 + part],
                to_seq,
            )
        )
    grad_land[half_block(line)] = att_grads[line]
    for k in (1, 2, 3):
        line_landed(k).wait_recv()
    for load in late_loads:
        load.wait()

    def pair_copy(h):
        return remote(kv_sent.at[h], kv_pair.at[h], pair_out.at[h], pair_in.at[h], to_pair)

    def head_grads(h):
        lanes = slice(h * HEAD, (h + 1) * HEAD)

        def row_grads(i, carry):
            where = block(i)
            packed = grad_land[half_block(i)]
            far_lanes = slice(third + h * HEAD, third + (h + 1) * HEAD)
            incoming = jnp.concatenate([packed[:, lanes], packed[:, far_lanes]], axis=0).astype(F32)
            row_total = totals[where, h : h + 1]
            delta = jnp.sum(incoming * att_full[where, lanes], axis=-1, keepdims=True)
            grad_scaled = (incoming / row_total).astype(BF16)
            scaled[where] = grad_scaled
            weights = dot_nt(grad_scaled, v_heads[h])
            ds = (probs[h, where].astype(F32) * (weights - delta / row_total)).astype(BF16)
            score_grads[where] = ds
            grad_query = (dot_nn(ds, k_heads[h]) * 0.125).astype(BF16)
            query_grads[half_block(i), lanes] = grad_query[: rows // 2]
            query_grads[half_block(i), far_lanes] = grad_query[rows // 2 :]
            return carry

        lax.fori_loop(0, LINE, row_grads, 0)
        both = jnp.concatenate(
            [dot_tn(q_heads[h], score_grads[...]) * 0.125, dot_tn(scaled[...], probs[h])], axis=0
        )
        both = jnp.transpose(both)
        kv_sent[h] = both[mid:].astype(BF16)
        pair_copy(h).start()
        kv_own[h] = both[:mid]

    def query_back(k):
        return remote(
            query_grads.at[half_block(ahead(k))],
            query_land.at[line],
            back_out.at[HEADS_OWN, k - 1],
            back_in.at[HEADS_OWN, k - 1],
            to_line(k),
        )

    def query_landed(k):
        return remote(
            query_grads.at[half_block(ahead(k))],
            query_land.at[behind(k)],
            back_out.at[HEADS_OWN, k - 1],
            back_in.at[HEADS_OWN, k - 1],
            to_line(k),
        )

    def kv_back(h, k):
        return remote(
            kv_sum.at[h, block(ahead(k))],
            kv_land.at[h, line],
            back_out.at[h, k - 1],
            back_in.at[h, k - 1],
            to_line(k),
        )

    def kv_landed(h, k):
        return remote(
            kv_sum.at[h, block(ahead(k))],
            kv_land.at[h, behind(k)],
            back_out.at[h, k - 1],
            back_in.at[h, k - 1],
            to_line(k),
        )

    def ready(first, last):
        for i in range(first, last):
            seq_copies[i].wait_recv()

    def send_kv(h):
        pair_copy(h).wait_recv()
        kv_sum[h] = (kv_own[h] + kv_pair[h].astype(F32)).astype(BF16)
        for k in (1, 2, 3):
            kv_back(h, k).start()
        kv_land[h, line] = kv_sum[h, block(line)]

    def query_done():
        for k in (1, 2, 3):
            query_landed(k).wait_recv()
        for d in range(LINE):
            for i in range(2):
                mixed[i * rows // 2 : (i + 1) * rows // 2, d * third : (d + 1) * third] = query_land[
                    d, :, i * third : (i + 1) * third
                ]
        mixed_copies[0].start()

    def kv_done():
        for h in range(HEADS_OWN):
            for k in (1, 2, 3):
                kv_landed(h, k).wait_recv()
            for d in range(LINE):
                at = width + d * third + h * HEAD
                mixed[:, at : at + HEAD] = kv_land[h, d, :, 0:HEAD]
                mixed[:, width + at : width + at + HEAD] = kv_land[h, d, :, HEAD:]
        for part in (1, 2):
            mixed_copies[part].start()

    def pack_vectors():
        parts[VEC][...] = jnp.zeros(parts[VEC].shape, F32)
        for j in range(4 * LINE):
            slot = parts[VEC].at[j % 2, j // 4, (j // 2) % 2]
            size = width // (4 * LINE)
            slot[0:8, 0:size] = vec_one[0:8, j * size : (j + 1) * size]
            query_part = mixed[:, j * size : (j + 1) * size].astype(F32)
            slot[8:9, 0:size] = jnp.sum(query_part, axis=0, keepdims=True)
            value_part = mixed[:, 2 * width + j * size : 2 * width + (j + 1) * size].astype(F32)
            slot[9:10, 0:size] = jnp.sum(value_part, axis=0, keepdims=True)
            at = (j % 4) * 4 * size
            slot[10:11, 0 : 4 * size] = vec_one[8 + j // 4 : 9 + j // 4, at : at + 4 * size]
        core_copy(VEC).start()

    head_grads(0)
    head_grads(1)
    ready(0, 3)
    multiply(DOWN)
    multiply(DOWN_B)
    send_kv(0)
    add_core(DOWN)
    head_grads(2)
    for k in (1, 2, 3):
        query_back(k).start()
    query_land[line] = query_grads[half_block(line)]
    send_kv(1)
    add_core(DOWN_B)
    ready(3, 4)
    multiply(UP)
    stage(DOWN, 1)
    send_kv(2)
    ready(4, 5)
    multiply(UP_B)
    add_core(UP)
    query_done()
    stage(DOWN_B, 1)
    stage(DOWN, 2)
    add_core(UP_B)
    ready(5, 7)
    multiply(OUT)
    kv_done()
    stage(DOWN, 3)
    stage(DOWN_B, 2)
    mixed_copies[0].wait_recv()
    multiply(QUERY)
    add_core(OUT)
    stage(UP, 1)
    stage(DOWN_B, 3)
    stage(DOWN, 4)
    pack_vectors()
    mixed_copies[1].wait_recv()
    multiply(KEY)
    add_core(QUERY)
    stage(UP, 2)
    stage(DOWN_B, 4)
    mixed_copies[2].wait_recv()
    multiply(VALUE)
    add_core(KEY)
    stage(UP_B, 1)
    stage(UP, 3)
    add_core(VALUE)
    add_core(VEC)
    stage(OUT, 1)
    stage(UP_B, 2)
    grad_hidden[...] = first[...] + dot_nt(mixed[...], w_all[...])
    stage(UP, 4)
    stage(UP_B, 3)
    for s in range(QUERY, VEC + 4):
        for n in (1, 2, 3, 4):
            if OUT <= s + 1 - n <= VEC:
                stage(s + 1 - n, n)
        if s == QUERY:
            stage(UP_B, 4)
    for u in units:
        last_copy(u).wait_recv()
    vec_own[...] = parts[VEC][core, line, side] + vec_seq[...]
    for k in (1, 2, 3):
        line_copy(k).wait_send()
        query_back(k).wait_send()
        for h in range(HEADS_OWN):
            kv_back(h, k).wait_send()
    for h in range(HEADS_OWN):
        pair_copy(h).wait_send()
    for copy in seq_copies + mixed_copies:
        copy.wait_send()
    for u in units:
        core_copy(u).wait_send()
        last_copy(u).wait_send()
        for k in range(LINE):
            side_copy(u, k).wait_send()
        for k in range(1, LINE):

            @pl.when(line < k)
            def _(k=k):
                up_copy(u, k).wait_send()

        for k in range(LINE - 1):

            @pl.when(line > k)
            def _(k=k):
                down_copy(u, k).wait_send()


def backward(*args):
    rows, width = args[1].shape
    ffn = args[6].shape[1]
    third = HEADS_OWN * HEAD
    mid, seq_rows = LINE * rows, 2 * LINE * rows
    shape = jax.ShapeDtypeStruct
    widths = ((ffn // 2, width // 2),) * 2 + ((width, ffn // 4),) * 2 + ((width, width // 2),) * 4
    dims = [(a // (4 * LINE), b, a == width) for a, b in widths]
    shard, ffn_shard = width // (4 * LINE), ffn // (4 * LINE)
    own_shapes = [(ffn_shard, width), (shard, ffn), (shard, 3 * width), (shard, width)]
    blocks = [((r, c), BF16) for r, c, _ in dims] + [((16, 256), F32)]
    count = len(blocks)
    vmem, dma = pltpu.VMEM, pltpu.SemaphoreType.DMA
    outs = [shape((rows, width), BF16), shape((rows, width), F32)]
    outs += [shape(own, BF16) for own in own_shapes]
    outs.append(shape((16, 256), F32))
    return pl.pallas_call(
        functools.partial(backward_kernel, dims),
        out_shape=outs,
        in_specs=[INNER] * 4 + [ANY] * 14,
        out_specs=[INNER] * len(outs),
        scratch_shapes=[
            vmem((width, width), BF16),
            vmem((width, ffn), BF16),
            vmem((ffn, width), BF16),
            vmem((rows, ffn), BF16),
            vmem((rows, ffn), F32),
            vmem((rows, width), F32),
            vmem((16, width), F32),
            vmem((LINE, rows // 2, 2 * third), BF16),
            vmem((2, rows, ffn // 2), BF16),
            vmem((2, rows, ffn // 2), BF16),
            vmem((2, rows, width // 2), BF16),
            vmem((HEADS_OWN, mid, HEAD), BF16),
            vmem((HEADS_OWN, seq_rows, HEAD), BF16),
            vmem((HEADS_OWN, seq_rows, HEAD), BF16),
            vmem((mid, third), F32),
            vmem((mid, 128), F32),
            vmem((width, 3 * width), BF16),
            vmem((HEADS_OWN, mid, seq_rows), BF16),
            vmem((mid // 2, 2 * third), BF16),
            vmem((mid, HEAD), BF16),
            vmem((mid, seq_rows), BF16),
            vmem((mid // 2, 2 * third), BF16),
            vmem((HEADS_OWN, mid, 128), F32),
            vmem((HEADS_OWN, mid, 128), BF16),
            vmem((HEADS_OWN, mid, 128), BF16),
            vmem((HEADS_OWN, mid, 128), BF16),
            vmem((HEADS_OWN, LINE, rows, 128), BF16),
            vmem((LINE, rows // 2, 2 * third), BF16),
            vmem((rows, 3 * width), BF16),
            [vmem((rows, a), BF16) for a in (ffn // 2, width, width, width, width)],
            [vmem((rows, b), BF16) for b in (width, width, ffn // 2) + (width // 2,) * 4],
            [vmem((2, LINE, 2) + block, kind) for block, kind in blocks],
            [vmem((LINE, 2) + block, kind) for block, kind in blocks],
            [vmem((LINE,) + block, kind) for block, kind in blocks],
            [vmem((LINE - 1,) + block, kind) for block, kind in blocks],
            [vmem((LINE - 1,) + block, kind) for block, kind in blocks],
            vmem((16, 256), F32),
            dma((6,)),
            dma((8,)),
            dma((3,)),
            dma((3,)),
            dma((3,)),
            dma((3,)),
            dma((4, 3)),
            dma((4, 3)),
            dma((10,)),
            dma((10,)),
            dma((2, count)),
            dma((2, count, LINE)),
            dma((2, count, LINE - 1)),
            dma((2, count, LINE - 1)),
            dma((2, count)),
        ],
        compiler_params=pltpu.CompilerParams(
            collective_id=2, has_side_effects=True, vmem_limit_bytes=63 << 20
        ),
        name="backward",
    )(*args)


def finish_kernel(*refs):
    for i in range(6):
        refs[7 + i][...] = refs[i][...].astype(refs[7 + i].dtype)
    vec = refs[6]
    for i, row in enumerate((8, 9, 0, 1, 2, 3, 4, 5, 10)):
        out = refs[13 + i]
        out[...] = vec[row, 0 : out.shape[0]]


def finish(*args):
    shape = jax.ShapeDtypeStruct
    outs = [shape(a.shape, F32) for a in args[:5]] + [shape(args[5].shape, BF16)]
    size = args[2].shape[0]
    outs += [shape((size,), F32)] * 8 + [shape((4 * size,), F32)]
    return pl.pallas_call(
        finish_kernel,
        out_shape=outs,
        in_specs=[INNER] * 7,
        out_specs=[INNER] * len(outs),
        name="finish",
    )(*args)


def block_device(
    hidden,
    segment_ids,
    out_grad,
    w_qkv,
    bias_query,
    bias_value,
    w_out,
    bias_out,
    gain_one,
    shift_one,
    w_up,
    bias_up,
    w_down,
    bias_down,
    gain_two,
    shift_two,
):
    tok, grad_out = hidden[0], out_grad[0]
    small = [
        bias_query,
        bias_value,
        bias_out,
        gain_one,
        shift_one,
        bias_down,
        gain_two,
        shift_two,
        bias_up,
    ]
    (
        attended,
        tok_pair,
        vec_all,
        w_full,
        out_other,
        up_other,
        down_other,
        q_heads,
        k_heads,
        v_heads,
        att_full,
        totals,
        probs,
    ) = attend_forward(tok, segment_ids, small, w_qkv, w_out, w_up, w_down)
    result, grad_hidden, down_own, up_own, qkv_own, out_own, vec_own = backward(
        attended,
        tok,
        grad_out,
        vec_all,
        w_out,
        out_other,
        w_up,
        up_other,
        w_down,
        down_other,
        q_heads,
        k_heads,
        v_heads,
        att_full,
        totals,
        probs,
        w_full,
        tok_pair,
    )
    grads = finish(up_own, down_own, qkv_own, out_own, grad_hidden, result, vec_own)
    up_grad, down_grad, qkv_grad, out_grads, grad_hidden, result = grads[:6]
    (
        query_bias,
        value_bias,
        out_bias,
        gain_first,
        shift_first,
        down_bias,
        gain_second,
        shift_second,
        up_bias,
    ) = grads[6:]
    return (
        result[None],
        grad_hidden[None],
        qkv_grad,
        query_bias,
        value_bias,
        out_grads,
        out_bias,
        gain_first,
        shift_first,
        up_grad,
        up_bias,
        down_grad,
        down_bias,
        gain_second,
        shift_second,
    )


def solution(mesh):
    small = (mesh.shape["seq"], mesh.shape["ctx"], mesh.shape["fsdp"]) == (2, 8, 2)
    return jax.shard_map(
        block_device if small else on_device,
        mesh=mesh,
        in_specs=(
            P(("seq", "fsdp"), "ctx", None),
            P(("seq", "fsdp"), None),
            P(("seq", "fsdp"), "ctx", None),
            P("fsdp", None),
            P("fsdp"),
            P("fsdp"),
            P("fsdp", None),
            P("fsdp"),
            P("fsdp"),
            P("fsdp"),
            P("fsdp", None),
            P("fsdp"),
            P("fsdp", None),
            P("fsdp"),
            P("fsdp"),
            P("fsdp"),
        ),
        out_specs=(
            P(("seq", "fsdp"), "ctx", None),
            P(("seq", "fsdp"), "ctx", None),
            P(("ctx", "fsdp"), None),
            P(("ctx", "fsdp")),
            P(("ctx", "fsdp")),
            P(("ctx", "fsdp"), None),
            P(("ctx", "fsdp")),
            P(("ctx", "fsdp")),
            P(("ctx", "fsdp")),
            P(("ctx", "fsdp"), None),
            P(("ctx", "fsdp")),
            P(("ctx", "fsdp"), None),
            P(("ctx", "fsdp")),
            P(("ctx", "fsdp")),
            P(("ctx", "fsdp")),
        ),
        check_vma=False,
    )
```

```python
import functools

import jax
import jax.numpy as jnp
from jax import lax
from jax.experimental import pallas as pl
from jax.experimental.pallas import tpu as pltpu
from jax.sharding import PartitionSpec as P

HEAD = 64


EPSILON = 1e-12
NEGATIVE = -1e30
LOG_TWO = 0.6931471805599453
LOG2_E = 1.4426950408889634


def norm_forward(rows_in, gain_vec, shift_vec):
    row_mean = jnp.mean(rows_in, axis=-1, keepdims=True)
    centered = rows_in - row_mean
    variance = jnp.mean(centered * centered, axis=-1, keepdims=True)
    scaled = lax.rsqrt(variance + EPSILON)
    normed = centered * scaled
    return (normed * gain_vec + shift_vec, normed, scaled)


def norm_backward(grad_rows, normed, scaled, gain_vec):
    grad_normed = grad_rows * gain_vec
    inner_part = (
        grad_normed
        - jnp.mean(grad_normed, axis=-1, keepdims=True)
        - normed * jnp.mean(grad_normed * normed, axis=-1, keepdims=True)
    )
    return (inner_part * scaled, jnp.sum(grad_rows * normed, axis=0), jnp.sum(grad_rows, axis=0))


def head_scores(query_heads, key_heads):
    return (
        jnp.einsum("qhd,khd->hqk", query_heads, key_heads, preferred_element_type=jnp.float32)
        * 0.125
    )


def column_sums(rows_b):
    return jnp.sum(rows_b.astype(jnp.float32), axis=0)


def sweep(steps_total, advance, start_carry):

    def advance_one(running, block_index):
        running = advance(running, block_index)
        return (running, None)

    return lax.scan(advance_one, start_carry, jnp.arange(steps_total))[0]


def local_grads(scores, allowed, shift_rows, ratio_rows, grad_heads, value_heads):
    unnorm = jnp.where(allowed, jnp.exp(scores - shift_rows[..., None]), 0.0)
    grad_weights = jnp.einsum(
        "qhd,khd->hqk", grad_heads, value_heads, preferred_element_type=jnp.float32
    )
    grad_scores = (unnorm * (grad_weights - ratio_rows[..., None])).astype(jnp.bfloat16)
    return (unnorm.astype(jnp.bfloat16), grad_scores)


def on_device(
    hidden,
    segment_ids,
    out_grad,
    w_qkv,
    bias_query,
    bias_value,
    w_out,
    bias_out,
    gain_one,
    shift_one,
    w_up,
    bias_up,
    w_down,
    bias_down,
    gain_two,
    shift_two,
):
    (
        w_qkv,
        bias_query,
        bias_value,
        w_out,
        bias_out,
        gain_one,
        shift_one,
        w_up,
        bias_up,
        w_down,
        bias_down,
        gain_two,
        shift_two,
    ) = (
        lax.all_gather(w_qkv, "fsdp", axis=0, tiled=True),
        lax.all_gather(bias_query, "fsdp", axis=0, tiled=True),
        lax.all_gather(bias_value, "fsdp", axis=0, tiled=True),
        lax.all_gather(w_out, "fsdp", axis=0, tiled=True),
        lax.all_gather(bias_out, "fsdp", axis=0, tiled=True),
        lax.all_gather(gain_one, "fsdp", axis=0, tiled=True),
        lax.all_gather(shift_one, "fsdp", axis=0, tiled=True),
        lax.all_gather(w_up, "fsdp", axis=0, tiled=True),
        lax.all_gather(bias_up, "fsdp", axis=0, tiled=True),
        lax.all_gather(w_down, "fsdp", axis=0, tiled=True),
        lax.all_gather(bias_down, "fsdp", axis=0, tiled=True),
        lax.all_gather(gain_two, "fsdp", axis=0, tiled=True),
        lax.all_gather(shift_two, "fsdp", axis=0, tiled=True),
    )
    f32 = jnp.float32
    bf16 = jnp.bfloat16
    tokens = hidden[0]
    tok_rows = tokens.shape[0]
    model_width = tokens.shape[1]
    head_count = model_width // HEAD
    seq_rows = tok_rows * lax.axis_size("ctx")
    key_span = 4 * tok_rows
    block_total = seq_rows // key_span
    doc_ids = segment_ids[0]
    own_ids = lax.dynamic_slice_in_dim(doc_ids, lax.axis_index("ctx") * tok_rows, tok_rows)
    mixed_rows = jnp.dot(tokens, w_qkv, preferred_element_type=f32)
    query_rows = (mixed_rows[:, :model_width] + bias_query.astype(f32)).astype(bf16)
    key_value = jnp.concatenate(
        [
            mixed_rows[:, model_width : 2 * model_width],
            mixed_rows[:, 2 * model_width :] + bias_value.astype(f32),
        ],
        axis=1,
    ).astype(bf16)
    all_kv = lax.all_gather(key_value, "ctx", axis=0, tiled=True)
    query_heads = query_rows.reshape(tok_rows, head_count, HEAD)

    def key_block(block_index):
        kv_piece = lax.dynamic_slice_in_dim(all_kv, block_index * key_span, key_span, 0)
        key_ids = lax.dynamic_slice_in_dim(doc_ids, block_index * key_span, key_span)
        return (
            kv_piece[:, :model_width].reshape(key_span, head_count, HEAD),
            kv_piece[:, model_width:].reshape(key_span, head_count, HEAD),
            key_ids,
        )

    def forward_step(running, block_index):
        level_run, total_run, sum_run = running
        key_heads, value_heads, key_ids = key_block(block_index)
        allowed = (own_ids[:, None] == key_ids[None, :])[None]
        scores = jnp.where(allowed, head_scores(query_heads, key_heads), NEGATIVE)
        level_new = jnp.maximum(level_run, jnp.ceil(jnp.max(scores, axis=-1) * LOG2_E))
        rescale = jnp.exp(LOG_TWO * (level_run - level_new))
        unnorm = jnp.where(allowed, jnp.exp(scores - (LOG_TWO * level_new)[..., None]), 0.0)
        total_new = total_run * rescale + jnp.sum(unnorm, axis=-1)
        sum_new = sum_run * jnp.transpose(rescale)[:, :, None] + jnp.einsum(
            "hqk,khd->qhd", unnorm.astype(bf16), value_heads, preferred_element_type=f32
        )
        return (level_new, total_new, sum_new)

    start_state = (
        jnp.full((head_count, tok_rows), NEGATIVE, f32),
        jnp.zeros((head_count, tok_rows), f32),
        jnp.zeros((tok_rows, head_count, HEAD), f32),
    )
    level_end, row_total, raw_sum = sweep(block_total, forward_step, start_state)
    row_shift = LOG_TWO * level_end
    att_sum = raw_sum / jnp.transpose(row_total)[:, :, None]
    attended = att_sum.reshape(tok_rows, model_width).astype(bf16)
    branch = jnp.dot(attended, w_out, preferred_element_type=f32) + bias_out.astype(f32)
    normed_one, norm_one, scale_one = norm_forward(
        tokens.astype(f32) + branch, gain_one.astype(f32), shift_one.astype(f32)
    )
    normed_b = normed_one.astype(bf16)
    up_rows = jnp.dot(normed_b, w_up, preferred_element_type=f32) + bias_up.astype(f32)
    active, gelu_back = jax.vjp(lambda pre_act: jax.nn.gelu(pre_act, approximate=False), up_rows)
    active_b = active.astype(bf16)
    second = (
        normed_one + jnp.dot(active_b, w_down, preferred_element_type=f32) + bias_down.astype(f32)
    )
    result, norm_two, scale_two = norm_forward(second, gain_two.astype(f32), shift_two.astype(f32))
    grad_second, grad_gain_two, grad_shift_two = norm_backward(
        out_grad[0].astype(f32), norm_two, scale_two, gain_two.astype(f32)
    )
    grad_ffn = grad_second.astype(bf16)
    grad_bias_down = column_sums(grad_ffn)
    grad_w_down = jnp.dot(active_b.T, grad_ffn, preferred_element_type=f32)
    grad_active = jnp.dot(grad_ffn, w_down.T, preferred_element_type=f32)
    grad_up = gelu_back(grad_active)[0].astype(bf16)
    grad_bias_up = column_sums(grad_up)
    grad_w_up = jnp.dot(normed_b.T, grad_up, preferred_element_type=f32)
    grad_normed = grad_second + jnp.dot(grad_up, w_up.T, preferred_element_type=f32)
    grad_first, grad_gain_one, grad_shift_one = norm_backward(
        grad_normed, norm_one, scale_one, gain_one.astype(f32)
    )
    grad_branch = grad_first.astype(bf16)
    grad_bias_out = column_sums(grad_branch)
    grad_w_out = jnp.dot(attended.T, grad_branch, preferred_element_type=f32)
    grad_attended = jnp.dot(grad_branch, w_out.T, preferred_element_type=f32).astype(bf16)
    grad_att_f32 = grad_attended.reshape(tok_rows, head_count, HEAD).astype(f32)
    delta = jnp.einsum("qhd,qhd->hq", grad_att_f32, att_sum)
    delta_ratio = delta / row_total
    grad_scaled = (grad_att_f32 / jnp.transpose(row_total)[:, :, None]).astype(bf16)
    zero_query = jnp.zeros((tok_rows, head_count, HEAD), f32)

    def full_step(running, block_index):
        grad_query, grad_kv = running
        key_heads, value_heads, key_ids = key_block(block_index)
        allowed = (own_ids[:, None] == key_ids[None, :])[None]
        unnorm_b, grad_scores = local_grads(
            head_scores(query_heads, key_heads),
            allowed,
            row_shift,
            delta_ratio,
            grad_scaled,
            value_heads,
        )
        grad_query = (
            grad_query
            + jnp.einsum("hqk,khd->qhd", grad_scores, key_heads, preferred_element_type=f32) * 0.125
        )
        grad_keys = (
            jnp.einsum("hqk,qhd->khd", grad_scores, query_heads, preferred_element_type=f32) * 0.125
        )
        grad_values = jnp.einsum("hqk,qhd->khd", unnorm_b, grad_scaled, preferred_element_type=f32)
        both_grads = jnp.concatenate(
            [grad_keys.reshape(key_span, model_width), grad_values.reshape(key_span, model_width)],
            axis=1,
        )
        grad_kv = lax.dynamic_update_slice_in_dim(grad_kv, both_grads, block_index * key_span, 0)
        return (grad_query, grad_kv)

    start_full = (zero_query, jnp.zeros((seq_rows, 2 * model_width), f32))
    grad_query, grad_kv = sweep(block_total, full_step, start_full)
    own_kv = lax.psum_scatter(grad_kv, "ctx", scatter_dimension=0, tiled=True)
    grad_query_b = grad_query.reshape(tok_rows, model_width).astype(bf16)
    grad_kv_b = own_kv.astype(bf16)
    grad_mixed = jnp.concatenate([grad_query_b, grad_kv_b], axis=1)
    grad_tokens = grad_first + jnp.dot(grad_mixed, w_qkv.T, preferred_element_type=f32)
    grad_w_qkv = jnp.dot(tokens.T, grad_mixed, preferred_element_type=f32)
    grad_bias_query = column_sums(grad_query_b)
    grad_bias_value = column_sums(grad_kv_b[:, model_width:])
    shares = (
        lax.psum_scatter(grad_w_qkv, ("ctx", "fsdp"), scatter_dimension=0, tiled=True),
        lax.psum_scatter(grad_bias_query, ("ctx", "fsdp"), scatter_dimension=0, tiled=True),
        lax.psum_scatter(grad_bias_value, ("ctx", "fsdp"), scatter_dimension=0, tiled=True),
        lax.psum_scatter(grad_w_out, ("ctx", "fsdp"), scatter_dimension=0, tiled=True),
        lax.psum_scatter(grad_bias_out, ("ctx", "fsdp"), scatter_dimension=0, tiled=True),
        lax.psum_scatter(grad_gain_one, ("ctx", "fsdp"), scatter_dimension=0, tiled=True),
        lax.psum_scatter(grad_shift_one, ("ctx", "fsdp"), scatter_dimension=0, tiled=True),
        lax.psum_scatter(grad_w_up, ("ctx", "fsdp"), scatter_dimension=0, tiled=True),
        lax.psum_scatter(grad_bias_up, ("ctx", "fsdp"), scatter_dimension=0, tiled=True),
        lax.psum_scatter(grad_w_down, ("ctx", "fsdp"), scatter_dimension=0, tiled=True),
        lax.psum_scatter(grad_bias_down, ("ctx", "fsdp"), scatter_dimension=0, tiled=True),
        lax.psum_scatter(grad_gain_two, ("ctx", "fsdp"), scatter_dimension=0, tiled=True),
        lax.psum_scatter(grad_shift_two, ("ctx", "fsdp"), scatter_dimension=0, tiled=True),
    )
    summed = (
        lax.psum(shares[0].astype(jnp.bfloat16), "seq").astype(jnp.float32),
        lax.psum(shares[1].astype(jnp.bfloat16), "seq").astype(jnp.float32),
        lax.psum(shares[2].astype(jnp.bfloat16), "seq").astype(jnp.float32),
        lax.psum(shares[3].astype(jnp.bfloat16), "seq").astype(jnp.float32),
        lax.psum(shares[4].astype(jnp.bfloat16), "seq").astype(jnp.float32),
        lax.psum(shares[5].astype(jnp.bfloat16), "seq").astype(jnp.float32),
        lax.psum(shares[6].astype(jnp.bfloat16), "seq").astype(jnp.float32),
        lax.psum(shares[7].astype(jnp.bfloat16), "seq").astype(jnp.float32),
        lax.psum(shares[8].astype(jnp.bfloat16), "seq").astype(jnp.float32),
        lax.psum(shares[9].astype(jnp.bfloat16), "seq").astype(jnp.float32),
        lax.psum(shares[10].astype(jnp.bfloat16), "seq").astype(jnp.float32),
        lax.psum(shares[11].astype(jnp.bfloat16), "seq").astype(jnp.float32),
        lax.psum(shares[12].astype(jnp.bfloat16), "seq").astype(jnp.float32),
    )
    return (
        result.astype(bf16)[None],
        grad_tokens[None],
        summed[0],
        summed[1],
        summed[2],
        summed[3],
        summed[4],
        summed[5],
        summed[6],
        summed[7],
        summed[8],
        summed[9],
        summed[10],
        summed[11],
        summed[12],
    )


MESH_ID = pl.DeviceIdType.MESH
LINE = 4


def remote(src, dst, send, recv, target):
    return pltpu.make_async_remote_copy(
        src_ref=src,
        dst_ref=dst,
        send_sem=send,
        recv_sem=recv,
        device_id=target,
        device_id_type=MESH_ID,
    )


HEADS_OWN = 3
F32 = jnp.float32
BF16 = jnp.bfloat16
ANY = pl.BlockSpec(memory_space=pl.ANY)
INNER = pl.BlockSpec(memory_space=pltpu.VMEM)


def dot_nt(a, b):
    return lax.dot_general(a, b, (((1,), (1,)), ((), ())), preferred_element_type=F32)


def dot_tn(a, b):
    return lax.dot_general(a, b, (((0,), (0,)), ((), ())), preferred_element_type=F32)


def dot_nn(a, b):
    return lax.dot_general(a, b, (((1,), (0,)), ((), ())), preferred_element_type=F32)


def greet(targets):
    barrier = pltpu.get_barrier_semaphore()
    for target in targets:
        pl.semaphore_signal(barrier, inc=1, device_id=target, device_id_type=MESH_ID)
    pl.semaphore_wait(barrier, len(targets))


def attend_kernel(
    tok,
    ids,
    small,
    w_qkv,
    w_out,
    w_up,
    w_down,
    attended,
    tok_pair,
    vec_all,
    w_full,
    out_other,
    up_other,
    down_other,
    q_out,
    k_out,
    v_out,
    att_out,
    totals_out,
    probs_out,
    att_full,
    totals,
    q_heads,
    k_heads,
    v_heads,
    w_all,
    mixed,
    sent_kv,
    sent_q,
    mine,
    mine_q,
    other,
    att_sent,
    att_land,
    probs,
    vec,
    ids_row,
    ids_col,
    local_sem,
    probs_sem,
    core_out,
    core_in,
    line_out,
    line_in,
    pair_out,
    pair_in,
    back_out,
    back_in,
    seq_out,
    seq_in,
):
    place = lax.axis_index("ctx")
    core = lax.axis_index("fsdp")
    group = lax.axis_index("seq")
    line, side = place // 2, place % 2
    to_core = {"fsdp": 1 - core}
    to_pair = {"ctx": place + 1 - 2 * side}
    to_seq = {"seq": 1 - group}
    rows = tok.shape[0]
    width = tok.shape[1]
    half = width // 2
    third = HEADS_OWN * HEAD

    def ahead(k):
        return lax.rem(line + k, LINE)

    def behind(k):
        return lax.rem(line + LINE - k, LINE)

    def to_line(k):
        return {"ctx": 2 * ahead(k) + side}

    def block(which):
        return pl.ds(pl.multiple_of(which * rows, 32), rows)

    def half_block(which):
        return pl.ds(pl.multiple_of(which * (rows // 2), 16), rows // 2)

    own_rows = pl.ds(pl.multiple_of(core * half, 128), half)
    other_rows = pl.ds(pl.multiple_of((1 - core) * half, 128), half)

    own_load = pltpu.make_async_copy(w_qkv, w_all.at[own_rows], local_sem.at[0])
    own_load.start()
    at = 0
    for piece in small:
        for first in range(0, piece.shape[0], half):
            vec[at : at + 1] = piece[first : first + half].astype(F32)[None]
            at += 1
    vec[at:] = jnp.zeros((vec.shape[0] - at, half), F32)
    greet([to_core, to_pair, to_seq] + [to_line(k) for k in range(1, LINE)])
    core_copies = [
        remote(vec, vec_all.at[:, own_rows], core_out.at[0], core_in.at[0], to_core),
        remote(w_out, out_other, core_out.at[1], core_in.at[1], to_core),
        remote(w_up, up_other, core_out.at[2], core_in.at[2], to_core),
        remote(w_down, down_other, core_out.at[3], core_in.at[3], to_core),
    ]
    qkv_copies = []
    for part in range(3):
        lanes = slice(part * width, (part + 1) * width)
        sems = core_out.at[4 + part], core_in.at[4 + part]
        qkv_copies.append(remote(w_qkv.at[:, lanes], w_all.at[own_rows, lanes], *sems, to_core))
    seq_copy = remote(tok, tok_pair, seq_out.at[0], seq_in.at[0], to_seq)
    core_copies[0].start()
    for part in (1, 2, 0):
        qkv_copies[part].start()
    seq_copy.start()
    vec_all[:, own_rows] = vec[...]
    own_load.wait()
    step = width // 2
    for first in range(0, 3 * width, step):
        mixed[:, first : first + step] = dot_nn(
            tok[:, own_rows], w_all[own_rows, first : first + step]
        )
    core_copies[0].wait_recv()

    def kv_copy(k, to):
        return remote(
            sent_kv.at[ahead(k)],
            mine.at[block(to)],
            line_out.at[0, k - 1],
            line_in.at[0, k - 1],
            to_line(k),
        )

    def q_copy(k, to):
        return remote(
            sent_q.at[ahead(k)],
            mine_q.at[half_block(to)],
            line_out.at[1, k - 1],
            line_in.at[1, k - 1],
            to_line(k),
        )

    def pair_copy(k):
        where = block(behind(k))
        return remote(mine.at[where], other.at[where], pair_out.at[k], pair_in.at[k], to_pair)

    bias = vec_all[...]
    for part in (1, 2, 0):
        qkv_copies[part].wait_recv()
        for first in range(part * width, (part + 1) * width, step):
            total = mixed[:, first : first + step] + dot_nn(
                tok[:, other_rows], w_all[other_rows, first : first + step]
            )
            within = first - part * width
            if part == 0:
                total += bias[0:1, within : within + step]
            if part == 2:
                total += bias[1:2, within : within + step]
            total = total.astype(BF16)
            for j in range(2):
                d, piece = within // third + j, total[:, j * third : (j + 1) * third]
                if part == 0:
                    sent_q[d, :, 0:third] = piece[: rows // 2]
                    sent_q[d, :, third:] = piece[rows // 2 :]
                else:
                    sent_kv[d, :, (part - 1) * third : part * third] = piece
        for k in (1, 2, 3):
            if part == 2:
                kv_copy(k, line).start()
            if part == 0:
                q_copy(k, line).start()
        if part == 2:
            mine[block(line)] = sent_kv[line]
            pair_copy(0).start()
    for copy in core_copies[1:]:
        copy.start()
    full_store = pltpu.make_async_copy(w_all, w_full, local_sem.at[1])
    full_store.start()
    mine_q[half_block(line)] = sent_q[line]
    for k in (1, 2, 3):
        kv_copy(k, behind(k)).wait_recv()
        pair_copy(k).start()
    seq_rows = 2 * LINE * rows
    mid = LINE * rows
    for z in range(LINE):
        even = ids[:, 2 * z * rows : (2 * z + 1) * rows].astype(F32)
        odd = ids[:, (2 * z + 1) * rows : (2 * z + 2) * rows].astype(F32)
        ids_row[:, z * rows : (z + 1) * rows] = jnp.where(side == 0, even, odd)
        ids_row[:, mid + z * rows : mid + (z + 1) * rows] = jnp.where(side == 0, odd, even)
    ids_col[...] = jnp.transpose(jnp.broadcast_to(ids_row[:, 0:mid], (8, mid)))[:, 0:1]
    for h in range(HEADS_OWN):
        k_heads[h, 0:mid] = mine[:, h * HEAD : (h + 1) * HEAD]
        v_heads[h, 0:mid] = mine[:, third + h * HEAD : third + (h + 1) * HEAD]
    for k in (1, 2, 3):
        q_copy(k, behind(k)).wait_recv()
    for h in range(HEADS_OWN):
        for i in range(2 * LINE):
            from_rows = slice((i // 2) * rows // 2, (i // 2 + 1) * rows // 2)
            at = (i % 2) * third + h * HEAD
            q_heads[h, i * rows // 2 : (i + 1) * rows // 2] = mine_q[from_rows, at : at + HEAD]
    for k in range(LINE):
        pair_copy(k).wait_recv()
    for h in range(HEADS_OWN):
        k_heads[h, mid:seq_rows] = other[:, h * HEAD : (h + 1) * HEAD]
        v_heads[h, mid:seq_rows] = other[:, third + h * HEAD : third + (h + 1) * HEAD]

    head_stores = []
    for i, (src, dst) in enumerate(((q_heads, q_out), (k_heads, k_out), (v_heads, v_out))):
        head_stores.append(pltpu.make_async_copy(src, dst, local_sem.at[2 + i]))
        head_stores[i].start()

    def back_copy(k):
        return remote(
            att_sent.at[ahead(k)],
            att_land.at[line],
            back_out.at[k - 1],
            back_in.at[k - 1],
            to_line(k),
        )

    def back_landed(k):
        return remote(
            att_sent.at[ahead(k)],
            att_land.at[behind(k)],
            back_out.at[k - 1],
            back_in.at[k - 1],
            to_line(k),
        )

    def probs_copy(k):
        where = block(ahead(k))
        return pltpu.make_async_copy(
            probs.at[:, where], probs_out.at[:, where], probs_sem.at[k - 1]
        )

    def attend(k, carry):
        which = ahead(k)
        where = block(which)
        allowed = ids_col[where] == ids_row[...]
        for h in range(HEADS_OWN):
            scores = dot_nt(q_heads[h, where], k_heads[h]) * 0.125
            scores = jnp.where(allowed, scores, NEGATIVE)
            level = jnp.ceil(jnp.max(scores, axis=-1, keepdims=True) * LOG2_E)
            unnorm = jnp.exp(scores - LOG_TWO * level)
            row_total = jnp.sum(unnorm, axis=-1, keepdims=True)
            unnorm_b = unnorm.astype(BF16)
            probs[h, where] = unnorm_b
            value = dot_nn(unnorm_b, v_heads[h]) / row_total
            att_full[where, h * HEAD : (h + 1) * HEAD] = value
            totals[where, h : h + 1] = row_total
            value_b = value.astype(BF16)
            for i in range(2):
                att_sent[which, :, i * third + h * HEAD : i * third + (h + 1) * HEAD] = value_b[
                    i * rows // 2 : (i + 1) * rows // 2
                ]
        probs_copy(k).start()

        @pl.when(k < LINE)
        def _():
            back_copy(k).start()

        return carry

    lax.fori_loop(1, LINE + 1, attend, 0)
    for i, (src, dst) in enumerate(((att_full, att_out), (totals, totals_out))):
        head_stores.append(pltpu.make_async_copy(src, dst, local_sem.at[5 + i]))
        head_stores[-1].start()
    att_land[line] = att_sent[line]
    for k in (1, 2, 3):
        back_landed(k).wait_recv()
    for d in range(LINE):
        for i in range(2):
            attended[i * rows // 2 : (i + 1) * rows // 2, d * third : (d + 1) * third] = att_land[
                d, :, i * third : (i + 1) * third
            ]
    for k in (1, 2, 3):
        kv_copy(k, line).wait_send()
        q_copy(k, line).wait_send()
        back_copy(k).wait_send()
    for k in range(LINE):
        pair_copy(k).wait_send()
        probs_copy(k + 1).wait()
    for copy in core_copies[1:]:
        copy.wait_recv()
    for copy in core_copies + qkv_copies:
        copy.wait_send()
    for store in head_stores:
        store.wait()
    seq_copy.wait()
    full_store.wait()


def attend_forward(tok, ids, small, w_qkv, w_out, w_up, w_down):
    rows, width = tok.shape
    third = HEADS_OWN * HEAD
    mid, seq_rows = LINE * rows, 2 * LINE * rows
    shape = jax.ShapeDtypeStruct
    outs = [
        (shape((rows, width), BF16), INNER),
        (shape((rows, width), BF16), INNER),
        (shape((16, width), F32), INNER),
        (shape((width, 3 * width), BF16), ANY),
        (shape(w_out.shape, BF16), ANY),
        (shape(w_up.shape, BF16), ANY),
        (shape(w_down.shape, BF16), ANY),
        (shape((HEADS_OWN, mid, HEAD), BF16), ANY),
        (shape((HEADS_OWN, seq_rows, HEAD), BF16), ANY),
        (shape((HEADS_OWN, seq_rows, HEAD), BF16), ANY),
        (shape((mid, third), F32), ANY),
        (shape((mid, 128), F32), ANY),
        (shape((HEADS_OWN, mid, seq_rows), BF16), ANY),
    ]
    dma = pltpu.SemaphoreType.DMA
    return pl.pallas_call(
        attend_kernel,
        out_shape=[o[0] for o in outs],
        in_specs=[INNER, INNER, [INNER] * len(small)] + [ANY] * 4,
        out_specs=[o[1] for o in outs],
        scratch_shapes=[
            pltpu.VMEM((mid, third), F32),
            pltpu.VMEM((mid, 128), F32),
            pltpu.VMEM((HEADS_OWN, mid, HEAD), BF16),
            pltpu.VMEM((HEADS_OWN, seq_rows, HEAD), BF16),
            pltpu.VMEM((HEADS_OWN, seq_rows, HEAD), BF16),
            pltpu.VMEM((width, 3 * width), BF16),
            pltpu.VMEM((rows, 3 * width), F32),
            pltpu.VMEM((LINE, rows, 2 * third), BF16),
            pltpu.VMEM((LINE, rows // 2, 2 * third), BF16),
            pltpu.VMEM((mid, 2 * third), BF16),
            pltpu.VMEM((mid // 2, 2 * third), BF16),
            pltpu.VMEM((mid, 2 * third), BF16),
            pltpu.VMEM((LINE, rows // 2, 2 * third), BF16),
            pltpu.VMEM((LINE, rows // 2, 2 * third), BF16),
            pltpu.VMEM((HEADS_OWN, mid, seq_rows), BF16),
            pltpu.VMEM((16, width // 2), F32),
            pltpu.VMEM((1, seq_rows), F32),
            pltpu.VMEM((mid, 1), F32),
            dma((7,)),
            dma((LINE,)),
            dma((7,)),
            dma((7,)),
            dma((2, 3)),
            dma((2, 3)),
            dma((LINE,)),
            dma((LINE,)),
            dma((3,)),
            dma((3,)),
            dma((1,)),
            dma((1,)),
        ],
        compiler_params=pltpu.CompilerParams(
            collective_id=1, has_side_effects=True, vmem_limit_bytes=63 << 20
        ),
        name="attend_forward",
    )(tok, ids, small, w_qkv, w_out, w_up, w_down)


DOWN, DOWN_B, UP, UP_B, OUT, QUERY, KEY, VALUE, VEC = range(9)


def backward_kernel(
    dims,
    attended,
    tok,
    grad_out,
    vec_in,
    w_out,
    out_other,
    w_up,
    up_other,
    w_down,
    down_other,
    q_in,
    k_in,
    v_in,
    att_in,
    totals_in,
    probs_in,
    w_full,
    tok_pair,
    result,
    grad_hidden,
    down_own,
    up_own,
    qkv_own,
    out_own,
    vec_own,
    result_rows,
    hidden_rows,
    out_all,
    up_all,
    down_all,
    active,
    slope,
    first,
    vec_one,
    att_grads,
    act_halves,
    up_halves,
    branch_halves,
    q_heads,
    k_heads,
    v_heads,
    att_full,
    totals,
    w_all,
    probs,
    grad_land,
    scaled,
    score_grads,
    query_grads,
    kv_own,
    kv_sent,
    kv_pair,
    kv_sum,
    kv_land,
    query_land,
    mixed,
    left_refs,
    right_refs,
    parts,
    from_core,
    from_pair,
    from_low,
    from_high,
    vec_seq,
    sem,
    local_sem,
    line_out,
    line_in,
    pair_out,
    pair_in,
    back_out,
    back_in,
    seq_out,
    seq_in,
    core_sem,
    side_sem,
    low_sem,
    high_sem,
    last_sem,
):
    place = lax.axis_index("ctx")
    core = lax.axis_index("fsdp")
    group = lax.axis_index("seq")
    line, side = place // 2, place % 2
    to_core = {"fsdp": 1 - core}
    to_pair = {"ctx": place + 1 - 2 * side}
    to_seq = {"seq": 1 - group}
    to_up = {"ctx": lax.rem(place + 2, 2 * LINE)}
    to_down = {"ctx": lax.rem(place + 2 * LINE - 2, 2 * LINE)}
    rows, width = grad_hidden.shape
    third = HEADS_OWN * HEAD
    mid = LINE * rows
    half = width // 2
    hidden_units = active.shape[1]
    outs = (down_own, down_own, up_own, up_own, out_own, qkv_own, qkv_own, qkv_own)
    left = [
        (act_halves.at[group], left_refs[0]),
        (left_refs[1], left_refs[2]),
        (attended, left_refs[3]),
        (tok, left_refs[4]),
    ]
    grad_ffn_own, grad_ffn_pair, up_pair, branch_pair = right_refs[:4]
    right = []
    for i in range(2):
        lanes = slice(i * half, (i + 1) * half)
        right.append((grad_ffn_own.at[:, lanes], grad_ffn_pair.at[:, lanes]))
    for i in range(2):
        lanes = slice(i * width, (i + 1) * width)
        right.append((up_halves.at[group, :, lanes], up_pair.at[:, lanes]))
    right.append((branch_halves.at[group], branch_pair))
    units = range(VEC + 1)
    def ahead(k):
        return lax.rem(line + k, LINE)

    def behind(k):
        return lax.rem(line + LINE - k, LINE)

    def to_line(k):
        return {"ctx": 2 * ahead(k) + side}

    def block(which):
        return pl.ds(pl.multiple_of(which * rows, 32), rows)

    def half_block(which):
        return pl.ds(pl.multiple_of(which * (rows // 2), 16), rows // 2)

    def half_of(part, which):
        return pl.ds(pl.multiple_of(part * width + which * half, 128), half)

    for part in range(3):
        right.append((mixed.at[:, half_of(part, group)], right_refs[4 + part]))


    def own_place(u):
        size, columns, wide = dims[u]
        if not wide:
            lanes = slice((u - DOWN) * columns, (u - DOWN + 1) * columns)
            return (pl.ds(pl.multiple_of(group * size, 16), size), lanes)
        if u >= QUERY:
            return (slice(None), half_of(u - QUERY, group))
        if u == OUT:
            return (slice(None), half_of(0, group))
        start = pl.multiple_of((2 * group + u - UP) * columns, 128)
        return (slice(None), pl.ds(start, columns))

    def core_copy(u):
        return remote(
            parts[u].at[1 - core], from_core[u], core_sem.at[0, u], core_sem.at[1, u], to_core
        )

    def side_copy(u, k):
        return remote(
            parts[u].at[core, k, 1 - side],
            from_pair[u].at[k],
            side_sem.at[0, u, k],
            side_sem.at[1, u, k],
            to_pair,
        )

    def up_copy(u, k):
        return remote(
            parts[u].at[core, k, side],
            from_low[u].at[k - 1],
            low_sem.at[0, u, k - 1],
            low_sem.at[1, u, k - 1],
            to_up,
        )

    def down_copy(u, k):
        return remote(
            parts[u].at[core, k, side],
            from_high[u].at[k],
            high_sem.at[0, u, k],
            high_sem.at[1, u, k],
            to_down,
        )

    def last_copy(u):
        if u == VEC:
            where = vec_seq
        else:
            where = outs[u].at[own_place(u)]
        return remote(
            parts[u].at[core, line, side], where, last_sem.at[0, u], last_sem.at[1, u], to_seq
        )

    def multiply(u):
        size, columns, _ = dims[u]
        (a_own, a_pair), (b_own, b_pair) = left[(0, 0, 1, 1, 2, 3, 3, 3)[u]], right[u]
        step = 384
        for first in range(0, a_own.shape[1], step):
            span = slice(first, first + step)
            product = dot_tn(a_own[:, span], b_own[...]) + dot_tn(a_pair[:, span], b_pair[...])
            product = product.astype(BF16)
            for i in range(step // size):
                j = first // size + i
                parts[u][j % 2, j // 4, (j // 2) % 2] = product[i * size : (i + 1) * size]
        core_copy(u).start()

    def line_start(u):
        @pl.when(line == 0)
        def _():
            for k in range(LINE - 1, 0, -1):
                up_copy(u, k).start()

        @pl.when(line == LINE - 1)
        def _():
            for k in range(LINE - 1):
                down_copy(u, k).start()

    def add_core(u):
        core_copy(u).wait_recv()
        for k in (3, 0, 2, 1):
            parts[u][core, k, 1 - side] += from_core[u][k, 1 - side]
            side_copy(u, k).start()
        for k in range(LINE):
            parts[u][core, k, side] += from_core[u][k, side]

    def add_pair(u):
        for k in (3, 0, 2, 1):
            side_copy(u, k).wait_recv()
            parts[u][core, k, side] += from_pair[u][k]
        line_start(u)

    def pass_up(u, k):
        up_copy(u, k).wait_recv()
        parts[u][core, k, side] += from_low[u][k - 1]
        up_copy(u, k).start()

    def pass_down(u, k):
        down_copy(u, k).wait_recv()
        parts[u][core, k, side] += from_high[u][k]
        down_copy(u, k).start()

    def first_hop(u):
        @pl.when(line == 1)
        def _():
            pass_up(u, 3)
            pass_up(u, 2)

        @pl.when(line == 2)
        def _():
            pass_down(u, 0)
            pass_down(u, 1)

    def second_hop(u):
        @pl.when(line == 2)
        def _():
            pass_up(u, 3)

        @pl.when(line == 1)
        def _():
            pass_down(u, 0)

    def line_end(u):
        for k in range(LINE):

            @pl.when(line == k)
            def _(k=k):
                if k > 0:
                    up_copy(u, k).wait_recv()
                    parts[u][core, k, side] += from_low[u][k - 1]
                if k < LINE - 1:
                    down_copy(u, k).wait_recv()
                    parts[u][core, k, side] += from_high[u][k]

    def last_start(u):
        last_copy(u).start()
        if u != VEC:
            outs[u][own_place(u)] = parts[u][core, line, side]

    def stage(u, n):
        if n == 1:
            add_pair(u)
        if n == 2:
            first_hop(u)
        if n == 3:
            second_hop(u)
        if n == 4:
            line_end(u)
            last_start(u)


    seq_copies = []
    for i, (src, dst) in enumerate(
        (
            (left[1][0], left[1][1]),
            (act_halves.at[1 - group], left[0][1]),
            (grad_ffn_own, grad_ffn_pair),
            (up_halves.at[1 - group, :, 0:width], up_pair.at[:, 0:width]),
            (up_halves.at[1 - group, :, width:], up_pair.at[:, width:]),
            (branch_halves.at[1 - group], branch_pair),
            (attended, left[2][1]),
        )
    ):
        seq_copies.append(remote(src, dst, seq_out.at[i], seq_in.at[i], to_seq))

    def place_of(which, size):
        return pl.ds(pl.multiple_of(which * size, 128), size)

    loads = []
    for i, (own, far, full) in enumerate(
        ((w_out, out_other, out_all), (w_up, up_other, up_all), (w_down, down_other, down_all))
    ):
        size = own.shape[0]
        loads.append(
            (
                pltpu.make_async_copy(own, full.at[place_of(core, size)], sem.at[2 * i]),
                pltpu.make_async_copy(far, full.at[place_of(1 - core, size)], sem.at[2 * i + 1]),
            )
        )
    for pair in loads:
        for load in pair:
            load.start()
    late_loads = []
    for i, (src, dst) in enumerate(
        (
            (q_in, q_heads),
            (k_in, k_heads),
            (v_in, v_heads),
            (att_in, att_full),
            (totals_in, totals),
            (probs_in, probs),
            (w_full, w_all),
            (tok_pair, left[3][1]),
        )
    ):
        late_loads.append(pltpu.make_async_copy(src, dst, local_sem.at[i]))
    greet([to_core, to_pair, to_seq] + [to_line(k) for k in range(1, LINE)])

    def arrived(i):
        for load in loads[i]:
            load.wait()

    bias_out, gain_one, shift_one = vec_in[2:3], vec_in[3:4], vec_in[4:5]
    bias_down, gain_two, shift_two = vec_in[5:6], vec_in[6:7], vec_in[7:8]
    arrived(0)
    branch = dot_nn(attended[...], out_all[...]) + bias_out
    normed_one, norm_one, scale_one = norm_forward(tok[...].astype(F32) + branch, gain_one, shift_one)
    normed_b = normed_one.astype(BF16)
    left[1][0][...] = normed_b
    seq_copies[0].start()
    arrived(1)
    step = width
    for c in range(hidden_units // step):
        at, row = (c // 2) * half, 8 + 2 * (c % 2)
        bias = jnp.concatenate([vec_in[row : row + 1, at : at + half], vec_in[row + 1 : row + 2, at : at + half]], axis=1)
        up = dot_nn(normed_b, up_all[:, c * step : (c + 1) * step]) + bias
        cdf = 0.5 * (1.0 + lax.erf(up * 0.7071067811865476))
        active[:, c * step : (c + 1) * step] = (up * cdf).astype(BF16)
        slope[:, c * step : (c + 1) * step] = cdf + up * (
            0.3989422804014327 * jnp.exp(-0.5 * up * up)
        )
    piece = hidden_units // (8 * LINE)
    for j in range(4 * LINE):
        for g in range(2):
            at = (2 * j + g) * piece
            act_halves[g, :, j * piece : (j + 1) * piece] = active[:, at : at + piece]
    seq_copies[1].start()
    arrived(2)
    for load in late_loads:
        load.start()
    second = normed_one + bias_down
    second += dot_nn(active[...], down_all[...])
    final, norm_two, scale_two = norm_forward(second, gain_two, shift_two)
    result_rows[...] = final.astype(BF16)
    stores = [
        pltpu.make_async_copy(result_rows, result, local_sem.at[8]),
        pltpu.make_async_copy(hidden_rows, grad_hidden, local_sem.at[9]),
    ]
    stores[0].start()
    grad_second, gain_grad, shift_grad = norm_backward(
        grad_out[...].astype(F32), norm_two, scale_two, gain_two
    )
    grad_ffn = grad_second.astype(BF16)
    grad_ffn_own[...] = grad_ffn
    seq_copies[2].start()
    vec_one[...] = jnp.zeros(vec_one.shape, F32)
    vec_one[3:4] = jnp.sum(grad_ffn.astype(F32), axis=0, keepdims=True)
    vec_one[4:5] = gain_grad[None]
    vec_one[5:6] = shift_grad[None]
    grad_normed = grad_second
    for c in range(hidden_units // step):
        span = slice(c * step, (c + 1) * step)
        grad_up = (dot_nt(grad_ffn, down_all[span]) * slope[:, span]).astype(BF16)
        vec_one[8 + c : 9 + c] = jnp.sum(grad_up.astype(F32), axis=0, keepdims=True)
        grad_normed += dot_nt(grad_up, up_all[:, span])
        up_halves[c // 2, :, (c % 2) * step : (c % 2 + 1) * step] = grad_up
    seq_copies[3].start()
    seq_copies[4].start()
    grad_first, gain_grad, shift_grad = norm_backward(grad_normed, norm_one, scale_one, gain_one)
    first[...] = grad_first
    vec_one[1:2] = gain_grad[None]
    vec_one[2:3] = shift_grad[None]
    grad_branch = grad_first.astype(BF16)
    vec_one[0:1] = jnp.sum(grad_branch.astype(F32), axis=0, keepdims=True)
    for g in range(2):
        branch_halves[g] = grad_branch[:, g * half : (g + 1) * half]
    seq_copies[5].start()
    seq_copies[6].start()
    grad_att = dot_nt(grad_branch, out_all[...]).astype(BF16)
    for d in range(LINE):
        for i in range(2):
            att_grads[d, :, i * third : (i + 1) * third] = grad_att[
                i * rows // 2 : (i + 1) * rows // 2, d * third : (d + 1) * third
            ]


    def line_copy(k):
        return remote(
            att_grads.at[ahead(k)],
            grad_land.at[half_block(line)],
            line_out.at[k - 1],
            line_in.at[k - 1],
            to_line(k),
        )

    def line_landed(k):
        return remote(
            att_grads.at[ahead(k)],
            grad_land.at[half_block(behind(k))],
            line_out.at[k - 1],
            line_in.at[k - 1],
            to_line(k),
        )

    for k in (1, 2, 3):
        line_copy(k).start()
    mixed_copies = []
    for part in range(3):
        mixed_copies.append(
            remote(
                mixed.at[:, half_of(part, 1 - group)],
                right[QUERY + part][1],
                seq_out.at[7 + part],
                seq_in.at[7 + part],
                to_seq,
            )
        )
    grad_land[half_block(line)] = att_grads[line]
    for k in (1, 2, 3):
        line_landed(k).wait_recv()
    for load in late_loads:
        load.wait()

    def pair_copy(h):
        return remote(kv_sent.at[h], kv_pair.at[h], pair_out.at[h], pair_in.at[h], to_pair)

    def head_grads(h):
        lanes = slice(h * HEAD, (h + 1) * HEAD)

        def row_grads(i, carry):
            where = block(i)
            packed = grad_land[half_block(i)]
            far_lanes = slice(third + h * HEAD, third + (h + 1) * HEAD)
            incoming = jnp.concatenate([packed[:, lanes], packed[:, far_lanes]], axis=0).astype(F32)
            row_total = totals[where, h : h + 1]
            delta = jnp.sum(incoming * att_full[where, lanes], axis=-1, keepdims=True)
            grad_scaled = (incoming / row_total).astype(BF16)
            scaled[where] = grad_scaled
            weights = dot_nt(grad_scaled, v_heads[h])
            ds = (probs[h, where].astype(F32) * (weights - delta / row_total)).astype(BF16)
            score_grads[where] = ds
            grad_query = (dot_nn(ds, k_heads[h]) * 0.125).astype(BF16)
            query_grads[half_block(i), lanes] = grad_query[: rows // 2]
            query_grads[half_block(i), far_lanes] = grad_query[rows // 2 :]
            return carry

        lax.fori_loop(0, LINE, row_grads, 0)
        both = jnp.concatenate(
            [dot_tn(q_heads[h], score_grads[...]) * 0.125, dot_tn(scaled[...], probs[h])], axis=0
        )
        both = jnp.transpose(both)
        kv_sent[h] = both[mid:].astype(BF16)
        pair_copy(h).start()
        kv_own[h] = both[:mid]

    def query_back(k):
        return remote(
            query_grads.at[half_block(ahead(k))],
            query_land.at[line],
            back_out.at[HEADS_OWN, k - 1],
            back_in.at[HEADS_OWN, k - 1],
            to_line(k),
        )

    def query_landed(k):
        return remote(
            query_grads.at[half_block(ahead(k))],
            query_land.at[behind(k)],
            back_out.at[HEADS_OWN, k - 1],
            back_in.at[HEADS_OWN, k - 1],
            to_line(k),
        )

    def kv_back(h, k):
        return remote(
            kv_sum.at[h, block(ahead(k))],
            kv_land.at[h, line],
            back_out.at[h, k - 1],
            back_in.at[h, k - 1],
            to_line(k),
        )

    def kv_landed(h, k):
        return remote(
            kv_sum.at[h, block(ahead(k))],
            kv_land.at[h, behind(k)],
            back_out.at[h, k - 1],
            back_in.at[h, k - 1],
            to_line(k),
        )

    def ready(first, last):
        for i in range(first, last):
            seq_copies[i].wait_recv()

    def send_kv(h):
        pair_copy(h).wait_recv()
        kv_sum[h] = (kv_own[h] + kv_pair[h].astype(F32)).astype(BF16)
        for k in (1, 2, 3):
            kv_back(h, k).start()
        kv_land[h, line] = kv_sum[h, block(line)]

    def query_done():
        for k in (1, 2, 3):
            query_landed(k).wait_recv()
        for d in range(LINE):
            for i in range(2):
                mixed[i * rows // 2 : (i + 1) * rows // 2, d * third : (d + 1) * third] = query_land[
                    d, :, i * third : (i + 1) * third
                ]
        mixed_copies[0].start()

    def kv_done():
        for h in range(HEADS_OWN):
            for k in (1, 2, 3):
                kv_landed(h, k).wait_recv()
            for d in range(LINE):
                at = width + d * third + h * HEAD
                mixed[:, at : at + HEAD] = kv_land[h, d, :, 0:HEAD]
                mixed[:, width + at : width + at + HEAD] = kv_land[h, d, :, HEAD:]
        for part in (1, 2):
            mixed_copies[part].start()

    def pack_vectors():
        parts[VEC][...] = jnp.zeros(parts[VEC].shape, F32)
        for j in range(4 * LINE):
            slot = parts[VEC].at[j % 2, j // 4, (j // 2) % 2]
            size = width // (4 * LINE)
            slot[0:8, 0:size] = vec_one[0:8, j * size : (j + 1) * size]
            query_part = mixed[:, j * size : (j + 1) * size].astype(F32)
            slot[8:9, 0:size] = jnp.sum(query_part, axis=0, keepdims=True)
            value_part = mixed[:, 2 * width + j * size : 2 * width + (j + 1) * size].astype(F32)
            slot[9:10, 0:size] = jnp.sum(value_part, axis=0, keepdims=True)
            at = (j % 4) * 4 * size
            slot[10:11, 0 : 4 * size] = vec_one[8 + j // 4 : 9 + j // 4, at : at + 4 * size]
        core_copy(VEC).start()

    head_grads(0)
    head_grads(1)
    ready(0, 3)
    multiply(DOWN)
    multiply(DOWN_B)
    send_kv(0)
    add_core(DOWN)
    head_grads(2)
    for k in (1, 2, 3):
        query_back(k).start()
    query_land[line] = query_grads[half_block(line)]
    send_kv(1)
    add_core(DOWN_B)
    ready(3, 4)
    multiply(UP)
    stage(DOWN, 1)
    send_kv(2)
    ready(4, 5)
    multiply(UP_B)
    add_core(UP)
    query_done()
    stage(DOWN_B, 1)
    stage(DOWN, 2)
    add_core(UP_B)
    ready(5, 7)
    multiply(OUT)
    kv_done()
    stage(DOWN, 3)
    stage(DOWN_B, 2)
    mixed_copies[0].wait_recv()
    multiply(QUERY)
    add_core(OUT)
    stage(UP, 1)
    stage(DOWN_B, 3)
    stage(DOWN, 4)
    pack_vectors()
    mixed_copies[1].wait_recv()
    multiply(KEY)
    add_core(QUERY)
    stage(UP, 2)
    stage(DOWN_B, 4)
    mixed_copies[2].wait_recv()
    multiply(VALUE)
    add_core(KEY)
    stage(UP_B, 1)
    stage(UP, 3)
    add_core(VALUE)
    add_core(VEC)
    stage(OUT, 1)
    stage(UP_B, 2)
    hidden_rows[...] = first[...] + dot_nt(mixed[...], w_all[...])
    stores[1].start()
    stage(UP, 4)
    stage(UP_B, 3)
    for s in range(QUERY, VEC + 4):
        for n in (1, 2, 3, 4):
            if OUT <= s + 1 - n <= VEC:
                stage(s + 1 - n, n)
        if s == QUERY:
            stage(UP_B, 4)
    for u in units:
        last_copy(u).wait_recv()
    for store in stores:
        store.wait()
    vec_own[...] = parts[VEC][core, line, side] + vec_seq[...]
    for k in (1, 2, 3):
        line_copy(k).wait_send()
        query_back(k).wait_send()
        for h in range(HEADS_OWN):
            kv_back(h, k).wait_send()
    for h in range(HEADS_OWN):
        pair_copy(h).wait_send()
    for copy in seq_copies + mixed_copies:
        copy.wait_send()
    for u in units:
        core_copy(u).wait_send()
        last_copy(u).wait_send()
        for k in range(LINE):
            side_copy(u, k).wait_send()
        for k in range(1, LINE):

            @pl.when(line < k)
            def _(k=k):
                up_copy(u, k).wait_send()

        for k in range(LINE - 1):

            @pl.when(line > k)
            def _(k=k):
                down_copy(u, k).wait_send()


def backward(*args):
    rows, width = args[1].shape
    ffn = args[6].shape[1]
    third = HEADS_OWN * HEAD
    mid, seq_rows = LINE * rows, 2 * LINE * rows
    shape = jax.ShapeDtypeStruct
    widths = ((ffn // 2, width // 2),) * 2 + ((width, ffn // 4),) * 2 + ((width, width // 2),) * 4
    dims = [(a // (4 * LINE), b, a == width) for a, b in widths]
    shard, ffn_shard = width // (4 * LINE), ffn // (4 * LINE)
    own_shapes = [(ffn_shard, width), (shard, ffn), (shard, 3 * width), (shard, width)]
    blocks = [((r, c), BF16) for r, c, _ in dims] + [((16, 256), F32)]
    count = len(blocks)
    vmem, dma = pltpu.VMEM, pltpu.SemaphoreType.DMA
    outs = [shape((rows, width), BF16), shape((rows, width), F32)]
    outs += [shape(own, BF16) for own in own_shapes]
    outs.append(shape((16, 256), F32))
    return pl.pallas_call(
        functools.partial(backward_kernel, dims),
        out_shape=outs,
        in_specs=[INNER] * 4 + [ANY] * 14,
        out_specs=[ANY] * 2 + [INNER] * (len(outs) - 2),
        scratch_shapes=[
            vmem((rows, width), BF16),
            vmem((rows, width), F32),
            vmem((width, width), BF16),
            vmem((width, ffn), BF16),
            vmem((ffn, width), BF16),
            vmem((rows, ffn), BF16),
            vmem((rows, ffn), F32),
            vmem((rows, width), F32),
            vmem((16, width), F32),
            vmem((LINE, rows // 2, 2 * third), BF16),
            vmem((2, rows, ffn // 2), BF16),
            vmem((2, rows, ffn // 2), BF16),
            vmem((2, rows, width // 2), BF16),
            vmem((HEADS_OWN, mid, HEAD), BF16),
            vmem((HEADS_OWN, seq_rows, HEAD), BF16),
            vmem((HEADS_OWN, seq_rows, HEAD), BF16),
            vmem((mid, third), F32),
            vmem((mid, 128), F32),
            vmem((width, 3 * width), BF16),
            vmem((HEADS_OWN, mid, seq_rows), BF16),
            vmem((mid // 2, 2 * third), BF16),
            vmem((mid, HEAD), BF16),
            vmem((mid, seq_rows), BF16),
            vmem((mid // 2, 2 * third), BF16),
            vmem((HEADS_OWN, mid, 128), F32),
            vmem((HEADS_OWN, mid, 128), BF16),
            vmem((HEADS_OWN, mid, 128), BF16),
            vmem((HEADS_OWN, mid, 128), BF16),
            vmem((HEADS_OWN, LINE, rows, 128), BF16),
            vmem((LINE, rows // 2, 2 * third), BF16),
            vmem((rows, 3 * width), BF16),
            [vmem((rows, a), BF16) for a in (ffn // 2, width, width, width, width)],
            [vmem((rows, b), BF16) for b in (width, width, ffn // 2) + (width // 2,) * 4],
            [vmem((2, LINE, 2) + block, kind) for block, kind in blocks],
            [vmem((LINE, 2) + block, kind) for block, kind in blocks],
            [vmem((LINE,) + block, kind) for block, kind in blocks],
            [vmem((LINE - 1,) + block, kind) for block, kind in blocks],
            [vmem((LINE - 1,) + block, kind) for block, kind in blocks],
            vmem((16, 256), F32),
            dma((6,)),
            dma((10,)),
            dma((3,)),
            dma((3,)),
            dma((3,)),
            dma((3,)),
            dma((4, 3)),
            dma((4, 3)),
            dma((10,)),
            dma((10,)),
            dma((2, count)),
            dma((2, count, LINE)),
            dma((2, count, LINE - 1)),
            dma((2, count, LINE - 1)),
            dma((2, count)),
        ],
        compiler_params=pltpu.CompilerParams(
            collective_id=2, has_side_effects=True, vmem_limit_bytes=63 << 20
        ),
        name="backward",
    )(*args)


def finish_kernel(*refs):
    for i in range(6):
        refs[7 + i][...] = refs[i][...].astype(refs[7 + i].dtype)
    vec = refs[6]
    for i, row in enumerate((8, 9, 0, 1, 2, 3, 4, 5, 10)):
        out = refs[13 + i]
        out[...] = vec[row, 0 : out.shape[0]]


def finish(*args):
    shape = jax.ShapeDtypeStruct
    outs = [shape(a.shape, F32) for a in args[:5]] + [shape(args[5].shape, BF16)]
    size = args[2].shape[0]
    outs += [shape((size,), F32)] * 8 + [shape((4 * size,), F32)]
    return pl.pallas_call(
        finish_kernel,
        out_shape=outs,
        in_specs=[INNER] * 7,
        out_specs=[INNER] * len(outs),
        name="finish",
    )(*args)


def block_device(
    hidden,
    segment_ids,
    out_grad,
    w_qkv,
    bias_query,
    bias_value,
    w_out,
    bias_out,
    gain_one,
    shift_one,
    w_up,
    bias_up,
    w_down,
    bias_down,
    gain_two,
    shift_two,
):
    tok, grad_out = hidden[0], out_grad[0]
    small = [
        bias_query,
        bias_value,
        bias_out,
        gain_one,
        shift_one,
        bias_down,
        gain_two,
        shift_two,
        bias_up,
    ]
    (
        attended,
        tok_pair,
        vec_all,
        w_full,
        out_other,
        up_other,
        down_other,
        q_heads,
        k_heads,
        v_heads,
        att_full,
        totals,
        probs,
    ) = attend_forward(tok, segment_ids, small, w_qkv, w_out, w_up, w_down)
    result, grad_hidden, down_own, up_own, qkv_own, out_own, vec_own = backward(
        attended,
        tok,
        grad_out,
        vec_all,
        w_out,
        out_other,
        w_up,
        up_other,
        w_down,
        down_other,
        q_heads,
        k_heads,
        v_heads,
        att_full,
        totals,
        probs,
        w_full,
        tok_pair,
    )
    grads = finish(up_own, down_own, qkv_own, out_own, grad_hidden, result, vec_own)
    up_grad, down_grad, qkv_grad, out_grads, grad_hidden, result = grads[:6]
    (
        query_bias,
        value_bias,
        out_bias,
        gain_first,
        shift_first,
        down_bias,
        gain_second,
        shift_second,
        up_bias,
    ) = grads[6:]
    return (
        result[None],
        grad_hidden[None],
        qkv_grad,
        query_bias,
        value_bias,
        out_grads,
        out_bias,
        gain_first,
        shift_first,
        up_grad,
        up_bias,
        down_grad,
        down_bias,
        gain_second,
        shift_second,
    )


def solution(mesh):
    small = (mesh.shape["seq"], mesh.shape["ctx"], mesh.shape["fsdp"]) == (2, 8, 2)
    return jax.shard_map(
        block_device if small else on_device,
        mesh=mesh,
        in_specs=(
            P(("seq", "fsdp"), "ctx", None),
            P(("seq", "fsdp"), None),
            P(("seq", "fsdp"), "ctx", None),
            P("fsdp", None),
            P("fsdp"),
            P("fsdp"),
            P("fsdp", None),
            P("fsdp"),
            P("fsdp"),
            P("fsdp"),
            P("fsdp", None),
            P("fsdp"),
            P("fsdp", None),
            P("fsdp"),
            P("fsdp"),
            P("fsdp"),
        ),
        out_specs=(
            P(("seq", "fsdp"), "ctx", None),
            P(("seq", "fsdp"), "ctx", None),
            P(("ctx", "fsdp"), None),
            P(("ctx", "fsdp")),
            P(("ctx", "fsdp")),
            P(("ctx", "fsdp"), None),
            P(("ctx", "fsdp")),
            P(("ctx", "fsdp")),
            P(("ctx", "fsdp")),
            P(("ctx", "fsdp"), None),
            P(("ctx", "fsdp")),
            P(("ctx", "fsdp"), None),
            P(("ctx", "fsdp")),
            P(("ctx", "fsdp")),
            P(("ctx", "fsdp")),
        ),
        check_vma=False,
    )
```
